768 devices in a mesh: ctx: 48 (over x, z_lo, core), tp: 16 (over z_hi, y).
Axes of the slice: x: 4, y: 8, z: 12 (z_hi: 2, z_lo: 6; z = z_hi * 6 + z_lo), core: 2. Of those that a mesh axis runs over, the one named last changes fastest.
Arguments:
- queries: bfloat16 [6144, 6144], P('ctx', 'tp'), may hold values from -80 to 80
- key_rows: bfloat16 [6144, 1024], P('ctx'), may hold values from -4 to 4
- value_rows: bfloat16 [6144, 1024], P('ctx'), may hold values from -6 to 6
- out_grad: bfloat16 [6144, 6144], P('ctx', 'tp'), may hold values from -6 to 6
- attn_out: bfloat16 [6144, 6144], P('ctx', 'tp'), may hold values from -6 to 6
- doc_ids: int32 [6144], replicated, may hold values from 0 to 7, never falling along the last dimension, each value on 1 to 3200 neighbouring positions
- row_grad: bfloat16 [6144, 6144], P('ctx', 'tp'), may hold values from -6 to 6
- gate_weights: float32 [6144, 2], P('ctx'), may hold values from 0.1 to 0.9
- expert_ids: int32 [6144, 2], P('ctx'), may hold values from 0 to 7, all different within a row; in each aligned block of 128 rows (0 to 127, 128 to 255, ...) at most 64 rows name the same one
- expert_out: bfloat16 [48, 512, 6144], P('ctx', 'tp'), may hold values from -0.079589844 to 0.079589844
Outputs:
- query_grad: bfloat16 [6144, 6144], P('ctx', 'tp')
- key_grad: bfloat16 [6144, 1024], P('ctx', 'tp')
- value_grad: bfloat16 [6144, 1024], P('ctx', 'tp')
- gate_grad: float32 [48, 512], P('ctx', 'tp')
- expert_grad: bfloat16 [48, 512, 6144], P('ctx', 'tp')
The draws below stay inside these ranges and needn't reach their ends.
Inputs may be any that keep to these rules, and one draw needn't show every extreme that they name: `doc_ids`: never falling along the tokens; each document holds 1 to 3200 tokens and one holds exactly 3200. `expert_ids`: A token's 2 experts differ; within each aligned block of 128 tokens no expert is named by more than 64 entries, and in some block an expert is named by exactly 64.
All inputs are finite; a program needn't handle non-finite values.
Results may differ from the reference program's by a relative error of at most 0.006.
Values may be sent and summed in bfloat16 or wider, within the bound.
No kernel may reach another device: no remote copies, remote signals or barrier semaphores. Data moves between devices by JAX's collectives and lax.ppermute only.
A program may use at most 32 MiB of HBM per device.

```python
import math
import jax
import jax.numpy as jnp
import numpy as np
from jax import lax

D = 6144
HD = 128
TOP = 2
DOCS = 8
TOK_DEV = 128
H = 48
KVH = 8
EXPERTS = 8
TOKENS = 6144
DOC_MAX = 3200
CAP_E = 64
CAP = 32
GROUPS = 48


def raw_keys(key):
    return jnp.clip(jax.random.normal(jax.random.fold_in(key, 11), (TOKENS, KVH * HD), jnp.float32), -4.0, 4.0)


def draw_key_rows(key, part):
    return raw_keys(key).astype(jnp.bfloat16)


def draw_queries(key, part):
    base_queries = jnp.clip(jax.random.normal(jax.random.fold_in(key, 23), (TOKENS, H * HD), jnp.float32), -6.0, 6.0)
    return base_queries.astype(jnp.bfloat16)


def block_levels(key, dims, cuts, least, high):
    level = 1.0
    for dim, shards_of in cuts:
        draws = jax.random.uniform(jax.random.fold_in(jax.random.fold_in(key, 6), dim), (shards_of,), jnp.float32, least / len(cuts), high / len(cuts))
        level = level * jnp.repeat(jnp.exp(draws), dims[dim] // shards_of).reshape((-1,) + (1,) * (len(dims) - 1 - dim))
    return level


def profile(number_of, total, most, slope):
    portions = [(1 << 20) // math.isqrt(grade ** slope) + 1 for grade in range(2, number_of + 1)]
    spare, holding = total - most - (number_of - 1), [1] * (number_of - 1)
    while spare > 0:
        free = [i for i in range(number_of - 1) if holding[i] < most]
        whole, remaining = sum([portions[i] for i in free]), spare
        for i in free:
            more = min(most - holding[i], max(1, remaining * portions[i] // whole), spare)
            holding[i] = holding[i] + more
            spare = spare - more
    return np.array([most] + holding)


def ragged(own_key, number_of, total, reach, slope):
    if number_of == 2:
        one = jax.random.randint(own_key, (), max(1, total - reach), min(reach, total - 1) + 1)
        return jnp.stack([one, total - one])
    tallies = jnp.asarray(profile(number_of, total, reach, slope), jnp.int32)
    couples = (number_of - 1) // 2
    giver, taker = tallies[1:1 + 2 * couples:2], tallies[2:2 + 2 * couples:2]
    room = jnp.minimum(giver - 1, reach - taker)
    moved = jax.random.randint(jax.random.fold_in(own_key, 1), (couples,), 0, 1 << 20) % (room + 1)
    tallies = tallies.at[1:1 + 2 * couples:2].set(giver - moved).at[2:2 + 2 * couples:2].set(taker + moved)
    return tallies[jax.random.permutation(jax.random.fold_in(own_key, 2), number_of)]


def shared_out(own_key, own, number, rows, amount, top, bound, slope):
    order = jax.random.permutation(own_key, amount)
    crowded, common = portions_of(amount, rows * top, bound, slope, True), portions_of(amount, rows * top, bound, slope, False)
    places = jnp.arange(amount)

    def named(tallies, offset_by):
        used = int((tallies > 0).sum())
        fixed = max(1, used // 4)
        passed = fixed + (places - fixed + offset_by * (used - fixed)) % max(1, amount - fixed)
        return jnp.zeros((amount,), jnp.int32).at[order[jnp.where(places < fixed, places, passed)]].set(jnp.asarray(tallies, jnp.int32))

    tallies = jnp.where(number % 4 == 0, named(crowded, number // 4), named(common, number - number // 4 - 1))
    mixed = jax.random.permutation(jax.random.fold_in(own, 3), amount)
    donor, receiver = mixed[0:amount // 2 * 2:2], mixed[1:amount // 2 * 2:2]
    room = jnp.minimum(tallies[donor] - 1, bound - tallies[receiver]) // 2
    room = jnp.where((donor == order[0]) | (receiver == order[0]) | (tallies[receiver] == 0), 0, jnp.maximum(room, 0))
    passed = jax.random.randint(jax.random.fold_in(own, 4), (amount // 2,), 0, 1 << 20) % (room + 1)
    tallies = tallies.at[donor].add(-passed).at[receiver].add(passed)
    items = jnp.searchsorted(jnp.cumsum(tallies), jnp.arange(rows * top), side="right").astype(jnp.int32)
    table = items.reshape(top, rows).T
    table = table[jax.random.permutation(jax.random.fold_in(own, 1), rows)]
    offset_by = jax.random.randint(jax.random.fold_in(own, 2), (rows, 1), 0, top)
    return jnp.take_along_axis(table, (jnp.arange(top)[None, :] + offset_by) % top, axis=1)


def portions_of(amount, total, reach, lean, full):
    weights = [(1 << 20) // math.isqrt(standing ** lean) + 1 for standing in range(1, amount + 1)]
    largest = reach if full else min(reach, max(-(-total // amount), total * weights[0] // sum(weights)))
    least = 1 if total - largest >= amount - 1 else 0
    counts, rest = [largest] + [least] * (amount - 1), total - largest - least * (amount - 1)
    while rest > 0:
        movable = [i for i in range(1, amount) if counts[i] < largest] or [i for i in range(1, amount) if counts[i] < reach]
        pool, remaining = sum([weights[i] for i in movable]), rest
        for i in movable:
            extra = min(reach - counts[i], max(1, remaining * weights[i] // pool), rest)
            counts[i] = counts[i] + extra
            rest = rest - extra
    return np.array(counts)


def bell_draw(key, extent, width, reach, split=(), kind=jnp.bfloat16):
    drawn = width * jax.random.normal(key, extent, jnp.float32)
    if split:
        drawn = drawn * block_levels(key, extent, split, -0.22, 0.18)
    return jnp.clip(drawn, -reach, reach).astype(kind)


def setup_inputs(seed: int = 0) -> dict:
    seeds = jax.random.split(jax.random.key(seed), 11)
    queries = draw_queries(jax.random.fold_in(seeds[10], 71), 0)
    key_rows = draw_key_rows(jax.random.fold_in(seeds[10], 71), 0)
    value_rows = bell_draw(seeds[2], (TOKENS, KVH * HD), 1.0, 6.0, ((0, 48),))
    out_grad = bell_draw(seeds[3], (TOKENS, H * HD), 1.0, 6.0, ((0, 48), (1, 16)))
    attn_out = bell_draw(seeds[4], (TOKENS, H * HD), 1.0, 6.0, ((0, 48), (1, 16)))
    doc_ids = jnp.searchsorted(jnp.cumsum(ragged(seeds[5], DOCS, TOKENS, DOC_MAX, 2)), jnp.arange(TOKENS), side="right").astype(jnp.int32)
    row_grad = bell_draw(seeds[6], (TOKENS, D), 1.0, 6.0, ((0, 48), (1, 16)))
    gate_weights = jnp.clip(0.1 + 0.79999997 * jax.random.uniform(seeds[7], (TOKENS, TOP), jnp.float32) ** block_levels(seeds[7], (TOKENS, TOP), ((0, 48),), -0.2, 0.2), 0.1, 0.9)
    expert_ids_keys = jax.random.split(jax.random.fold_in(seeds[8], 1), TOKENS // TOK_DEV)
    expert_ids_turns = jax.random.permutation(jax.random.fold_in(seeds[8], 3), TOKENS // TOK_DEV)
    expert_ids = jax.vmap(lambda own, number: shared_out(jax.random.fold_in(seeds[8], 2), own, number, TOK_DEV, EXPERTS, TOP, CAP_E, 2))(expert_ids_keys, expert_ids_turns).reshape((TOKENS, TOP))
    expert_out = bell_draw(seeds[9], (GROUPS, 2 * EXPERTS * CAP, D), 0.0128, 0.079589844, ((0, 48), (1, 16)))
    return {"queries": queries, "key_rows": key_rows, "value_rows": value_rows, "out_grad": out_grad, "attn_out": attn_out, "doc_ids": doc_ids, "row_grad": row_grad, "gate_weights": gate_weights, "expert_ids": expert_ids, "expert_out": expert_out}


def slot_table(routes_block, experts_total, capacity):
    flat_ids = routes_block.reshape(-1).astype(jnp.int32)
    onehot = (flat_ids[:, None] == jnp.arange(experts_total, dtype=jnp.int32)[None, :]).astype(jnp.int32)
    earlier = jnp.cumsum(onehot, axis=0) - onehot
    ranking = lax.optimization_barrier(jnp.sum(earlier * onehot, axis=1))
    return (2 * flat_ids + ranking // capacity) * capacity + ranking % capacity

def route_group(packed):
    row_block, gate_block, route_block, stored = packed
    slot_count = 2 * EXPERTS * CAP
    positions = slot_table(route_block, EXPERTS, CAP)
    chosen = jnp.arange(slot_count, dtype=jnp.int32)[:, None] == positions[None, :]
    by_token = lax.optimization_barrier(jnp.sum(chosen.reshape(slot_count, TOK_DEV, TOP).astype(jnp.int32), axis=2))
    routed = jnp.dot(by_token.astype(jnp.bfloat16), row_block, preferred_element_type=jnp.float32).astype(jnp.bfloat16)
    slot_gates = lax.optimization_barrier(jnp.sum(jnp.where(chosen, gate_block.reshape(-1)[None, :], 0.0), axis=1))
    gate_part = lax.optimization_barrier(jnp.sum(routed.astype(jnp.float32) * stored.astype(jnp.float32), axis=1))
    expert_part = (slot_gates[:, None] * routed.astype(jnp.float32)).astype(jnp.bfloat16)
    return (gate_part, expert_part)

def reference(queries, key_rows, value_rows, out_grad, attn_out, doc_ids, row_grad, gate_weights, expert_ids, expert_out):
    scaling = 1.0 / math.sqrt(HD)
    positions = jnp.arange(TOKENS, dtype=jnp.int32)
    allowed = (doc_ids[:, None] == doc_ids[None, :]) & (positions[None, :] <= positions[:, None])
    group_size = H // KVH

    def one_head(head_index):
        group_index = head_index // group_size
        query_head = lax.dynamic_slice_in_dim(queries, head_index * HD, HD, 1)
        key_head = lax.dynamic_slice_in_dim(key_rows, group_index * HD, HD, 1)
        value_head = lax.dynamic_slice_in_dim(value_rows, group_index * HD, HD, 1)
        grad_head = lax.dynamic_slice_in_dim(out_grad, head_index * HD, HD, 1)
        output_head = lax.dynamic_slice_in_dim(attn_out, head_index * HD, HD, 1)
        scores = jnp.dot(query_head, key_head.T, preferred_element_type=jnp.float32) * scaling
        scores = jnp.where(allowed, scores, -1e+30)
        row_max = lax.optimization_barrier(jnp.max(scores, axis=1, keepdims=True))
        totals = lax.optimization_barrier(jnp.sum(jnp.where(allowed, jnp.exp(scores - row_max), 0.0), axis=1, keepdims=True))
        log_total = row_max + jnp.log(totals)
        probs = jnp.where(allowed, jnp.exp(scores - log_total), 0.0)
        probs_low = probs.astype(jnp.bfloat16)
        row_delta = lax.optimization_barrier(jnp.sum(grad_head.astype(jnp.float32) * output_head.astype(jnp.float32), axis=1, keepdims=True))
        prob_grad = jnp.dot(grad_head, value_head.T, preferred_element_type=jnp.float32)
        score_grad = (probs * (prob_grad - row_delta)).astype(jnp.bfloat16)
        query_part = (jnp.dot(score_grad, key_head, preferred_element_type=jnp.float32) * scaling).astype(jnp.bfloat16)
        key_part = jnp.dot(score_grad.T, query_head, preferred_element_type=jnp.float32) * scaling
        value_part = jnp.dot(probs_low.T, grad_head, preferred_element_type=jnp.float32)
        return (query_part, key_part, value_part)
    query_parts, key_parts, value_parts = lax.map(one_head, jnp.arange(H, dtype=jnp.int32))
    query_grad = jnp.transpose(query_parts, (1, 0, 2)).reshape(TOKENS, H * HD)
    key_sum = lax.optimization_barrier(jnp.sum(key_parts.reshape(KVH, group_size, TOKENS, HD), axis=1))
    value_sum = lax.optimization_barrier(jnp.sum(value_parts.reshape(KVH, group_size, TOKENS, HD), axis=1))
    key_grad = jnp.transpose(key_sum, (1, 0, 2)).reshape(TOKENS, KVH * HD).astype(jnp.bfloat16)
    value_grad = jnp.transpose(value_sum, (1, 0, 2)).reshape(TOKENS, KVH * HD).astype(jnp.bfloat16)
    gate_grad, expert_grad = lax.map(route_group, (row_grad.reshape(GROUPS, TOK_DEV, D), gate_weights.reshape(GROUPS, TOK_DEV, TOP), expert_ids.reshape(GROUPS, TOK_DEV, TOP), expert_out))
    return (query_grad, key_grad, value_grad, gate_grad, expert_grad)
```

```python
import functools
import math

import jax
import jax.numpy as jnp
from jax import lax
from jax.experimental import pallas as pl
from jax.experimental.pallas import tpu as pltpu
from jax.sharding import Mesh
from jax.sharding import PartitionSpec as P

HD = 128
X, Z = 4, 6
ROWS = 128
KB = 64
PLANE = Z * KB
HEADS = 6
OWN = 3
WINDOW = 14
CHUNK = 2 * KB
STEPS = WINDOW // 2
PLACES = KB + 3 * PLANE
SCALE = 1.0 / math.sqrt(HD)
LOG2E = 1.4426950408889634
NEG = -1e30
SLOTS = 32

F32 = jnp.float32
BF16 = jnp.bfloat16
VMEM_LIMIT = 48 * 1024 * 1024


def dot_nt(a, b):
    return lax.dot_general(a, b, (((1,), (1,)), ((), ())), preferred_element_type=F32)


def dot_nn(a, b):
    return lax.dot_general(a, b, (((1,), (0,)), ((), ())), preferred_element_type=F32)


def call(kernel, out_shape, scratch_shapes, flops=0, nbytes=1 << 20, name=None):
    return pl.pallas_call(
        kernel,
        out_shape=out_shape,
        scratch_shapes=scratch_shapes,
        compiler_params=pltpu.CompilerParams(vmem_limit_bytes=VMEM_LIMIT),
        cost_estimate=pl.CostEstimate(flops=flops, bytes_accessed=nbytes, transcendentals=0),
        name=name,
    )


def place(z, c, p, parts, q_s, do_s, kv_s):
    qd, qd_y, qd_c, kvx, kv2, kv1, kv0 = parts
    for owner, ref, base in ((p, qd, 0), (1 - p, qd_y, 0)):
        for h in range(OWN):
            q_s[owner * OWN + h, pl.ds(c * ROWS, ROWS), :] = ref[:, h * HD : (h + 1) * HD]
            do_s[owner * OWN + h, pl.ds(c * ROWS, ROWS), :] = ref[:, (OWN + h) * HD : (OWN + h + 1) * HD]
    for owner, base in ((p, 0), (1 - p, ROWS)):
        for h in range(OWN):
            q_s[owner * OWN + h, pl.ds((1 - c) * ROWS, ROWS), :] = qd_c[base : base + ROWS, h * HD : (h + 1) * HD]
            do_s[owner * OWN + h, pl.ds((1 - c) * ROWS, ROWS), :] = qd_c[
                base : base + ROWS, (OWN + h) * HD : (OWN + h + 1) * HD
            ]
    kv_s[0:KB, :] = kvx[...]
    kv_s[KB : KB + PLANE, :] = kv2[...]
    kv_s[KB + PLANE : KB + 2 * PLANE, :] = kv1[...]
    kv_s[KB + 2 * PLANE : KB + 3 * PLANE, :] = kv0[...]


def query_spans(doc, chip):
    docs = doc[...]
    mine = jnp.concatenate([doc[pl.ds(2 * chip, 1), :], doc[pl.ds(2 * chip + 1, 1), :]], axis=1)
    first = jnp.zeros((1, 2 * ROWS), jnp.int32)
    for d in range(1, 8):
        before = jnp.sum((docs < d).astype(F32)).astype(jnp.int32)
        first = jnp.where(mine == d, before, first)
    last = chip * 2 * ROWS + lax.broadcasted_iota(jnp.int32, (1, 2 * ROWS), 1)
    return first, last


def bias_of(t, chip, c, p, first, last):
    i = lax.broadcasted_iota(jnp.int32, (CHUNK, 2 * ROWS), 0)
    base = (2 * (chip - (WINDOW - 1) + 2 * t) + c) * ROWS + p * KB
    pos = base + (i // KB) * (2 * ROWS) + i % KB
    return jnp.where((pos >= first) & (pos <= last), 0.0, NEG)


def stats_kernel(qd, qd_y, qd_c, kvx, kv2, kv1, kv0, o_own, doc, stats, q_s, do_s, kv_s, m_s, l_s):
    x, z, c, p = (lax.axis_index(a) for a in ("x", "z", "c", "yl"))
    chip = x * Z + z
    place(z, c, p, (qd, qd_y, qd_c, kvx, kv2, kv1, kv0), q_s, do_s, kv_s)
    first, last = query_spans(doc, chip)
    m_s[...] = jnp.full(m_s.shape, NEG, F32)
    l_s[...] = jnp.zeros(l_s.shape, F32)

    def step(t, _):
        keys = kv_s[pl.ds(pl.multiple_of(z * KB + t * CHUNK, KB), CHUNK), 0:HD]
        bias = bias_of(t, chip, c, p, first, last)
        for h in range(HEADS):
            s = dot_nt(keys, q_s[h]) * (SCALE * LOG2E) + bias
            s = s.reshape(CHUNK // 8, 8, 2 * ROWS)
            old = m_s[h]
            new = jnp.maximum(old, jnp.max(s, axis=0))
            l_s[h] = l_s[h] * jnp.exp2(old - new) + jnp.sum(jnp.exp2(s - new[None]), axis=0)
            m_s[h] = new
        return 0

    lax.fori_loop(0, STEPS, step, 0)
    for h in range(HEADS):
        top = jnp.max(m_s[h], axis=0, keepdims=True)
        total = jnp.sum(l_s[h] * jnp.exp2(m_s[h] - top), axis=0, keepdims=True)
        for r in range(2):
            stats[2 * h + r : 2 * h + r + 1, :] = top[:, r * ROWS : (r + 1) * ROWS]
            stats[12 + 2 * h + r : 13 + 2 * h + r, :] = total[:, r * ROWS : (r + 1) * ROWS]
    for h in range(OWN):
        prod = qd[:, (OWN + h) * HD : (OWN + h + 1) * HD].astype(F32) * o_own[:, h * HD : (h + 1) * HD].astype(F32)
        stats[24 + h : 25 + h, :] = jnp.sum(prod.T, axis=0, keepdims=True)
    stats[27:32, :] = jnp.zeros((5, ROWS), F32)


def grads_kernel(
    qd, qd_y, qd_c, kvx, kv2, kv1, kv0, doc, stats, d2, d1, d0, dx, dq, q_s, do_s, kv_s, acc_s, dq_s
):
    x, z, c, p = (lax.axis_index(a) for a in ("x", "z", "c", "yl"))
    chip = x * Z + z
    place(z, c, p, (qd, qd_y, qd_c, kvx, kv2, kv1, kv0), q_s, do_s, kv_s)
    first, last = query_spans(doc, chip)
    acc_s[...] = jnp.zeros(acc_s.shape, F32)
    dq_s[...] = jnp.zeros(dq_s.shape, F32)
    tops = [stats[i, 0:12, :] for i in range(4)]
    top = jnp.maximum(jnp.maximum(tops[0], tops[1]), jnp.maximum(tops[2], tops[3]))
    total = sum(stats[i, 12:24, :] * jnp.exp2(tops[i] - top) for i in range(4))
    lse = top + jnp.log(total) * LOG2E
    lses, deltas = [], []
    for h in range(HEADS):
        lses.append(jnp.concatenate([lse[2 * h : 2 * h + 1, :], lse[2 * h + 1 : 2 * h + 2, :]], axis=1))
        owner, k = h // OWN, 24 + h % OWN
        deltas.append(jnp.concatenate([stats[owner, k : k + 1, :], stats[2 + owner, k : k + 1, :]], axis=1))

    def step(t, _):
        at = pl.multiple_of(z * KB + t * CHUNK, KB)
        keys = kv_s[pl.ds(at, CHUNK), 0:HD]
        values = kv_s[pl.ds(at, CHUNK), HD : 2 * HD]
        keys_t = keys.astype(F32).T.astype(BF16)
        bias = bias_of(t, chip, c, p, first, last)
        dk = jnp.zeros((CHUNK, HD), F32)
        dv = jnp.zeros((CHUNK, HD), F32)
        for h in range(HEADS):
            q, do = q_s[h], do_s[h]
            probs = jnp.exp2(dot_nt(keys, q) * (SCALE * LOG2E) + bias - lses[h])
            score = (probs * (dot_nt(values, do) - deltas[h])).astype(BF16)
            dv = dv + dot_nn(probs.astype(BF16), do)
            dk = dk + dot_nn(score, q)
            dq_s[h] += dot_nn(keys_t, score)
        acc_s[pl.ds(at, CHUNK), 0:HD] = dk * SCALE
        acc_s[pl.ds(at, CHUNK), HD : 2 * HD] = dv
        return 0

    lax.fori_loop(0, STEPS, step, 0)
    for ref, start, size in (
        (dx, 0, KB),
        (d2, KB, PLANE),
        (d1, KB + PLANE, PLANE),
        (d0, KB + 2 * PLANE, PLANE),
    ):
        dk, dv = acc_s[start : start + size, 0:HD], acc_s[start : start + size, HD : 2 * HD]
        low = lax.broadcasted_iota(jnp.int32, (size, HD), 1) < HD // 2
        ref[:, 0:HD] = jnp.where(low, dk, pltpu.roll(dv, HD // 2, 1)).astype(ref.dtype)
        ref[:, HD : 2 * HD] = jnp.where(low, pltpu.roll(dk, HD // 2, 1), dv).astype(ref.dtype)
    for core in range(2):
        for owner in range(2):
            for h in range(OWN):
                part = dq_s[owner * OWN + h, :, core * ROWS : (core + 1) * ROWS] * SCALE
                dq[2 * core + owner, h * HD : (h + 1) * HD, :] = part.astype(dq.dtype)


def plane_kernel(d0, r1, r2, rx, out):
    for block in range(Z):
        rows = slice(block * KB, (block + 1) * KB)
        total = d0[rows, :] + r1[rows, :].astype(F32) + r2[rows, :].astype(F32)
        if block == Z - 1:
            total = total + rx[...].astype(F32)
        for half in range(2):
            out[2 * block + half] = total[:, half * HD : (half + 1) * HD].astype(BF16)


def block_kernel(parts, key_grad, value_grad):
    for half in range(2):
        total = parts[half].astype(F32)
        for block in range(1, Z):
            total = total + parts[2 * block + half].astype(F32)
        rows = slice(half * KB, (half + 1) * KB)
        key_grad[rows, :] = total[:, 0 : HD // 2].astype(BF16)
        value_grad[rows, :] = total[:, HD // 2 :].astype(BF16)


def query_kernel(parts, query_grad):
    for h in range(OWN):
        rows = slice(h * HD, (h + 1) * HD)
        total = sum(parts[i, rows, :].astype(F32) for i in range(4))
        query_grad[:, rows] = total.T.astype(BF16)


def attention(queries, key_rows, value_rows, out_grad, attn_out, doc_ids):
    group = lax.axis_index("zh") * lax.axis_size("yh") + lax.axis_index("yh")
    half = lax.axis_index("yl")
    keys = lax.dynamic_slice(key_rows, (half * KB, group * HD), (KB, HD))
    values = lax.dynamic_slice(value_rows, (half * KB, group * HD), (KB, HD))
    own = jnp.concatenate([keys, values], axis=1)
    plane = lax.all_to_all(
        jnp.broadcast_to(own[None], (Z, KB, 2 * HD)), "z", split_axis=0, concat_axis=0, tiled=True
    ).reshape(PLANE, 2 * HD)
    lone = [((0 * Z + 5) * 2 + 1, (3 * Z + 0) * 2 + 1)]
    ahead1 = lax.ppermute(plane, "x", [(i, i + 1) for i in range(X - 1)])
    ahead2 = lax.ppermute(plane, "x", [(i, i + 2) for i in range(X - 2)])
    aheadx = lax.ppermute(own, ("x", "z", "c"), lone)

    pool = jnp.concatenate([queries, out_grad], axis=1)
    pool_y = lax.ppermute(pool, "yl", [(0, 1), (1, 0)])
    pool_c = lax.ppermute(jnp.concatenate([pool, pool_y], axis=0), "c", [(0, 1), (1, 0)])

    doc = doc_ids.reshape(-1, ROWS)
    shared = (pool, pool_y, pool_c, aheadx, ahead2, ahead1, plane)
    pool_scratch = [
        pltpu.VMEM((HEADS, 2 * ROWS, HD), BF16),
        pltpu.VMEM((HEADS, 2 * ROWS, HD), BF16),
        pltpu.VMEM((PLACES, 2 * HD), BF16),
    ]
    pairs = WINDOW * KB * HEADS * 2 * ROWS
    stats = call(
        stats_kernel,
        jax.ShapeDtypeStruct((32, ROWS), F32),
        pool_scratch + [pltpu.VMEM((HEADS, 8, 2 * ROWS), F32), pltpu.VMEM((HEADS, 8, 2 * ROWS), F32)],
        flops=2 * HD * pairs,
        name="softmax_stats",
    )(*shared, attn_out, doc)
    stats = lax.all_to_all(
        jnp.broadcast_to(stats[None], (4, 32, ROWS)), ("c", "yl"), split_axis=0, concat_axis=0, tiled=True
    )
    d2, d1, d0, dx, dq = call(
        grads_kernel,
        (
            jax.ShapeDtypeStruct((PLANE, 2 * HD), BF16),
            jax.ShapeDtypeStruct((PLANE, 2 * HD), BF16),
            jax.ShapeDtypeStruct((PLANE, 2 * HD), F32),
            jax.ShapeDtypeStruct((KB, 2 * HD), BF16),
            jax.ShapeDtypeStruct((4, OWN * HD, ROWS), BF16),
        ),
        pool_scratch + [pltpu.VMEM((PLACES, 2 * HD), F32), pltpu.VMEM((HEADS, HD, 2 * ROWS), F32)],
        flops=10 * HD * pairs,
        name="score_grads",
    )(*shared, doc, stats)
    back2 = lax.ppermute(d2, "x", [(i + 2, i) for i in range(X - 2)])
    back1 = lax.ppermute(d1, "x", [(i + 1, i) for i in range(X - 1)])
    backx = lax.ppermute(dx, ("x", "z", "c"), [(b, a) for a, b in lone])
    plane_sums = call(plane_kernel, jax.ShapeDtypeStruct((2 * Z, KB, HD), BF16), [], name="plane_sum")(
        d0, back1, back2, backx
    )
    parts = lax.all_to_all(plane_sums, ("z", "yl"), split_axis=0, concat_axis=0, tiled=True)
    key_grad, value_grad = call(
        block_kernel,
        (jax.ShapeDtypeStruct((ROWS, HD // 2), BF16), jax.ShapeDtypeStruct((ROWS, HD // 2), BF16)),
        [],
        name="block_sum",
    )(parts)
    dq_parts = lax.all_to_all(dq, ("c", "yl"), split_axis=0, concat_axis=0, tiled=True)
    query_grad = call(query_kernel, jax.ShapeDtypeStruct((ROWS, OWN * HD), BF16), [], name="query_sum")(dq_parts)
    return query_grad, key_grad, value_grad


def combine_kernel(rows, ids, gates, stored, gate_grad, expert_grad):
    y = lax.axis_index("yh") * 2 + lax.axis_index("yl")
    place_in_tp = lax.axis_index("zh") * 8 + y
    expert, second = place_in_tp // 2, place_in_tp % 2
    first_hit, other_hit = ids[0:1, :] == expert, ids[1:2, :] == expert
    hit = jnp.where(first_hit | other_hit, 1.0, 0.0)
    earlier = lax.broadcasted_iota(jnp.int32, (ROWS, ROWS), 0) < lax.broadcasted_iota(jnp.int32, (ROWS, ROWS), 1)
    rank = dot_nn(
        jnp.broadcast_to(hit, (16, ROWS)).astype(BF16), jnp.where(earlier, 1.0, 0.0).astype(BF16)
    )[0:1, :].astype(jnp.int32)
    slot = second * SLOTS + lax.broadcasted_iota(jnp.int32, (SLOTS, ROWS), 0)
    chosen = jnp.where((slot == rank) & (hit > 0.0), 1.0, 0.0)
    gate = jnp.where(first_hit, gates[0:1, :], 0.0) + jnp.where(other_hit, gates[1:2, :], 0.0)
    slot_gate = jnp.sum(jnp.where(chosen > 0.0, gate, 0.0), axis=1, keepdims=True)
    chosen = chosen.astype(BF16)
    total = jnp.zeros((SLOTS, OWN * HD), F32)
    for hi in range(2):
        for y in range(8):
            routed = dot_nn(chosen, rows[y, hi])
            cols = slice((hi * 8 + y) * OWN * HD, (hi * 8 + y + 1) * OWN * HD)
            total = total + routed * stored[:, cols].astype(F32)
            expert_grad[:, cols] = (slot_gate * routed).astype(BF16)
    gate_grad[...] = jnp.sum(total.T, axis=0, keepdims=True)


def combine(row_grad, gate_weights, expert_ids, expert_out):
    high = lax.axis_index("zh")
    other = lax.ppermute(row_grad, "zh", [(0, 1), (1, 0)])
    both = jnp.where(
        high == 0, jnp.stack([row_grad, other]), jnp.stack([other, row_grad])
    )
    rows = lax.all_gather(both, ("yh", "yl"), axis=0, tiled=False)
    gate_grad, expert_grad = call(
        combine_kernel,
        (
            jax.ShapeDtypeStruct((1, SLOTS), F32),
            jax.ShapeDtypeStruct((SLOTS, expert_out.shape[2]), BF16),
        ),
        [],
        name="combine_grads",
    )(rows, expert_ids.T, gate_weights.T, expert_out[0])
    return gate_grad, expert_grad[None]


def local(
    queries,
    key_rows,
    value_rows,
    out_grad,
    attn_out,
    doc_ids,
    row_grad,
    gate_weights,
    expert_ids,
    expert_out,
):
    gate_grad, expert_grad = combine(row_grad, gate_weights, expert_ids, expert_out)
    query_grad, key_grad, value_grad = attention(queries, key_rows, value_rows, out_grad, attn_out, doc_ids)
    return (query_grad, key_grad, value_grad, gate_grad, expert_grad)


def solution(mesh):
    devices = mesh.devices.reshape(X, Z, 2, 2, 4, 2)
    split = Mesh(devices, ("x", "z", "c", "zh", "yh", "yl"))
    ctx, tp = ("x", "z", "c"), ("zh", "yh", "yl")
    in_specs = (
        P(ctx, tp),
        P(ctx, None),
        P(ctx, None),
        P(ctx, tp),
        P(ctx, tp),
        P(),
        P(ctx, tp),
        P(ctx, None),
        P(ctx, None),
        P(ctx, tp, None),
    )
    out_specs = (P(ctx, tp), P(ctx, tp), P(ctx, tp), P(ctx, tp), P(ctx, tp, None))
    return jax.shard_map(local, mesh=split, in_specs=in_specs, out_specs=out_specs, check_vma=False)
```

```python
import functools
import math

import jax
import jax.numpy as jnp
from jax import lax
from jax.experimental import pallas as pl
from jax.experimental.pallas import tpu as pltpu
from jax.sharding import Mesh
from jax.sharding import PartitionSpec as P

HD = 128
X, Z = 4, 6
ROWS = 128
KB = 64
PLANE = Z * KB
HEADS = 6
OWN = 3
WINDOW = 14
SPAN = WINDOW * KB
PLACES = KB + 3 * PLANE
SCALE = 1.0 / math.sqrt(HD)
LOG2E = 1.4426950408889634
NEG = -1e30
SLOTS = 32

F32 = jnp.float32
BF16 = jnp.bfloat16
VMEM_LIMIT = 48 * 1024 * 1024


def dot_nt(a, b):
    return lax.dot_general(a, b, (((1,), (1,)), ((), ())), preferred_element_type=F32)


def dot_nn(a, b):
    return lax.dot_general(a, b, (((1,), (0,)), ((), ())), preferred_element_type=F32)


def call(kernel, out_shape, scratch_shapes, flops=0, nbytes=1 << 20, name=None, vmem=VMEM_LIMIT, **specs):
    return pl.pallas_call(
        kernel,
        out_shape=out_shape,
        scratch_shapes=scratch_shapes,
        compiler_params=pltpu.CompilerParams(vmem_limit_bytes=vmem),
        cost_estimate=pl.CostEstimate(flops=flops, bytes_accessed=nbytes, transcendentals=0),
        name=name,
        **specs,
    )


def place(z, c, p, parts, q_s, do_s, kv_s):
    qd, qd_y, qd_c, kvx, kv2, kv1, kv0 = parts
    for owner, ref, base in ((p, qd, 0), (1 - p, qd_y, 0)):
        for h in range(OWN):
            q_s[owner * OWN + h, pl.ds(c * ROWS, ROWS), :] = ref[:, h * HD : (h + 1) * HD]
            do_s[owner * OWN + h, pl.ds(c * ROWS, ROWS), :] = ref[:, (OWN + h) * HD : (OWN + h + 1) * HD]
    for owner, base in ((p, 0), (1 - p, ROWS)):
        for h in range(OWN):
            q_s[owner * OWN + h, pl.ds((1 - c) * ROWS, ROWS), :] = qd_c[base : base + ROWS, h * HD : (h + 1) * HD]
            do_s[owner * OWN + h, pl.ds((1 - c) * ROWS, ROWS), :] = qd_c[
                base : base + ROWS, (OWN + h) * HD : (OWN + h + 1) * HD
            ]
    kv_s[0:KB, :] = kvx[...]
    kv_s[KB : KB + PLANE, :] = kv2[...]
    kv_s[KB + PLANE : KB + 2 * PLANE, :] = kv1[...]
    kv_s[KB + 2 * PLANE : KB + 3 * PLANE, :] = kv0[...]


def query_spans(doc, chip):
    docs = doc[...]
    mine = jnp.concatenate([doc[pl.ds(2 * chip, 1), :], doc[pl.ds(2 * chip + 1, 1), :]], axis=1)
    first = jnp.zeros((1, 2 * ROWS), jnp.int32)
    for d in range(1, 8):
        before = jnp.sum((docs < d).astype(F32)).astype(jnp.int32)
        first = jnp.where(mine == d, before, first)
    last = chip * 2 * ROWS + lax.broadcasted_iota(jnp.int32, (1, 2 * ROWS), 1)
    return first, last


def bias_of(chip, c, p, first, last):
    i = lax.broadcasted_iota(jnp.int32, (SPAN, 2 * ROWS), 0)
    base = (2 * (chip - (WINDOW - 1)) + c) * ROWS + p * KB
    pos = base + (i // KB) * (2 * ROWS) + i % KB
    return jnp.where((pos >= first) & (pos <= last), 0.0, NEG)


def prep_kernel(queries, out_grad, key_rows, value_rows, pool, spread, sems):
    group = lax.axis_index("zh") * 4 + lax.axis_index("yh")
    rows = pl.ds(pl.multiple_of(lax.axis_index("yl") * KB, KB), KB)
    cols = pl.ds(pl.multiple_of(group * HD, HD), HD)
    copies = [
        pltpu.make_async_copy(key_rows.at[rows, cols], spread.at[0, :, 0:HD], sems.at[0]),
        pltpu.make_async_copy(value_rows.at[rows, cols], spread.at[0, :, HD : 2 * HD], sems.at[1]),
        pltpu.make_async_copy(queries, pool.at[:, 0 : OWN * HD], sems.at[2]),
        pltpu.make_async_copy(out_grad, pool.at[:, OWN * HD : 2 * OWN * HD], sems.at[3]),
    ]
    for copy in copies:
        copy.start()
    copies[0].wait()
    copies[1].wait()
    for block in range(1, Z):
        spread[block] = spread[0]
    copies[2].wait()
    copies[3].wait()


def stats_kernel(qd, qd_y, qd_c, kvx, kv2, kv1, kv0, o_own, doc, stats, q_s, do_s, kv_s):
    x, z, c, p = (lax.axis_index(a) for a in ("x", "z", "c", "yl"))
    chip = x * Z + z
    place(z, c, p, (qd, qd_y, qd_c, kvx, kv2, kv1, kv0), q_s, do_s, kv_s)
    first, last = query_spans(doc, chip)
    keys = kv_s[pl.ds(pl.multiple_of(z * KB, KB), SPAN), 0:HD]
    bias = bias_of(chip, c, p, first, last)
    rows = []
    for h in range(HEADS):
        s = dot_nt(keys, q_s[h]) * (SCALE * LOG2E) + bias
        s = s.reshape(SPAN // 8, 8, 2 * ROWS)
        fold = jnp.max(s, axis=0)
        sums = jnp.sum(jnp.exp2(s - fold[None]), axis=0)
        top = jnp.max(fold, axis=0, keepdims=True)
        total = jnp.sum(sums * jnp.exp2(fold - top), axis=0, keepdims=True)
        for r in range(2):
            rows.append((2 * h + r, top[:, r * ROWS : (r + 1) * ROWS]))
            rows.append((12 + 2 * h + r, total[:, r * ROWS : (r + 1) * ROWS]))
    for h in range(OWN):
        prod = qd[:, (OWN + h) * HD : (OWN + h + 1) * HD].astype(F32) * o_own[:, h * HD : (h + 1) * HD].astype(F32)
        rows.append((24 + h, jnp.sum(prod.T, axis=0, keepdims=True)))
    for peer in range(4):
        for at, row in rows:
            stats[peer, at : at + 1, :] = row
        stats[peer, 27:32, :] = jnp.zeros((5, ROWS), F32)


def grads_kernel(
    qd, qd_y, qd_c, kvx, kv2, kv1, kv0, doc, stats, d2, d1, d0, dx, dq_keep, dq_send, q_s, do_s, kv_s, acc_s
):
    x, z, c, p = (lax.axis_index(a) for a in ("x", "z", "c", "yl"))
    chip = x * Z + z
    place(z, c, p, (qd, qd_y, qd_c, kvx, kv2, kv1, kv0), q_s, do_s, kv_s)
    first, last = query_spans(doc, chip)
    acc_s[...] = jnp.zeros(acc_s.shape, F32)
    tops = [stats[i, 0:12, :] for i in range(4)]
    top = jnp.maximum(jnp.maximum(tops[0], tops[1]), jnp.maximum(tops[2], tops[3]))
    total = sum(stats[i, 12:24, :] * jnp.exp2(tops[i] - top) for i in range(4))
    lse = top + jnp.log(total) * LOG2E

    at = pl.multiple_of(z * KB, KB)
    keys = kv_s[pl.ds(at, SPAN), 0:HD]
    values = kv_s[pl.ds(at, SPAN), HD : 2 * HD]
    keys_t = keys.astype(F32).T.astype(BF16)
    bias = bias_of(chip, c, p, first, last)
    dk = jnp.zeros((SPAN, HD), F32)
    dv = jnp.zeros((SPAN, HD), F32)
    for h in range(HEADS):
        owner, k = h // OWN, 24 + h % OWN
        row_lse = jnp.concatenate([lse[2 * h : 2 * h + 1, :], lse[2 * h + 1 : 2 * h + 2, :]], axis=1)
        delta = jnp.concatenate([stats[owner, k : k + 1, :], stats[2 + owner, k : k + 1, :]], axis=1)
        q, do = q_s[h], do_s[h]
        probs = jnp.exp2(dot_nt(keys, q) * (SCALE * LOG2E) + bias - row_lse)
        score = (probs * (dot_nt(values, do) - delta)).astype(BF16)
        dv = dv + dot_nn(probs.astype(BF16), do)
        dk = dk + dot_nn(score, q)
        part = dot_nn(keys_t, score) * SCALE
        lower, upper = part[:, 0:ROWS], part[:, ROWS : 2 * ROWS]
        rows = slice((h % OWN) * HD, (h % OWN + 1) * HD)
        dq_keep[owner, rows, :] = jnp.where(c == 0, lower, upper)
        dq_send[owner, rows, :] = jnp.where(c == 0, upper, lower).astype(BF16)
    acc_s[pl.ds(at, SPAN), 0:HD] = dk * SCALE
    acc_s[pl.ds(at, SPAN), HD : 2 * HD] = dv
    for ref, start, size in (
        (dx, 0, KB),
        (d2, KB, PLANE),
        (d1, KB + PLANE, PLANE),
        (d0, KB + 2 * PLANE, PLANE),
    ):
        dk, dv = acc_s[start : start + size, 0:HD], acc_s[start : start + size, HD : 2 * HD]
        low = lax.broadcasted_iota(jnp.int32, (size, HD), 1) < HD // 2
        ref[:, 0:HD] = jnp.where(low, dk, pltpu.roll(dv, HD // 2, 1)).astype(ref.dtype)
        ref[:, HD : 2 * HD] = jnp.where(low, pltpu.roll(dk, HD // 2, 1), dv).astype(ref.dtype)


def plane_kernel(d0, r1, r2, rx, out):
    for block in range(Z):
        rows = slice(block * KB, (block + 1) * KB)
        total = d0[rows, :] + r1[rows, :].astype(F32) + r2[rows, :].astype(F32)
        if block == Z - 1:
            total = total + rx[...].astype(F32)
        for half in range(2):
            out[2 * block + half] = total[:, half * HD : (half + 1) * HD].astype(BF16)


def block_kernel(parts, key_grad, value_grad):
    halves = []
    for half in range(2):
        total = parts[half].astype(F32)
        for block in range(1, Z):
            total = total + parts[2 * block + half].astype(F32)
        halves.append(total)
    total = jnp.concatenate(halves, axis=0).T
    key_grad[...] = total[0 : HD // 2, :].astype(BF16)
    value_grad[...] = total[HD // 2 :, :].astype(BF16)


def pool_kernel(keep, arrived, mine, other):
    p = lax.axis_index("yl")
    mine[...] = keep[p] + arrived[p].astype(F32)
    other[...] = (keep[1 - p] + arrived[1 - p].astype(F32)).astype(BF16)


def query_kernel(mine, arrived, query_grad):
    for h in range(OWN):
        rows = slice(h * HD, (h + 1) * HD)
        query_grad[:, rows] = (mine[rows, :] + arrived[rows, :].astype(F32)).T.astype(BF16)


def combine_kernel(rows, ids, gates, stored, gate_grad, expert_grad):
    y = lax.axis_index("yh") * 2 + lax.axis_index("yl")
    high = lax.axis_index("zh")
    place_in_tp = high * 8 + y
    expert, second = place_in_tp // 2, place_in_tp % 2
    first_hit, other_hit = ids[0:1, :] == expert, ids[1:2, :] == expert
    hit = jnp.where(first_hit | other_hit, 1.0, 0.0)
    earlier = lax.broadcasted_iota(jnp.int32, (ROWS, ROWS), 0) < lax.broadcasted_iota(jnp.int32, (ROWS, ROWS), 1)
    rank = dot_nn(
        jnp.broadcast_to(hit, (16, ROWS)).astype(BF16), jnp.where(earlier, 1.0, 0.0).astype(BF16)
    )[0:1, :].astype(jnp.int32)
    slot = second * SLOTS + lax.broadcasted_iota(jnp.int32, (SLOTS, ROWS), 0)
    chosen = jnp.where((slot == rank) & (hit > 0.0), 1.0, 0.0)
    gate = jnp.where(first_hit, gates[0:1, :], 0.0) + jnp.where(other_hit, gates[1:2, :], 0.0)
    slot_gate = jnp.sum(jnp.where(chosen > 0.0, gate, 0.0), axis=1, keepdims=True)
    chosen = chosen.astype(BF16)
    total = jnp.zeros((SLOTS, OWN * HD), F32)
    for other in range(2):
        for y in range(8):
            routed = dot_nn(chosen, rows[y, other])
            half = jnp.where(high == other, 0, 1)
            cols = pl.ds(pl.multiple_of((half * 8 + y) * OWN * HD, HD), OWN * HD)
            total = total + routed * stored[:, cols].astype(F32)
            expert_grad[:, cols] = (slot_gate * routed).astype(BF16)
    gate_grad[...] = jnp.sum(total.T, axis=0, keepdims=True)


def local(
    queries,
    key_rows,
    value_rows,
    out_grad,
    attn_out,
    doc_ids,
    row_grad,
    gate_weights,
    expert_ids,
    expert_out,
):
    pool, spread = call(
        prep_kernel,
        (
            jax.ShapeDtypeStruct((ROWS, 2 * OWN * HD), BF16),
            jax.ShapeDtypeStruct((Z, KB, 2 * HD), BF16),
        ),
        [pltpu.SemaphoreType.DMA((4,))],
        name="prep",
        vmem=None,
        in_specs=[pl.BlockSpec(memory_space=pltpu.HBM)] * 4,
    )(queries, out_grad, key_rows, value_rows)
    plane = lax.all_to_all(spread, "z", split_axis=0, concat_axis=0, tiled=True).reshape(PLANE, 2 * HD)
    pool_y = lax.ppermute(pool, "yl", [(0, 1), (1, 0)])
    row_grad, pool_y = lax.optimization_barrier((row_grad, pool_y))
    pool_c = lax.ppermute(jnp.concatenate([pool, pool_y], axis=0), "c", [(0, 1), (1, 0)])
    plane, pool_c = lax.optimization_barrier((plane, pool_c))
    row_other = lax.ppermute(row_grad, "zh", [(0, 1), (1, 0)])
    row_pair, plane = lax.optimization_barrier((jnp.stack([row_grad, row_other]), plane))
    rows = lax.all_gather(row_pair, ("yh", "yl"), axis=0, tiled=False)

    lone = [((0 * Z + 5) * 2 + 1, (3 * Z + 0) * 2 + 1)]
    ahead2 = lax.ppermute(plane, "x", [(i, i + 2) for i in range(X - 2)])
    ahead1 = lax.ppermute(plane, "x", [(i, i + 1) for i in range(X - 1)])
    aheadx = lax.ppermute(spread[0], ("x", "z", "c"), lone)

    doc = doc_ids.reshape(-1, ROWS)
    shared = (pool, pool_y, pool_c, aheadx, ahead2, ahead1, plane)
    pool_scratch = [
        pltpu.VMEM((HEADS, 2 * ROWS, HD), BF16),
        pltpu.VMEM((HEADS, 2 * ROWS, HD), BF16),
        pltpu.VMEM((PLACES, 2 * HD), BF16),
    ]
    pairs = SPAN * HEADS * 2 * ROWS
    stats = call(
        stats_kernel,
        jax.ShapeDtypeStruct((4, 32, ROWS), F32),
        pool_scratch,
        flops=2 * HD * pairs,
        name="softmax_stats",
    )(*shared, attn_out, doc)
    stats = lax.all_to_all(stats, ("c", "yl"), split_axis=0, concat_axis=0, tiled=True)
    d2, d1, d0, dx, dq_keep, dq_send = call(
        grads_kernel,
        (
            jax.ShapeDtypeStruct((PLANE, 2 * HD), BF16),
            jax.ShapeDtypeStruct((PLANE, 2 * HD), BF16),
            jax.ShapeDtypeStruct((PLANE, 2 * HD), F32),
            jax.ShapeDtypeStruct((KB, 2 * HD), BF16),
            jax.ShapeDtypeStruct((2, OWN * HD, ROWS), F32),
            jax.ShapeDtypeStruct((2, OWN * HD, ROWS), BF16),
        ),
        pool_scratch + [pltpu.VMEM((PLACES, 2 * HD), F32)],
        flops=10 * HD * pairs,
        name="score_grads",
    )(*shared, doc, stats)
    back2 = lax.ppermute(d2, "x", [(i + 2, i) for i in range(X - 2)])
    back1 = lax.ppermute(d1, "x", [(i + 1, i) for i in range(X - 1)])
    backx = lax.ppermute(dx, ("x", "z", "c"), [(b, a) for a, b in lone])
    dq_mine, dq_other = call(
        pool_kernel,
        (jax.ShapeDtypeStruct((OWN * HD, ROWS), F32), jax.ShapeDtypeStruct((OWN * HD, ROWS), BF16)),
        [],
        name="query_pool",
    )(dq_keep, lax.ppermute(dq_send, "c", [(0, 1), (1, 0)]))
    dq_other = lax.ppermute(dq_other, "yl", [(0, 1), (1, 0)])
    plane_sums = call(plane_kernel, jax.ShapeDtypeStruct((2 * Z, KB, HD), BF16), [], name="plane_sum")(
        d0, back1, back2, backx
    )
    parts = lax.all_to_all(plane_sums, ("z", "yl"), split_axis=0, concat_axis=0, tiled=True)

    expert_stored, _ = lax.optimization_barrier((expert_out[0], plane_sums))
    gate_grad, expert_grad = call(
        combine_kernel,
        (
            jax.ShapeDtypeStruct((1, SLOTS), F32),
            jax.ShapeDtypeStruct((SLOTS, expert_out.shape[2]), BF16),
        ),
        [],
        name="combine_grads",
    )(rows, expert_ids.T, gate_weights.T, expert_stored)
    query_grad = call(query_kernel, jax.ShapeDtypeStruct((ROWS, OWN * HD), BF16), [], name="query_sum")(
        dq_mine, dq_other
    )
    parts, expert_grad, query_grad = lax.optimization_barrier((parts, expert_grad, query_grad))
    key_grad, value_grad = call(
        block_kernel,
        (jax.ShapeDtypeStruct((HD // 2, ROWS), BF16), jax.ShapeDtypeStruct((HD // 2, ROWS), BF16)),
        [],
        name="block_sum",
    )(parts)
    return (query_grad, key_grad.T, value_grad.T, gate_grad, expert_grad[None])


def solution(mesh):
    devices = mesh.devices.reshape(X, Z, 2, 2, 4, 2)
    split = Mesh(devices, ("x", "z", "c", "zh", "yh", "yl"))
    ctx, tp = ("x", "z", "c"), ("zh", "yh", "yl")
    in_specs = (
        P(ctx, tp),
        P(ctx, None),
        P(ctx, None),
        P(ctx, tp),
        P(ctx, tp),
        P(),
        P(ctx, tp),
        P(ctx, None),
        P(ctx, None),
        P(ctx, tp, None),
    )
    out_specs = (P(ctx, tp), P(ctx, tp), P(ctx, tp), P(ctx, tp), P(ctx, tp, None))
    return jax.shard_map(local, mesh=split, in_specs=in_specs, out_specs=out_specs, check_vma=False)
```

```python
import functools
import math

import jax
import jax.numpy as jnp
from jax import lax
from jax.experimental import pallas as pl
from jax.experimental.pallas import tpu as pltpu
from jax.sharding import Mesh
from jax.sharding import PartitionSpec as P

HD = 128
X, Z = 4, 6
ROWS = 128
KB = 64
PLANE = Z * KB
HEADS = 6
OWN = 3
WINDOW = 14
SPAN = WINDOW * KB
PLACES = KB + 3 * PLANE
SCALE = 1.0 / math.sqrt(HD)
LOG2E = 1.4426950408889634
NEG = -1e30
SLOTS = 32

F32 = jnp.float32
BF16 = jnp.bfloat16
VMEM_LIMIT = 48 * 1024 * 1024


def dot_nt(a, b):
    return lax.dot_general(a, b, (((1,), (1,)), ((), ())), preferred_element_type=F32)


def dot_nn(a, b):
    return lax.dot_general(a, b, (((1,), (0,)), ((), ())), preferred_element_type=F32)


def call(kernel, out_shape, scratch_shapes, flops=0, nbytes=1 << 20, name=None, vmem=VMEM_LIMIT, **specs):
    return pl.pallas_call(
        kernel,
        out_shape=out_shape,
        scratch_shapes=scratch_shapes,
        compiler_params=pltpu.CompilerParams(vmem_limit_bytes=vmem),
        cost_estimate=pl.CostEstimate(flops=flops, bytes_accessed=nbytes, transcendentals=0),
        name=name,
        **specs,
    )


def place(z, c, p, parts, q_s, do_s, kv_s):
    qd, qd_y, qd_c, kvx, kv2, kv1, kv0 = parts
    for owner, ref, base in ((p, qd, 0), (1 - p, qd_y, 0)):
        for h in range(OWN):
            q_s[owner * OWN + h, pl.ds(c * ROWS, ROWS), :] = ref[:, h * HD : (h + 1) * HD]
            do_s[owner * OWN + h, pl.ds(c * ROWS, ROWS), :] = ref[:, (OWN + h) * HD : (OWN + h + 1) * HD]
    for owner, base in ((p, 0), (1 - p, ROWS)):
        for h in range(OWN):
            q_s[owner * OWN + h, pl.ds((1 - c) * ROWS, ROWS), :] = qd_c[base : base + ROWS, h * HD : (h + 1) * HD]
            do_s[owner * OWN + h, pl.ds((1 - c) * ROWS, ROWS), :] = qd_c[
                base : base + ROWS, (OWN + h) * HD : (OWN + h + 1) * HD
            ]
    kv_s[0:KB, :] = kvx[...]
    kv_s[KB : KB + PLANE, :] = kv2[...]
    kv_s[KB + PLANE : KB + 2 * PLANE, :] = kv1[...]
    kv_s[KB + 2 * PLANE : KB + 3 * PLANE, :] = kv0[...]


def query_spans(doc, chip):
    docs = doc[...]
    mine = jnp.concatenate([doc[pl.ds(2 * chip, 1), :], doc[pl.ds(2 * chip + 1, 1), :]], axis=1)
    first = jnp.zeros((1, 2 * ROWS), jnp.int32)
    for d in range(1, 8):
        before = jnp.sum((docs < d).astype(F32)).astype(jnp.int32)
        first = jnp.where(mine == d, before, first)
    last = chip * 2 * ROWS + lax.broadcasted_iota(jnp.int32, (1, 2 * ROWS), 1)
    return first, last


def bias_of(chip, c, p, first, last):
    i = lax.broadcasted_iota(jnp.int32, (SPAN, 2 * ROWS), 0)
    base = (2 * (chip - (WINDOW - 1)) + c) * ROWS + p * KB
    pos = base + (i // KB) * (2 * ROWS) + i % KB
    return jnp.where((pos >= first) & (pos <= last), 0.0, NEG)


def prep_kernel(queries, out_grad, key_rows, value_rows, pool, spread, sems):
    group = lax.axis_index("zh") * 4 + lax.axis_index("yh")
    rows = pl.ds(pl.multiple_of(lax.axis_index("yl") * KB, KB), KB)
    cols = pl.ds(pl.multiple_of(group * HD, HD), HD)
    copies = [
        pltpu.make_async_copy(key_rows.at[rows, cols], spread.at[0, :, 0:HD], sems.at[0]),
        pltpu.make_async_copy(value_rows.at[rows, cols], spread.at[0, :, HD : 2 * HD], sems.at[1]),
        pltpu.make_async_copy(queries, pool.at[:, 0 : OWN * HD], sems.at[2]),
        pltpu.make_async_copy(out_grad, pool.at[:, OWN * HD : 2 * OWN * HD], sems.at[3]),
    ]
    for copy in copies:
        copy.start()
    copies[0].wait()
    copies[1].wait()
    for block in range(1, Z):
        spread[block] = spread[0]
    copies[2].wait()
    copies[3].wait()


def stats_kernel(qd, qd_y, qd_c, kvx, kv2, kv1, kv0, o_own, doc, stats, q_s, do_s, kv_s):
    x, z, c, p = (lax.axis_index(a) for a in ("x", "z", "c", "yl"))
    chip = x * Z + z
    place(z, c, p, (qd, qd_y, qd_c, kvx, kv2, kv1, kv0), q_s, do_s, kv_s)
    first, last = query_spans(doc, chip)
    keys = kv_s[pl.ds(pl.multiple_of(z * KB, KB), SPAN), 0:HD]
    bias = bias_of(chip, c, p, first, last)
    rows = []
    for h in range(HEADS):
        s = dot_nt(keys, q_s[h]) * (SCALE * LOG2E) + bias
        s = s.reshape(SPAN // 8, 8, 2 * ROWS)
        fold = jnp.max(s, axis=0)
        sums = jnp.sum(jnp.exp2(s - fold[None]), axis=0)
        top = jnp.max(fold, axis=0, keepdims=True)
        total = jnp.sum(sums * jnp.exp2(fold - top), axis=0, keepdims=True)
        for r in range(2):
            rows.append((2 * h + r, top[:, r * ROWS : (r + 1) * ROWS]))
            rows.append((12 + 2 * h + r, total[:, r * ROWS : (r + 1) * ROWS]))
    for h in range(OWN):
        prod = qd[:, (OWN + h) * HD : (OWN + h + 1) * HD].astype(F32) * o_own[:, h * HD : (h + 1) * HD].astype(F32)
        rows.append((24 + h, jnp.sum(prod.T, axis=0, keepdims=True)))
    for peer in range(4):
        for at, row in rows:
            stats[peer, at : at + 1, :] = row
        stats[peer, 27:32, :] = jnp.zeros((5, ROWS), F32)


def grads_kernel(
    qd, qd_y, qd_c, kvx, kv2, kv1, kv0, doc, stats, d2, d1, d0, dx, dq_keep, dq_send, q_s, do_s, kv_s, acc_s
):
    x, z, c, p = (lax.axis_index(a) for a in ("x", "z", "c", "yl"))
    chip = x * Z + z
    place(z, c, p, (qd, qd_y, qd_c, kvx, kv2, kv1, kv0), q_s, do_s, kv_s)
    first, last = query_spans(doc, chip)
    acc_s[...] = jnp.zeros(acc_s.shape, F32)
    tops = [stats[i, 0:12, :] for i in range(4)]
    top = jnp.maximum(jnp.maximum(tops[0], tops[1]), jnp.maximum(tops[2], tops[3]))
    total = sum(stats[i, 12:24, :] * jnp.exp2(tops[i] - top) for i in range(4))
    lse = top + jnp.log(total) * LOG2E

    at = pl.multiple_of(z * KB, KB)
    keys = kv_s[pl.ds(at, SPAN), 0:HD]
    values = kv_s[pl.ds(at, SPAN), HD : 2 * HD]
    keys_t = keys.astype(F32).T.astype(BF16)
    bias = bias_of(chip, c, p, first, last)
    dk = jnp.zeros((SPAN, HD), F32)
    dv = jnp.zeros((SPAN, HD), F32)
    for h in range(HEADS):
        owner, k = h // OWN, 24 + h % OWN
        row_lse = jnp.concatenate([lse[2 * h : 2 * h + 1, :], lse[2 * h + 1 : 2 * h + 2, :]], axis=1)
        delta = jnp.concatenate([stats[owner, k : k + 1, :], stats[2 + owner, k : k + 1, :]], axis=1)
        q, do = q_s[h], do_s[h]
        probs = jnp.exp2(dot_nt(keys, q) * (SCALE * LOG2E) + bias - row_lse)
        score = (probs * (dot_nt(values, do) - delta)).astype(BF16)
        dv = dv + dot_nn(probs.astype(BF16), do)
        dk = dk + dot_nn(score, q)
        part = dot_nn(keys_t, score) * SCALE
        lower, upper = part[:, 0:ROWS], part[:, ROWS : 2 * ROWS]
        rows = slice((h % OWN) * HD, (h % OWN + 1) * HD)
        dq_keep[owner, rows, :] = jnp.where(c == 0, lower, upper)
        dq_send[owner, rows, :] = jnp.where(c == 0, upper, lower).astype(BF16)
    acc_s[pl.ds(at, SPAN), 0:HD] = dk * SCALE
    acc_s[pl.ds(at, SPAN), HD : 2 * HD] = dv
    for ref, start, size in (
        (dx, 0, KB),
        (d2, KB, PLANE),
        (d1, KB + PLANE, PLANE),
        (d0, KB + 2 * PLANE, PLANE),
    ):
        dk, dv = acc_s[start : start + size, 0:HD], acc_s[start : start + size, HD : 2 * HD]
        low = lax.broadcasted_iota(jnp.int32, (size, HD), 1) < HD // 2
        ref[:, 0:HD] = jnp.where(low, dk, pltpu.roll(dv, HD // 2, 1)).astype(ref.dtype)
        ref[:, HD : 2 * HD] = jnp.where(low, pltpu.roll(dk, HD // 2, 1), dv).astype(ref.dtype)


def plane_kernel(d0, r1, r2, rx, out):
    for block in range(Z):
        rows = slice(block * KB, (block + 1) * KB)
        total = d0[rows, :] + r1[rows, :].astype(F32) + r2[rows, :].astype(F32)
        if block == Z - 1:
            total = total + rx[...].astype(F32)
        for half in range(2):
            out[2 * block + half] = total[:, half * HD : (half + 1) * HD].astype(BF16)


def block_kernel(parts, key_grad, value_grad):
    halves = []
    for half in range(2):
        total = parts[half].astype(F32)
        for block in range(1, Z):
            total = total + parts[2 * block + half].astype(F32)
        halves.append(total)
    total = jnp.concatenate(halves, axis=0).T
    key_grad[...] = total[0 : HD // 2, :].astype(BF16)
    value_grad[...] = total[HD // 2 :, :].astype(BF16)


def pool_kernel(keep, arrived, mine, other):
    p = lax.axis_index("yl")
    mine[...] = keep[p] + arrived[p].astype(F32)
    other[...] = (keep[1 - p] + arrived[1 - p].astype(F32)).astype(BF16)


def query_kernel(mine, arrived, query_grad):
    for h in range(OWN):
        rows = slice(h * HD, (h + 1) * HD)
        query_grad[:, rows] = (mine[rows, :] + arrived[rows, :].astype(F32)).T.astype(BF16)


def choice(ids, expert, second):
    first_hit, other_hit = ids[0:1, :] == expert, ids[1:2, :] == expert
    hit = jnp.where(first_hit | other_hit, 1.0, 0.0)
    earlier = lax.broadcasted_iota(jnp.int32, (ROWS, ROWS), 0) < lax.broadcasted_iota(jnp.int32, (ROWS, ROWS), 1)
    rank = dot_nn(
        jnp.broadcast_to(hit, (16, ROWS)).astype(BF16), jnp.where(earlier, 1.0, 0.0).astype(BF16)
    )[0:1, :].astype(jnp.int32)
    slot = second * SLOTS + lax.broadcasted_iota(jnp.int32, (SLOTS, ROWS), 0)
    return (slot == rank) & (hit > 0.0), first_hit, other_hit


def select_kernel(mine, other, ids, out):
    high = lax.axis_index("zh")
    for pair in range(4):
        for second in range(2):
            chosen, _, _ = choice(ids, high * 4 + pair, second)
            chosen = jnp.where(chosen, 1.0, 0.0).astype(BF16)
            out[2 * pair + second, high] = dot_nn(chosen, mine[...]).astype(BF16)
            out[2 * pair + second, 1 - high] = dot_nn(chosen, other[...]).astype(BF16)


def combine_kernel(rows, ids, gates, stored, gate_grad, expert_grad):
    place_in_tp = lax.axis_index("zh") * 8 + lax.axis_index("yh") * 2 + lax.axis_index("yl")
    chosen, first_hit, other_hit = choice(ids, place_in_tp // 2, place_in_tp % 2)
    gate = jnp.where(first_hit, gates[0:1, :], 0.0) + jnp.where(other_hit, gates[1:2, :], 0.0)
    slot_gate = jnp.sum(jnp.where(chosen, gate, 0.0), axis=1, keepdims=True)
    total = jnp.zeros((SLOTS, OWN * HD), F32)
    for high in range(2):
        for y in range(8):
            routed = rows[y, high].astype(F32)
            cols = slice((high * 8 + y) * OWN * HD, (high * 8 + y + 1) * OWN * HD)
            total = total + routed * stored[:, cols].astype(F32)
            expert_grad[:, cols] = (slot_gate * routed).astype(BF16)
    gate_grad[...] = jnp.sum(total.T, axis=0, keepdims=True)


def local(
    queries,
    key_rows,
    value_rows,
    out_grad,
    attn_out,
    doc_ids,
    row_grad,
    gate_weights,
    expert_ids,
    expert_out,
):
    pool, spread = call(
        prep_kernel,
        (
            jax.ShapeDtypeStruct((ROWS, 2 * OWN * HD), BF16),
            jax.ShapeDtypeStruct((Z, KB, 2 * HD), BF16),
        ),
        [pltpu.SemaphoreType.DMA((4,))],
        name="prep",
        vmem=None,
        in_specs=[pl.BlockSpec(memory_space=pltpu.HBM)] * 4,
    )(queries, out_grad, key_rows, value_rows)
    plane = lax.all_to_all(spread, "z", split_axis=0, concat_axis=0, tiled=True).reshape(PLANE, 2 * HD)
    pool_y = lax.ppermute(pool, "yl", [(0, 1), (1, 0)])
    pool_c = lax.ppermute(jnp.concatenate([pool, pool_y], axis=0), "c", [(0, 1), (1, 0)])
    plane, pool_c = lax.optimization_barrier((plane, pool_c))
    row_other = lax.ppermute(row_grad, "zh", [(0, 1), (1, 0)])
    ids = expert_ids.T
    chosen_rows = call(
        select_kernel,
        jax.ShapeDtypeStruct((8, 2, SLOTS, OWN * HD), BF16),
        [],
        flops=2 * 256 * ROWS * 2 * OWN * HD,
        name="select_rows",
    )(row_grad, row_other, ids)
    rows = lax.all_to_all(chosen_rows, ("yh", "yl"), split_axis=0, concat_axis=0, tiled=True)

    lone = [((0 * Z + 5) * 2 + 1, (3 * Z + 0) * 2 + 1)]
    ahead2 = lax.ppermute(plane, "x", [(i, i + 2) for i in range(X - 2)])
    ahead1 = lax.ppermute(plane, "x", [(i, i + 1) for i in range(X - 1)])
    aheadx = lax.ppermute(spread[0], ("x", "z", "c"), lone)

    doc = doc_ids.reshape(-1, ROWS)
    shared = (pool, pool_y, pool_c, aheadx, ahead2, ahead1, plane)
    pool_scratch = [
        pltpu.VMEM((HEADS, 2 * ROWS, HD), BF16),
        pltpu.VMEM((HEADS, 2 * ROWS, HD), BF16),
        pltpu.VMEM((PLACES, 2 * HD), BF16),
    ]
    pairs = SPAN * HEADS * 2 * ROWS
    stats = call(
        stats_kernel,
        jax.ShapeDtypeStruct((4, 32, ROWS), F32),
        pool_scratch,
        flops=2 * HD * pairs,
        name="softmax_stats",
    )(*shared, attn_out, doc)
    stats = lax.all_to_all(stats, ("c", "yl"), split_axis=0, concat_axis=0, tiled=True)
    d2, d1, d0, dx, dq_keep, dq_send = call(
        grads_kernel,
        (
            jax.ShapeDtypeStruct((PLANE, 2 * HD), BF16),
            jax.ShapeDtypeStruct((PLANE, 2 * HD), BF16),
            jax.ShapeDtypeStruct((PLANE, 2 * HD), F32),
            jax.ShapeDtypeStruct((KB, 2 * HD), BF16),
            jax.ShapeDtypeStruct((2, OWN * HD, ROWS), F32),
            jax.ShapeDtypeStruct((2, OWN * HD, ROWS), BF16),
        ),
        pool_scratch + [pltpu.VMEM((PLACES, 2 * HD), F32)],
        flops=10 * HD * pairs,
        name="score_grads",
    )(*shared, doc, stats)
    back2 = lax.ppermute(d2, "x", [(i + 2, i) for i in range(X - 2)])
    back1 = lax.ppermute(d1, "x", [(i + 1, i) for i in range(X - 1)])
    backx = lax.ppermute(dx, ("x", "z", "c"), [(b, a) for a, b in lone])
    dq_mine, dq_other = call(
        pool_kernel,
        (jax.ShapeDtypeStruct((OWN * HD, ROWS), F32), jax.ShapeDtypeStruct((OWN * HD, ROWS), BF16)),
        [],
        name="query_pool",
    )(dq_keep, lax.ppermute(dq_send, "c", [(0, 1), (1, 0)]))
    back1, dq_other = lax.optimization_barrier((back1, dq_other))
    dq_other = lax.ppermute(dq_other, "yl", [(0, 1), (1, 0)])
    plane_sums = call(plane_kernel, jax.ShapeDtypeStruct((2 * Z, KB, HD), BF16), [], name="plane_sum")(
        d0, back1, back2, backx
    )
    parts = lax.all_to_all(plane_sums, ("z", "yl"), split_axis=0, concat_axis=0, tiled=True)

    gate_grad, expert_grad = call(
        combine_kernel,
        (
            jax.ShapeDtypeStruct((1, SLOTS), F32),
            jax.ShapeDtypeStruct((SLOTS, expert_out.shape[2]), BF16),
        ),
        [],
        name="combine_grads",
    )(rows, ids, gate_weights.T, expert_out[0])
    query_grad = call(query_kernel, jax.ShapeDtypeStruct((ROWS, OWN * HD), BF16), [], name="query_sum")(
        dq_mine, dq_other
    )
    parts, expert_grad, query_grad = lax.optimization_barrier((parts, expert_grad, query_grad))
    key_grad, value_grad = call(
        block_kernel,
        (jax.ShapeDtypeStruct((HD // 2, ROWS), BF16), jax.ShapeDtypeStruct((HD // 2, ROWS), BF16)),
        [],
        name="block_sum",
    )(parts)
    return (query_grad, key_grad.T, value_grad.T, gate_grad, expert_grad[None])


def solution(mesh):
    devices = mesh.devices.reshape(X, Z, 2, 2, 4, 2)
    split = Mesh(devices, ("x", "z", "c", "zh", "yh", "yl"))
    ctx, tp = ("x", "z", "c"), ("zh", "yh", "yl")
    in_specs = (
        P(ctx, tp),
        P(ctx, None),
        P(ctx, None),
        P(ctx, tp),
        P(ctx, tp),
        P(),
        P(ctx, tp),
        P(ctx, None),
        P(ctx, None),
        P(ctx, tp, None),
    )
    out_specs = (P(ctx, tp), P(ctx, tp), P(ctx, tp), P(ctx, tp), P(ctx, tp, None))
    return jax.shard_map(local, mesh=split, in_specs=in_specs, out_specs=out_specs, check_vma=False)
```

```python
import functools
import math

import jax
import jax.numpy as jnp
from jax import lax
from jax.experimental import pallas as pl
from jax.experimental.pallas import tpu as pltpu
from jax.sharding import Mesh
from jax.sharding import PartitionSpec as P

HD = 128
X, Z = 4, 6
ROWS = 128
KB = 64
PLANE = Z * KB
HEADS = 6
OWN = 3
WINDOW = 14
SPAN = WINDOW * KB
PLACES = KB + 3 * PLANE
SCALE = 1.0 / math.sqrt(HD)
LOG2E = 1.4426950408889634
NEG = -1e30
SLOTS = 32

F32 = jnp.float32
BF16 = jnp.bfloat16
VMEM_LIMIT = 48 * 1024 * 1024


def dot_nt(a, b):
    return lax.dot_general(a, b, (((1,), (1,)), ((), ())), preferred_element_type=F32)


def dot_nn(a, b):
    return lax.dot_general(a, b, (((1,), (0,)), ((), ())), preferred_element_type=F32)


def call(kernel, out_shape, scratch_shapes, flops=0, nbytes=1 << 20, name=None, vmem=VMEM_LIMIT, **specs):
    return pl.pallas_call(
        kernel,
        out_shape=out_shape,
        scratch_shapes=scratch_shapes,
        compiler_params=pltpu.CompilerParams(vmem_limit_bytes=vmem),
        cost_estimate=pl.CostEstimate(flops=flops, bytes_accessed=nbytes, transcendentals=0),
        name=name,
        **specs,
    )


def place(z, c, p, parts, q_s, do_s, kv_s):
    qd, qd_y, qd_c, kvx, kv2, kv1, kv0 = parts
    for owner, ref, base in ((p, qd, 0), (1 - p, qd_y, 0)):
        for h in range(OWN):
            q_s[owner * OWN + h, pl.ds(c * ROWS, ROWS), :] = ref[:, h * HD : (h + 1) * HD]
            do_s[owner * OWN + h, pl.ds(c * ROWS, ROWS), :] = ref[:, (OWN + h) * HD : (OWN + h + 1) * HD]
    for owner, base in ((p, 0), (1 - p, ROWS)):
        for h in range(OWN):
            q_s[owner * OWN + h, pl.ds((1 - c) * ROWS, ROWS), :] = qd_c[base : base + ROWS, h * HD : (h + 1) * HD]
            do_s[owner * OWN + h, pl.ds((1 - c) * ROWS, ROWS), :] = qd_c[
                base : base + ROWS, (OWN + h) * HD : (OWN + h + 1) * HD
            ]
    kv_s[0:KB, :] = kvx[...]
    kv_s[KB : KB + PLANE, :] = kv2[...]
    kv_s[KB + PLANE : KB + 2 * PLANE, :] = kv1[...]
    kv_s[KB + 2 * PLANE : KB + 3 * PLANE, :] = kv0[...]


def query_spans(doc, chip):
    docs = doc[...]
    mine = jnp.concatenate([doc[pl.ds(2 * chip, 1), :], doc[pl.ds(2 * chip + 1, 1), :]], axis=1)
    first = jnp.zeros((1, 2 * ROWS), jnp.int32)
    for d in range(1, 8):
        before = jnp.sum((docs < d).astype(F32)).astype(jnp.int32)
        first = jnp.where(mine == d, before, first)
    last = chip * 2 * ROWS + lax.broadcasted_iota(jnp.int32, (1, 2 * ROWS), 1)
    return first, last


def bias_of(chip, c, p, first, last):
    i = lax.broadcasted_iota(jnp.int32, (SPAN, 2 * ROWS), 0)
    base = (2 * (chip - (WINDOW - 1)) + c) * ROWS + p * KB
    pos = base + (i // KB) * (2 * ROWS) + i % KB
    return jnp.where((pos >= first) & (pos <= last), 0.0, NEG)


def prep_kernel(queries, out_grad, key_rows, value_rows, pool, spread, own, sems):
    group = lax.axis_index("zh") * 4 + lax.axis_index("yh")
    rows = pl.ds(pl.multiple_of(lax.axis_index("yl") * KB, KB), KB)
    cols = pl.ds(pl.multiple_of(group * HD, HD), HD)
    copies = [
        pltpu.make_async_copy(key_rows.at[rows, cols], spread.at[0, :, 0:HD], sems.at[0]),
        pltpu.make_async_copy(value_rows.at[rows, cols], spread.at[0, :, HD : 2 * HD], sems.at[1]),
        pltpu.make_async_copy(queries, pool.at[:, 0 : OWN * HD], sems.at[2]),
        pltpu.make_async_copy(out_grad, pool.at[:, OWN * HD : 2 * OWN * HD], sems.at[3]),
    ]
    for copy in copies:
        copy.start()
    copies[0].wait()
    copies[1].wait()
    for block in range(1, Z):
        spread[block] = spread[0]
    own[...] = spread[0]
    copies[2].wait()
    copies[3].wait()


def stats_kernel(qd, qd_y, qd_c, kvx, kv2, kv1, kv0, o_own, doc, stats, q_s, do_s, kv_s):
    x, z, c, p = (lax.axis_index(a) for a in ("x", "z", "c", "yl"))
    chip = x * Z + z
    place(z, c, p, (qd, qd_y, qd_c, kvx, kv2, kv1, kv0), q_s, do_s, kv_s)
    first, last = query_spans(doc, chip)
    keys = kv_s[pl.ds(pl.multiple_of(z * KB, KB), SPAN), 0:HD]
    bias = bias_of(chip, c, p, first, last)
    rows = []
    for h in range(HEADS):
        s = dot_nt(keys, q_s[h]) * (SCALE * LOG2E) + bias
        s = s.reshape(SPAN // 8, 8, 2 * ROWS)
        fold = jnp.max(s, axis=0)
        sums = jnp.sum(jnp.exp2(s - fold[None]), axis=0)
        top = jnp.max(fold, axis=0, keepdims=True)
        total = jnp.sum(sums * jnp.exp2(fold - top), axis=0, keepdims=True)
        for r in range(2):
            rows.append((2 * h + r, top[:, r * ROWS : (r + 1) * ROWS]))
            rows.append((12 + 2 * h + r, total[:, r * ROWS : (r + 1) * ROWS]))
    for h in range(OWN):
        prod = qd[:, (OWN + h) * HD : (OWN + h + 1) * HD].astype(F32) * o_own[:, h * HD : (h + 1) * HD].astype(F32)
        rows.append((24 + h, jnp.sum(prod.T, axis=0, keepdims=True)))
    for peer in range(4):
        for at, row in rows:
            stats[peer, at : at + 1, :] = row
        stats[peer, 27:32, :] = jnp.zeros((5, ROWS), F32)


def grads_kernel(
    qd, qd_y, qd_c, kvx, kv2, kv1, kv0, doc, stats, d2, d1, d0, dx, dq_keep, dq_send, q_s, do_s, kv_s, acc_s
):
    x, z, c, p = (lax.axis_index(a) for a in ("x", "z", "c", "yl"))
    chip = x * Z + z
    place(z, c, p, (qd, qd_y, qd_c, kvx, kv2, kv1, kv0), q_s, do_s, kv_s)
    first, last = query_spans(doc, chip)
    acc_s[...] = jnp.zeros(acc_s.shape, F32)
    tops = [stats[i, 0:12, :] for i in range(4)]
    top = jnp.maximum(jnp.maximum(tops[0], tops[1]), jnp.maximum(tops[2], tops[3]))
    total = sum(stats[i, 12:24, :] * jnp.exp2(tops[i] - top) for i in range(4))
    lse = top + jnp.log(total) * LOG2E

    at = pl.multiple_of(z * KB, KB)
    keys = kv_s[pl.ds(at, SPAN), 0:HD]
    values = kv_s[pl.ds(at, SPAN), HD : 2 * HD]
    keys_t = keys.astype(F32).T.astype(BF16)
    bias = bias_of(chip, c, p, first, last)
    dk = jnp.zeros((SPAN, HD), F32)
    dv = jnp.zeros((SPAN, HD), F32)
    for h in range(HEADS):
        owner, k = h // OWN, 24 + h % OWN
        row_lse = jnp.concatenate([lse[2 * h : 2 * h + 1, :], lse[2 * h + 1 : 2 * h + 2, :]], axis=1)
        delta = jnp.concatenate([stats[owner, k : k + 1, :], stats[2 + owner, k : k + 1, :]], axis=1)
        q, do = q_s[h], do_s[h]
        probs = jnp.exp2(dot_nt(keys, q) * (SCALE * LOG2E) + bias - row_lse)
        score = (probs * (dot_nt(values, do) - delta)).astype(BF16)
        dv = dv + dot_nn(probs.astype(BF16), do)
        dk = dk + dot_nn(score, q)
        part = dot_nn(keys_t, score) * SCALE
        lower, upper = part[:, 0:ROWS], part[:, ROWS : 2 * ROWS]
        rows = slice((h % OWN) * HD, (h % OWN + 1) * HD)
        dq_keep[owner, rows, :] = jnp.where(c == 0, lower, upper)
        dq_send[owner, rows, :] = jnp.where(c == 0, upper, lower).astype(BF16)
    acc_s[pl.ds(at, SPAN), 0:HD] = dk * SCALE
    acc_s[pl.ds(at, SPAN), HD : 2 * HD] = dv
    for ref, start, size in (
        (dx, 0, KB),
        (d2, KB, PLANE),
        (d1, KB + PLANE, PLANE),
        (d0, KB + 2 * PLANE, PLANE),
    ):
        dk, dv = acc_s[start : start + size, 0:HD], acc_s[start : start + size, HD : 2 * HD]
        low = lax.broadcasted_iota(jnp.int32, (size, HD), 1) < HD // 2
        ref[:, 0:HD] = jnp.where(low, dk, pltpu.roll(dv, HD // 2, 1)).astype(ref.dtype)
        ref[:, HD : 2 * HD] = jnp.where(low, pltpu.roll(dk, HD // 2, 1), dv).astype(ref.dtype)


def plane_kernel(d0, r1, r2, rx, out):
    for block in range(Z):
        rows = slice(block * KB, (block + 1) * KB)
        total = d0[rows, :] + r1[rows, :].astype(F32) + r2[rows, :].astype(F32)
        if block == Z - 1:
            total = total + rx[...].astype(F32)
        for half in range(2):
            out[2 * block + half] = total[:, half * HD : (half + 1) * HD].astype(BF16)


def block_kernel(parts, key_grad, value_grad):
    halves = []
    for half in range(2):
        total = parts[half].astype(F32)
        for block in range(1, Z):
            total = total + parts[2 * block + half].astype(F32)
        halves.append(total)
    total = jnp.concatenate(halves, axis=0).T
    key_grad[...] = total[0 : HD // 2, :].astype(BF16)
    value_grad[...] = total[HD // 2 :, :].astype(BF16)


def pool_kernel(keep, arrived, mine, other):
    p = lax.axis_index("yl")
    mine[...] = keep[p] + arrived[p].astype(F32)
    other[...] = (keep[1 - p] + arrived[1 - p].astype(F32)).astype(BF16)


def query_kernel(mine, arrived, query_grad):
    for h in range(OWN):
        rows = slice(h * HD, (h + 1) * HD)
        query_grad[:, rows] = (mine[rows, :] + arrived[rows, :].astype(F32)).T.astype(BF16)


def choice(ids, expert, second):
    first_hit, other_hit = ids[0:1, :] == expert, ids[1:2, :] == expert
    hit = jnp.where(first_hit | other_hit, 1.0, 0.0)
    earlier = lax.broadcasted_iota(jnp.int32, (ROWS, ROWS), 0) < lax.broadcasted_iota(jnp.int32, (ROWS, ROWS), 1)
    rank = dot_nn(
        jnp.broadcast_to(hit, (16, ROWS)).astype(BF16), jnp.where(earlier, 1.0, 0.0).astype(BF16)
    )[0:1, :].astype(jnp.int32)
    slot = second * SLOTS + lax.broadcasted_iota(jnp.int32, (SLOTS, ROWS), 0)
    return (slot == rank) & (hit > 0.0), first_hit, other_hit


def select_kernel(mine, other, ids, out):
    high = lax.axis_index("zh")
    for pair in range(4):
        for second in range(2):
            chosen, _, _ = choice(ids, high * 4 + pair, second)
            chosen = jnp.where(chosen, 1.0, 0.0).astype(BF16)
            out[2 * pair + second, high] = dot_nn(chosen, mine[...]).astype(BF16)
            out[2 * pair + second, 1 - high] = dot_nn(chosen, other[...]).astype(BF16)


def combine_kernel(rows, ids, gates, stored, gate_grad, expert_grad):
    place_in_tp = lax.axis_index("zh") * 8 + lax.axis_index("yh") * 2 + lax.axis_index("yl")
    chosen, first_hit, other_hit = choice(ids, place_in_tp // 2, place_in_tp % 2)
    gate = jnp.where(first_hit, gates[0:1, :], 0.0) + jnp.where(other_hit, gates[1:2, :], 0.0)
    slot_gate = jnp.sum(jnp.where(chosen, gate, 0.0), axis=1, keepdims=True)
    total = jnp.zeros((SLOTS, OWN * HD), F32)
    for high in range(2):
        for y in range(8):
            routed = rows[y, high].astype(F32)
            cols = slice((high * 8 + y) * OWN * HD, (high * 8 + y + 1) * OWN * HD)
            total = total + routed * stored[:, cols].astype(F32)
            expert_grad[:, cols] = (slot_gate * routed).astype(BF16)
    gate_grad[...] = jnp.sum(total.T, axis=0, keepdims=True)


def local(
    queries,
    key_rows,
    value_rows,
    out_grad,
    attn_out,
    doc_ids,
    row_grad,
    gate_weights,
    expert_ids,
    expert_out,
):
    pool, spread, own = call(
        prep_kernel,
        (
            jax.ShapeDtypeStruct((ROWS, 2 * OWN * HD), BF16),
            jax.ShapeDtypeStruct((Z, KB, 2 * HD), BF16),
            jax.ShapeDtypeStruct((KB, 2 * HD), BF16),
        ),
        [pltpu.SemaphoreType.DMA((4,))],
        name="prep",
        vmem=None,
        in_specs=[pl.BlockSpec(memory_space=pltpu.HBM)] * 4,
    )(queries, out_grad, key_rows, value_rows)
    plane = lax.all_to_all(spread, "z", split_axis=0, concat_axis=0, tiled=True).reshape(PLANE, 2 * HD)
    pool_y = lax.ppermute(pool, "yl", [(0, 1), (1, 0)])
    pool_c = lax.ppermute(jnp.concatenate([pool, pool_y], axis=0), "c", [(0, 1), (1, 0)])
    plane, pool_c = lax.optimization_barrier((plane, pool_c))
    row_other = lax.ppermute(row_grad, "zh", [(0, 1), (1, 0)])
    ids = expert_ids.T
    chosen_rows = call(
        select_kernel,
        jax.ShapeDtypeStruct((8, 2, SLOTS, OWN * HD), BF16),
        [],
        flops=2 * 256 * ROWS * 2 * OWN * HD,
        name="select_rows",
    )(row_grad, row_other, ids)
    rows = lax.all_to_all(chosen_rows, ("yh", "yl"), split_axis=0, concat_axis=0, tiled=True)

    lone = [((0 * Z + 5) * 2 + 1, (3 * Z + 0) * 2 + 1)]
    ahead2 = lax.ppermute(plane, "x", [(i, i + 2) for i in range(X - 2)])
    ahead1 = lax.ppermute(plane, "x", [(i, i + 1) for i in range(X - 1)])
    aheadx = lax.ppermute(own, ("x", "z", "c"), lone)

    doc = doc_ids.reshape(-1, ROWS)
    shared = (pool, pool_y, pool_c, aheadx, ahead2, ahead1, plane)
    pool_scratch = [
        pltpu.VMEM((HEADS, 2 * ROWS, HD), BF16),
        pltpu.VMEM((HEADS, 2 * ROWS, HD), BF16),
        pltpu.VMEM((PLACES, 2 * HD), BF16),
    ]
    pairs = SPAN * HEADS * 2 * ROWS
    stats = call(
        stats_kernel,
        jax.ShapeDtypeStruct((4, 32, ROWS), F32),
        pool_scratch,
        flops=2 * HD * pairs,
        name="softmax_stats",
    )(*shared, attn_out, doc)
    stats = lax.all_to_all(stats, ("c", "yl"), split_axis=0, concat_axis=0, tiled=True)
    gate_grad, expert_grad = call(
        combine_kernel,
        (
            jax.ShapeDtypeStruct((1, SLOTS), F32),
            jax.ShapeDtypeStruct((SLOTS, expert_out.shape[2]), BF16),
        ),
        [],
        name="combine_grads",
    )(rows, ids, gate_weights.T, expert_out[0])
    d2, d1, d0, dx, dq_keep, dq_send = call(
        grads_kernel,
        (
            jax.ShapeDtypeStruct((PLANE, 2 * HD), BF16),
            jax.ShapeDtypeStruct((PLANE, 2 * HD), BF16),
            jax.ShapeDtypeStruct((PLANE, 2 * HD), F32),
            jax.ShapeDtypeStruct((KB, 2 * HD), BF16),
            jax.ShapeDtypeStruct((2, OWN * HD, ROWS), F32),
            jax.ShapeDtypeStruct((2, OWN * HD, ROWS), BF16),
        ),
        pool_scratch + [pltpu.VMEM((PLACES, 2 * HD), F32)],
        flops=10 * HD * pairs,
        name="score_grads",
    )(*shared, doc, stats)
    back2 = lax.ppermute(d2, "x", [(i + 2, i) for i in range(X - 2)])
    back1 = lax.ppermute(d1, "x", [(i + 1, i) for i in range(X - 1)])
    backx = lax.ppermute(dx, ("x", "z", "c"), [(b, a) for a, b in lone])
    dq_mine, dq_other = call(
        pool_kernel,
        (jax.ShapeDtypeStruct((OWN * HD, ROWS), F32), jax.ShapeDtypeStruct((OWN * HD, ROWS), BF16)),
        [],
        name="query_pool",
        nbytes=1,
    )(dq_keep, lax.ppermute(dq_send, "c", [(0, 1), (1, 0)]))
    back1, dq_other = lax.optimization_barrier((back1, dq_other))
    dq_other = lax.ppermute(dq_other, "yl", [(0, 1), (1, 0)])
    plane_sums = call(plane_kernel, jax.ShapeDtypeStruct((2 * Z, KB, HD), BF16), [], name="plane_sum")(
        d0, back1, back2, backx
    )
    plane_sums, _ = lax.optimization_barrier((plane_sums, dq_other))
    parts = lax.all_to_all(plane_sums, ("z", "yl"), split_axis=0, concat_axis=0, tiled=True)

    query_grad = call(query_kernel, jax.ShapeDtypeStruct((ROWS, OWN * HD), BF16), [], name="query_sum")(
        dq_mine, dq_other
    )
    parts, query_grad = lax.optimization_barrier((parts, query_grad))
    key_grad, value_grad = call(
        block_kernel,
        (jax.ShapeDtypeStruct((HD // 2, ROWS), BF16), jax.ShapeDtypeStruct((HD // 2, ROWS), BF16)),
        [],
        name="block_sum",
    )(parts)
    return (query_grad, key_grad.T, value_grad.T, gate_grad, expert_grad[None])


def solution(mesh):
    devices = mesh.devices.reshape(X, Z, 2, 2, 4, 2)
    split = Mesh(devices, ("x", "z", "c", "zh", "yh", "yl"))
    ctx, tp = ("x", "z", "c"), ("zh", "yh", "yl")
    in_specs = (
        P(ctx, tp),
        P(ctx, None),
        P(ctx, None),
        P(ctx, tp),
        P(ctx, tp),
        P(),
        P(ctx, tp),
        P(ctx, None),
        P(ctx, None),
        P(ctx, tp, None),
    )
    out_specs = (P(ctx, tp), P(ctx, tp), P(ctx, tp), P(ctx, tp), P(ctx, tp, None))
    return jax.shard_map(local, mesh=split, in_specs=in_specs, out_specs=out_specs, check_vma=False)
```

```python
import functools
import math

import jax
import jax.numpy as jnp
from jax import lax
from jax.experimental import pallas as pl
from jax.experimental.pallas import tpu as pltpu
from jax.sharding import Mesh
from jax.sharding import PartitionSpec as P

HD = 128
X, Z = 4, 6
ROWS = 128
KB = 64
PLANE = Z * KB
HEADS = 6
OWN = 3
WINDOW = 14
SPAN = WINDOW * KB
PLACES = KB + 3 * PLANE
SCALE = 1.0 / math.sqrt(HD)
LOG2E = 1.4426950408889634
NEG = -1e30
SLOTS = 32

F32 = jnp.float32
BF16 = jnp.bfloat16
VMEM_LIMIT = 48 * 1024 * 1024


def dot_nt(a, b):
    return lax.dot_general(a, b, (((1,), (1,)), ((), ())), preferred_element_type=F32)


def dot_nn(a, b):
    return lax.dot_general(a, b, (((1,), (0,)), ((), ())), preferred_element_type=F32)


def call(kernel, out_shape, scratch_shapes, flops=0, nbytes=1 << 20, name=None, vmem=VMEM_LIMIT, **specs):
    return pl.pallas_call(
        kernel,
        out_shape=out_shape,
        scratch_shapes=scratch_shapes,
        compiler_params=pltpu.CompilerParams(vmem_limit_bytes=vmem),
        cost_estimate=pl.CostEstimate(flops=flops, bytes_accessed=nbytes, transcendentals=0),
        name=name,
        **specs,
    )


def place(z, c, p, parts, q_s, do_s, kv_s):
    qd, qd_c, qd_y, kvx, kv2, kv1, kv0 = parts
    for owner, core, ref, base in (
        (p, c, qd, 0),
        (p, 1 - c, qd_c, 0),
        (1 - p, c, qd_y, 0),
        (1 - p, 1 - c, qd_y, ROWS),
    ):
        for h in range(OWN):
            q_s[owner * OWN + h, pl.ds(core * ROWS, ROWS), :] = ref[base : base + ROWS, h * HD : (h + 1) * HD]
            do_s[owner * OWN + h, pl.ds(core * ROWS, ROWS), :] = ref[
                base : base + ROWS, (OWN + h) * HD : (OWN + h + 1) * HD
            ]
    kv_s[0:KB, :] = kvx[...]
    kv_s[KB : KB + PLANE, :] = kv2[...]
    kv_s[KB + PLANE : KB + 2 * PLANE, :] = kv1[...]
    kv_s[KB + 2 * PLANE : KB + 3 * PLANE, :] = kv0[...]


def query_spans(doc, chip):
    docs = doc[...]
    mine = jnp.concatenate([doc[pl.ds(2 * chip, 1), :], doc[pl.ds(2 * chip + 1, 1), :]], axis=1)
    first = jnp.zeros((1, 2 * ROWS), jnp.int32)
    for d in range(1, 8):
        before = jnp.sum((docs < d).astype(F32)).astype(jnp.int32)
        first = jnp.where(mine == d, before, first)
    last = chip * 2 * ROWS + lax.broadcasted_iota(jnp.int32, (1, 2 * ROWS), 1)
    return first, last


def bias_of(chip, c, p, first, last):
    i = lax.broadcasted_iota(jnp.int32, (SPAN, 2 * ROWS), 0)
    base = (2 * (chip - (WINDOW - 1)) + c) * ROWS + p * KB
    pos = base + (i // KB) * (2 * ROWS) + i % KB
    return jnp.where((pos >= first) & (pos <= last), 0.0, NEG)


def prep_kernel(queries, out_grad, key_rows, value_rows, pool, spread, own, sems):
    group = lax.axis_index("zh") * 4 + lax.axis_index("yh")
    rows = pl.ds(pl.multiple_of(lax.axis_index("yl") * KB, KB), KB)
    cols = pl.ds(pl.multiple_of(group * HD, HD), HD)
    copies = [
        pltpu.make_async_copy(key_rows.at[rows, cols], spread.at[0, :, 0:HD], sems.at[0]),
        pltpu.make_async_copy(value_rows.at[rows, cols], spread.at[0, :, HD : 2 * HD], sems.at[1]),
        pltpu.make_async_copy(queries, pool.at[:, 0 : OWN * HD], sems.at[2]),
        pltpu.make_async_copy(out_grad, pool.at[:, OWN * HD : 2 * OWN * HD], sems.at[3]),
    ]
    for copy in copies:
        copy.start()
    copies[0].wait()
    copies[1].wait()
    for block in range(1, Z):
        spread[block] = spread[0]
    own[...] = spread[0]
    copies[2].wait()
    copies[3].wait()


def stats_kernel(qd, qd_c, qd_y, kvx, kv2, kv1, kv0, o_own, doc, stats, q_s, do_s, kv_s):
    x, z, c, p = (lax.axis_index(a) for a in ("x", "z", "c", "yl"))
    chip = x * Z + z
    place(z, c, p, (qd, qd_c, qd_y, kvx, kv2, kv1, kv0), q_s, do_s, kv_s)
    first, last = query_spans(doc, chip)
    keys = kv_s[pl.ds(pl.multiple_of(z * KB, KB), SPAN), 0:HD]
    bias = bias_of(chip, c, p, first, last)
    rows = []
    for h in range(HEADS):
        s = dot_nt(keys, q_s[h]) * (SCALE * LOG2E) + bias
        s = s.reshape(SPAN // 8, 8, 2 * ROWS)
        fold = jnp.max(s, axis=0)
        sums = jnp.sum(jnp.exp2(s - fold[None]), axis=0)
        top = jnp.max(fold, axis=0, keepdims=True)
        total = jnp.sum(sums * jnp.exp2(fold - top), axis=0, keepdims=True)
        for r in range(2):
            rows.append((2 * h + r, top[:, r * ROWS : (r + 1) * ROWS]))
            rows.append((12 + 2 * h + r, total[:, r * ROWS : (r + 1) * ROWS]))
    for h in range(OWN):
        prod = qd[:, (OWN + h) * HD : (OWN + h + 1) * HD].astype(F32) * o_own[:, h * HD : (h + 1) * HD].astype(F32)
        rows.append((24 + h, jnp.sum(prod.T, axis=0, keepdims=True)))
    for peer in range(4):
        for at, row in rows:
            stats[peer, at : at + 1, :] = row
        stats[peer, 27:32, :] = jnp.zeros((5, ROWS), F32)


def grads_kernel(
    qd, qd_c, qd_y, kvx, kv2, kv1, kv0, doc, stats, d2, d1, d0, dx, dq_keep, dq_send, q_s, do_s, kv_s, acc_s
):
    x, z, c, p = (lax.axis_index(a) for a in ("x", "z", "c", "yl"))
    chip = x * Z + z
    place(z, c, p, (qd, qd_c, qd_y, kvx, kv2, kv1, kv0), q_s, do_s, kv_s)
    first, last = query_spans(doc, chip)
    acc_s[...] = jnp.zeros(acc_s.shape, F32)
    tops = [stats[i, 0:12, :] for i in range(4)]
    top = jnp.maximum(jnp.maximum(tops[0], tops[1]), jnp.maximum(tops[2], tops[3]))
    total = sum(stats[i, 12:24, :] * jnp.exp2(tops[i] - top) for i in range(4))
    lse = top + jnp.log(total) * LOG2E

    at = pl.multiple_of(z * KB, KB)
    keys = kv_s[pl.ds(at, SPAN), 0:HD]
    values = kv_s[pl.ds(at, SPAN), HD : 2 * HD]
    keys_t = keys.astype(F32).T.astype(BF16)
    bias = bias_of(chip, c, p, first, last)
    dk = jnp.zeros((SPAN, HD), F32)
    dv = jnp.zeros((SPAN, HD), F32)
    for h in range(HEADS):
        owner, k = h // OWN, 24 + h % OWN
        row_lse = jnp.concatenate([lse[2 * h : 2 * h + 1, :], lse[2 * h + 1 : 2 * h + 2, :]], axis=1)
        delta = jnp.concatenate([stats[owner, k : k + 1, :], stats[2 + owner, k : k + 1, :]], axis=1)
        q, do = q_s[h], do_s[h]
        probs = jnp.exp2(dot_nt(keys, q) * (SCALE * LOG2E) + bias - row_lse)
        score = (probs * (dot_nt(values, do) - delta)).astype(BF16)
        dv = dv + dot_nn(probs.astype(BF16), do)
        dk = dk + dot_nn(score, q)
        part = dot_nn(keys_t, score) * SCALE
        lower, upper = part[:, 0:ROWS], part[:, ROWS : 2 * ROWS]
        rows = slice((h % OWN) * HD, (h % OWN + 1) * HD)
        dq_keep[owner, rows, :] = jnp.where(c == 0, lower, upper)
        dq_send[owner, rows, :] = jnp.where(c == 0, upper, lower).astype(BF16)
    acc_s[pl.ds(at, SPAN), 0:HD] = dk * SCALE
    acc_s[pl.ds(at, SPAN), HD : 2 * HD] = dv
    for ref, start, size in (
        (dx, 0, KB),
        (d2, KB, PLANE),
        (d1, KB + PLANE, PLANE),
        (d0, KB + 2 * PLANE, PLANE),
    ):
        dk, dv = acc_s[start : start + size, 0:HD], acc_s[start : start + size, HD : 2 * HD]
        low = lax.broadcasted_iota(jnp.int32, (size, HD), 1) < HD // 2
        ref[:, 0:HD] = jnp.where(low, dk, pltpu.roll(dv, HD // 2, 1)).astype(ref.dtype)
        ref[:, HD : 2 * HD] = jnp.where(low, pltpu.roll(dk, HD // 2, 1), dv).astype(ref.dtype)


def plane_kernel(d0, r1, r2, rx, out):
    for block in range(Z):
        rows = slice(block * KB, (block + 1) * KB)
        total = d0[rows, :] + r1[rows, :].astype(F32) + r2[rows, :].astype(F32)
        if block == Z - 1:
            total = total + rx[...].astype(F32)
        for half in range(2):
            out[2 * block + half] = total[:, half * HD : (half + 1) * HD].astype(BF16)


def block_kernel(parts, key_grad, value_grad):
    halves = []
    for half in range(2):
        total = parts[half].astype(F32)
        for block in range(1, Z):
            total = total + parts[2 * block + half].astype(F32)
        halves.append(total)
    total = jnp.concatenate(halves, axis=0).T
    key_grad[...] = total[0 : HD // 2, :].astype(BF16)
    value_grad[...] = total[HD // 2 :, :].astype(BF16)


def pool_kernel(keep, arrived, mine, other):
    p = lax.axis_index("yl")
    mine[...] = keep[p] + arrived[p].astype(F32)
    other[...] = (keep[1 - p] + arrived[1 - p].astype(F32)).astype(BF16)


def query_kernel(mine, arrived, query_grad):
    for h in range(OWN):
        rows = slice(h * HD, (h + 1) * HD)
        query_grad[:, rows] = (mine[rows, :] + arrived[rows, :].astype(F32)).T.astype(BF16)


def choice(ids, expert, second):
    first_hit, other_hit = ids[0:1, :] == expert, ids[1:2, :] == expert
    hit = jnp.where(first_hit | other_hit, 1.0, 0.0)
    earlier = lax.broadcasted_iota(jnp.int32, (ROWS, ROWS), 0) < lax.broadcasted_iota(jnp.int32, (ROWS, ROWS), 1)
    rank = dot_nn(
        jnp.broadcast_to(hit, (16, ROWS)).astype(BF16), jnp.where(earlier, 1.0, 0.0).astype(BF16)
    )[0:1, :].astype(jnp.int32)
    slot = second * SLOTS + lax.broadcasted_iota(jnp.int32, (SLOTS, ROWS), 0)
    return (slot == rank) & (hit > 0.0), first_hit, other_hit


def select_kernel(mine, other, ids, out):
    high = lax.axis_index("zh")
    for pair in range(4):
        for second in range(2):
            chosen, _, _ = choice(ids, high * 4 + pair, second)
            chosen = jnp.where(chosen, 1.0, 0.0).astype(BF16)
            out[2 * pair + second, high] = dot_nn(chosen, mine[...]).astype(BF16)
            out[2 * pair + second, 1 - high] = dot_nn(chosen, other[...]).astype(BF16)


def combine_kernel(rows, ids, gates, stored, gate_grad, expert_grad):
    place_in_tp = lax.axis_index("zh") * 8 + lax.axis_index("yh") * 2 + lax.axis_index("yl")
    chosen, first_hit, other_hit = choice(ids, place_in_tp // 2, place_in_tp % 2)
    gate = jnp.where(first_hit, gates[0:1, :], 0.0) + jnp.where(other_hit, gates[1:2, :], 0.0)
    slot_gate = jnp.sum(jnp.where(chosen, gate, 0.0), axis=1, keepdims=True)
    total = jnp.zeros((SLOTS, OWN * HD), F32)
    for high in range(2):
        for y in range(8):
            routed = rows[y, high].astype(F32)
            cols = slice((high * 8 + y) * OWN * HD, (high * 8 + y + 1) * OWN * HD)
            total = total + routed * stored[:, cols].astype(F32)
            expert_grad[:, cols] = (slot_gate * routed).astype(BF16)
    gate_grad[...] = jnp.sum(total.T, axis=0, keepdims=True)


def local(
    queries,
    key_rows,
    value_rows,
    out_grad,
    attn_out,
    doc_ids,
    row_grad,
    gate_weights,
    expert_ids,
    expert_out,
):
    pool, spread, own = call(
        prep_kernel,
        (
            jax.ShapeDtypeStruct((ROWS, 2 * OWN * HD), BF16),
            jax.ShapeDtypeStruct((Z, KB, 2 * HD), BF16),
            jax.ShapeDtypeStruct((KB, 2 * HD), BF16),
        ),
        [pltpu.SemaphoreType.DMA((4,))],
        name="prep",
        vmem=None,
        in_specs=[pl.BlockSpec(memory_space=pltpu.HBM)] * 4,
    )(queries, out_grad, key_rows, value_rows)
    plane = lax.all_to_all(spread, "z", split_axis=0, concat_axis=0, tiled=True).reshape(PLANE, 2 * HD)
    pool_c = lax.ppermute(pool, "c", [(0, 1), (1, 0)])
    pool_y = lax.ppermute(jnp.concatenate([pool, pool_c], axis=0), "yl", [(0, 1), (1, 0)])
    row_other = lax.ppermute(row_grad, "zh", [(0, 1), (1, 0)])
    ids = expert_ids.T
    chosen_rows = call(
        select_kernel,
        jax.ShapeDtypeStruct((8, 2, SLOTS, OWN * HD), BF16),
        [],
        flops=400 * 256 * ROWS * 2 * OWN * HD,
        name="select_rows",
    )(row_grad, row_other, ids)
    rows = lax.all_to_all(chosen_rows, ("yh", "yl"), split_axis=0, concat_axis=0, tiled=True)

    lone = [((0 * Z + 5) * 2 + 1, (3 * Z + 0) * 2 + 1)]
    ahead2 = lax.ppermute(plane, "x", [(i, i + 2) for i in range(X - 2)])
    ahead1 = lax.ppermute(plane, "x", [(i, i + 1) for i in range(X - 1)])
    aheadx = lax.ppermute(own, ("x", "z", "c"), lone)

    doc = doc_ids.reshape(-1, ROWS)
    shared = (pool, pool_c, pool_y, aheadx, ahead2, ahead1, plane)
    pool_scratch = [
        pltpu.VMEM((HEADS, 2 * ROWS, HD), BF16),
        pltpu.VMEM((HEADS, 2 * ROWS, HD), BF16),
        pltpu.VMEM((PLACES, 2 * HD), BF16),
    ]
    pairs = SPAN * HEADS * 2 * ROWS
    stats = call(
        stats_kernel,
        jax.ShapeDtypeStruct((4, 32, ROWS), F32),
        pool_scratch,
        flops=30 * 2 * HD * pairs,
        name="softmax_stats",
    )(*shared, attn_out, doc)
    stats, _ = lax.optimization_barrier((stats, rows))
    stats = lax.all_to_all(stats, ("c", "yl"), split_axis=0, concat_axis=0, tiled=True)
    gate_grad, expert_grad = call(
        combine_kernel,
        (
            jax.ShapeDtypeStruct((1, SLOTS), F32),
            jax.ShapeDtypeStruct((SLOTS, expert_out.shape[2]), BF16),
        ),
        [],
        name="combine_grads",
    )(rows, ids, gate_weights.T, expert_out[0])
    stats, _ = lax.optimization_barrier((stats, expert_grad))
    d2, d1, d0, dx, dq_keep, dq_send = call(
        grads_kernel,
        (
            jax.ShapeDtypeStruct((PLANE, 2 * HD), BF16),
            jax.ShapeDtypeStruct((PLANE, 2 * HD), BF16),
            jax.ShapeDtypeStruct((PLANE, 2 * HD), F32),
            jax.ShapeDtypeStruct((KB, 2 * HD), BF16),
            jax.ShapeDtypeStruct((2, OWN * HD, ROWS), F32),
            jax.ShapeDtypeStruct((2, OWN * HD, ROWS), BF16),
        ),
        pool_scratch + [pltpu.VMEM((PLACES, 2 * HD), F32)],
        flops=10 * HD * pairs,
        name="score_grads",
    )(*shared, doc, stats)
    back2 = lax.ppermute(d2, "x", [(i + 2, i) for i in range(X - 2)])
    back1 = lax.ppermute(d1, "x", [(i + 1, i) for i in range(X - 1)])
    backx = lax.ppermute(dx, ("x", "z", "c"), [(b, a) for a, b in lone])
    dq_mine, dq_other = call(
        pool_kernel,
        (jax.ShapeDtypeStruct((OWN * HD, ROWS), F32), jax.ShapeDtypeStruct((OWN * HD, ROWS), BF16)),
        [],
        name="query_pool",
        nbytes=1,
    )(dq_keep, lax.ppermute(dq_send, "c", [(0, 1), (1, 0)]))
    back1, dq_other = lax.optimization_barrier((back1, dq_other))
    dq_other = lax.ppermute(dq_other, "yl", [(0, 1), (1, 0)])
    plane_sums = call(plane_kernel, jax.ShapeDtypeStruct((2 * Z, KB, HD), BF16), [], name="plane_sum")(
        d0, back1, back2, backx
    )
    parts = lax.all_to_all(plane_sums, ("z", "yl"), split_axis=0, concat_axis=0, tiled=True)

    query_grad = call(query_kernel, jax.ShapeDtypeStruct((ROWS, OWN * HD), BF16), [], name="query_sum")(
        dq_mine, dq_other
    )
    parts, query_grad = lax.optimization_barrier((parts, query_grad))
    key_grad, value_grad = call(
        block_kernel,
        (jax.ShapeDtypeStruct((HD // 2, ROWS), BF16), jax.ShapeDtypeStruct((HD // 2, ROWS), BF16)),
        [],
        name="block_sum",
    )(parts)
    return (query_grad, key_grad.T, value_grad.T, gate_grad, expert_grad[None])


def solution(mesh):
    devices = mesh.devices.reshape(X, Z, 2, 2, 4, 2)
    split = Mesh(devices, ("x", "z", "c", "zh", "yh", "yl"))
    ctx, tp = ("x", "z", "c"), ("zh", "yh", "yl")
    in_specs = (
        P(ctx, tp),
        P(ctx, None),
        P(ctx, None),
        P(ctx, tp),
        P(ctx, tp),
        P(),
        P(ctx, tp),
        P(ctx, None),
        P(ctx, None),
        P(ctx, tp, None),
    )
    out_specs = (P(ctx, tp), P(ctx, tp), P(ctx, tp), P(ctx, tp), P(ctx, tp, None))
    return jax.shard_map(local, mesh=split, in_specs=in_specs, out_specs=out_specs, check_vma=False)
```

```python
import functools
import math

import jax
import jax.numpy as jnp
from jax import lax
from jax.experimental import pallas as pl
from jax.experimental.pallas import tpu as pltpu
from jax.sharding import Mesh
from jax.sharding import PartitionSpec as P

HD = 128
X, Z = 4, 6
ROWS = 128
KB = 64
PLANE = Z * KB
HEADS = 6
OWN = 3
WINDOW = 14
SPAN = WINDOW * KB
PLACES = KB + 3 * PLANE
SCALE = 1.0 / math.sqrt(HD)
LOG2E = 1.4426950408889634
NEG = -1e30
SLOTS = 32

F32 = jnp.float32
BF16 = jnp.bfloat16
VMEM_LIMIT = 48 * 1024 * 1024


def dot_nt(a, b):
    return lax.dot_general(a, b, (((1,), (1,)), ((), ())), preferred_element_type=F32)


def dot_nn(a, b):
    return lax.dot_general(a, b, (((1,), (0,)), ((), ())), preferred_element_type=F32)


def call(kernel, out_shape, scratch_shapes, flops=0, nbytes=1 << 20, name=None, vmem=VMEM_LIMIT, **specs):
    return pl.pallas_call(
        kernel,
        out_shape=out_shape,
        scratch_shapes=scratch_shapes,
        compiler_params=pltpu.CompilerParams(vmem_limit_bytes=vmem),
        cost_estimate=pl.CostEstimate(flops=flops, bytes_accessed=nbytes, transcendentals=0),
        name=name,
        **specs,
    )


def place(z, c, p, parts, q_s, do_s, kv_s):
    qd, qd_c, qd_y, kvx, kv2, kv1, kv0 = parts
    for owner, core, ref, base in (
        (p, c, qd, 0),
        (p, 1 - c, qd_c, 0),
        (1 - p, c, qd_y, 0),
        (1 - p, 1 - c, qd_y, ROWS),
    ):
        for h in range(OWN):
            q_s[owner * OWN + h, pl.ds(core * ROWS, ROWS), :] = ref[base : base + ROWS, h * HD : (h + 1) * HD]
            do_s[owner * OWN + h, pl.ds(core * ROWS, ROWS), :] = ref[
                base : base + ROWS, (OWN + h) * HD : (OWN + h + 1) * HD
            ]
    kv_s[0:KB, :] = kvx[...]
    kv_s[KB : KB + PLANE, :] = kv2[...]
    kv_s[KB + PLANE : KB + 2 * PLANE, :] = kv1[...]
    kv_s[KB + 2 * PLANE : KB + 3 * PLANE, :] = kv0[...]


def query_spans(doc, chip):
    docs = doc[...]
    mine = jnp.concatenate([doc[pl.ds(2 * chip, 1), :], doc[pl.ds(2 * chip + 1, 1), :]], axis=1)
    first = jnp.zeros((1, 2 * ROWS), jnp.int32)
    for d in range(1, 8):
        before = jnp.sum((docs < d).astype(F32)).astype(jnp.int32)
        first = jnp.where(mine == d, before, first)
    last = chip * 2 * ROWS + lax.broadcasted_iota(jnp.int32, (1, 2 * ROWS), 1)
    return first, last


def bias_of(chip, c, p, first, last):
    i = lax.broadcasted_iota(jnp.int32, (SPAN, 2 * ROWS), 0)
    base = (2 * (chip - (WINDOW - 1)) + c) * ROWS + p * KB
    pos = base + (i // KB) * (2 * ROWS) + i % KB
    return jnp.where((pos >= first) & (pos <= last), 0.0, NEG)


def prep_kernel(queries, out_grad, key_rows, value_rows, pool, spread, own, sems):
    group = lax.axis_index("zh") * 4 + lax.axis_index("yh")
    rows = pl.ds(pl.multiple_of(lax.axis_index("yl") * KB, KB), KB)
    cols = pl.ds(pl.multiple_of(group * HD, HD), HD)
    copies = [
        pltpu.make_async_copy(key_rows.at[rows, cols], spread.at[0, :, 0:HD], sems.at[0]),
        pltpu.make_async_copy(value_rows.at[rows, cols], spread.at[0, :, HD : 2 * HD], sems.at[1]),
        pltpu.make_async_copy(queries, pool.at[:, 0 : OWN * HD], sems.at[2]),
        pltpu.make_async_copy(out_grad, pool.at[:, OWN * HD : 2 * OWN * HD], sems.at[3]),
    ]
    for copy in copies:
        copy.start()
    copies[0].wait()
    copies[1].wait()
    for block in range(1, Z):
        spread[block] = spread[0]
    own[...] = spread[0]
    copies[2].wait()
    copies[3].wait()


def stats_kernel(qd, qd_c, qd_y, kvx, kv2, kv1, kv0, o_own, doc, stats, q_s, do_s, kv_s):
    x, z, c, p = (lax.axis_index(a) for a in ("x", "z", "c", "yl"))
    chip = x * Z + z
    place(z, c, p, (qd, qd_c, qd_y, kvx, kv2, kv1, kv0), q_s, do_s, kv_s)
    first, last = query_spans(doc, chip)
    keys = kv_s[pl.ds(pl.multiple_of(z * KB, KB), SPAN), 0:HD]
    bias = bias_of(chip, c, p, first, last)
    rows = []
    for h in range(HEADS):
        s = dot_nt(keys, q_s[h]) * (SCALE * LOG2E) + bias
        s = s.reshape(SPAN // 8, 8, 2 * ROWS)
        fold = jnp.max(s, axis=0)
        sums = jnp.sum(jnp.exp2(s - fold[None]), axis=0)
        top = jnp.max(fold, axis=0, keepdims=True)
        total = jnp.sum(sums * jnp.exp2(fold - top), axis=0, keepdims=True)
        for r in range(2):
            rows.append((2 * h + r, top[:, r * ROWS : (r + 1) * ROWS]))
            rows.append((12 + 2 * h + r, total[:, r * ROWS : (r + 1) * ROWS]))
    for h in range(OWN):
        prod = qd[:, (OWN + h) * HD : (OWN + h + 1) * HD].astype(F32) * o_own[:, h * HD : (h + 1) * HD].astype(F32)
        rows.append((24 + h, jnp.sum(prod.T, axis=0, keepdims=True)))
    for peer in range(4):
        for at, row in rows:
            stats[peer, at : at + 1, :] = row
        stats[peer, 27:32, :] = jnp.zeros((5, ROWS), F32)


def grads_kernel(
    qd, qd_c, qd_y, kvx, kv2, kv1, kv0, doc, stats, d2, d1, d0, dx, dq_keep, dq_send, q_s, do_s, kv_s, acc_s
):
    x, z, c, p = (lax.axis_index(a) for a in ("x", "z", "c", "yl"))
    chip = x * Z + z
    place(z, c, p, (qd, qd_c, qd_y, kvx, kv2, kv1, kv0), q_s, do_s, kv_s)
    first, last = query_spans(doc, chip)
    acc_s[...] = jnp.zeros(acc_s.shape, F32)
    tops = [stats[i, 0:12, :] for i in range(4)]
    top = jnp.maximum(jnp.maximum(tops[0], tops[1]), jnp.maximum(tops[2], tops[3]))
    total = sum(stats[i, 12:24, :] * jnp.exp2(tops[i] - top) for i in range(4))
    lse = top + jnp.log(total) * LOG2E

    at = pl.multiple_of(z * KB, KB)
    keys = kv_s[pl.ds(at, SPAN), 0:HD]
    values = kv_s[pl.ds(at, SPAN), HD : 2 * HD]
    keys_t = keys.astype(F32).T.astype(BF16)
    bias = bias_of(chip, c, p, first, last)
    dk = jnp.zeros((SPAN, HD), F32)
    dv = jnp.zeros((SPAN, HD), F32)
    for h in range(HEADS):
        owner, k = h // OWN, 24 + h % OWN
        row_lse = jnp.concatenate([lse[2 * h : 2 * h + 1, :], lse[2 * h + 1 : 2 * h + 2, :]], axis=1)
        delta = jnp.concatenate([stats[owner, k : k + 1, :], stats[2 + owner, k : k + 1, :]], axis=1)
        q, do = q_s[h], do_s[h]
        probs = jnp.exp2(dot_nt(keys, q) * (SCALE * LOG2E) + bias - row_lse)
        score = (probs * (dot_nt(values, do) - delta)).astype(BF16)
        dv = dv + dot_nn(probs.astype(BF16), do)
        dk = dk + dot_nn(score, q)
        part = dot_nn(keys_t, score) * SCALE
        lower, upper = part[:, 0:ROWS], part[:, ROWS : 2 * ROWS]
        rows = slice((h % OWN) * HD, (h % OWN + 1) * HD)
        dq_keep[owner, rows, :] = jnp.where(c == 0, lower, upper)
        dq_send[owner, rows, :] = jnp.where(c == 0, upper, lower).astype(BF16)
    acc_s[pl.ds(at, SPAN), 0:HD] = dk * SCALE
    acc_s[pl.ds(at, SPAN), HD : 2 * HD] = dv
    for ref, start, size in (
        (dx, 0, KB),
        (d2, KB, PLANE),
        (d1, KB + PLANE, PLANE),
        (d0, KB + 2 * PLANE, PLANE),
    ):
        dk, dv = acc_s[start : start + size, 0:HD], acc_s[start : start + size, HD : 2 * HD]
        low = lax.broadcasted_iota(jnp.int32, (size, HD), 1) < HD // 2
        ref[:, 0:HD] = jnp.where(low, dk, pltpu.roll(dv, HD // 2, 1)).astype(ref.dtype)
        ref[:, HD : 2 * HD] = jnp.where(low, pltpu.roll(dk, HD // 2, 1), dv).astype(ref.dtype)


def plane_kernel(d0, r1, r2, rx, out):
    for block in range(Z):
        rows = slice(block * KB, (block + 1) * KB)
        total = d0[rows, :] + r1[rows, :].astype(F32) + r2[rows, :].astype(F32)
        if block == Z - 1:
            total = total + rx[...].astype(F32)
        for half in range(2):
            out[2 * block + half] = total[:, half * HD : (half + 1) * HD].astype(BF16)


def block_kernel(parts, key_grad, value_grad):
    halves = []
    for half in range(2):
        total = parts[half].astype(F32)
        for block in range(1, Z):
            total = total + parts[2 * block + half].astype(F32)
        halves.append(total)
    total = jnp.concatenate(halves, axis=0).T
    key_grad[...] = total[0 : HD // 2, :].astype(BF16)
    value_grad[...] = total[HD // 2 :, :].astype(BF16)


def pool_kernel(keep, arrived, mine, other):
    p = lax.axis_index("yl")
    mine[...] = keep[p] + arrived[p].astype(F32)
    other[...] = (keep[1 - p] + arrived[1 - p].astype(F32)).astype(BF16)


def query_kernel(mine, arrived, query_grad):
    for h in range(OWN):
        rows = slice(h * HD, (h + 1) * HD)
        query_grad[:, rows] = (mine[rows, :] + arrived[rows, :].astype(F32)).T.astype(BF16)


def choice(ids, expert, second):
    first_hit, other_hit = ids[0:1, :] == expert, ids[1:2, :] == expert
    hit = jnp.where(first_hit | other_hit, 1.0, 0.0)
    earlier = lax.broadcasted_iota(jnp.int32, (ROWS, ROWS), 0) < lax.broadcasted_iota(jnp.int32, (ROWS, ROWS), 1)
    rank = dot_nn(
        jnp.broadcast_to(hit, (16, ROWS)).astype(BF16), jnp.where(earlier, 1.0, 0.0).astype(BF16)
    )[0:1, :].astype(jnp.int32)
    slot = second * SLOTS + lax.broadcasted_iota(jnp.int32, (SLOTS, ROWS), 0)
    return (slot == rank) & (hit > 0.0), first_hit, other_hit


def select_kernel(mine, ids, out):
    for high in range(2):
        for pair in range(4):
            for second in range(2):
                chosen, _, _ = choice(ids, high * 4 + pair, second)
                chosen = jnp.where(chosen, 1.0, 0.0).astype(BF16)
                out[2 * pair + second, high] = dot_nn(chosen, mine[...]).astype(BF16)


def combine_kernel(rows, rows_other, ids, gates, stored, gate_grad, expert_grad):
    here = lax.axis_index("zh")
    place_in_tp = here * 8 + lax.axis_index("yh") * 2 + lax.axis_index("yl")
    chosen, first_hit, other_hit = choice(ids, place_in_tp // 2, place_in_tp % 2)
    gate = jnp.where(first_hit, gates[0:1, :], 0.0) + jnp.where(other_hit, gates[1:2, :], 0.0)
    slot_gate = jnp.sum(jnp.where(chosen, gate, 0.0), axis=1, keepdims=True)
    total = jnp.zeros((SLOTS, OWN * HD), F32)
    for other in range(2):
        high = here if other == 0 else 1 - here
        for y in range(8):
            routed = (rows[y, here] if other == 0 else rows_other[y]).astype(F32)
            cols = pl.ds(pl.multiple_of((high * 8 + y) * OWN * HD, HD), OWN * HD)
            total = total + routed * stored[:, cols].astype(F32)
            expert_grad[:, cols] = (slot_gate * routed).astype(BF16)
    gate_grad[...] = jnp.sum(total.T, axis=0, keepdims=True)


def local(
    queries,
    key_rows,
    value_rows,
    out_grad,
    attn_out,
    doc_ids,
    row_grad,
    gate_weights,
    expert_ids,
    expert_out,
):
    pool, spread, own = call(
        prep_kernel,
        (
            jax.ShapeDtypeStruct((ROWS, 2 * OWN * HD), BF16),
            jax.ShapeDtypeStruct((Z, KB, 2 * HD), BF16),
            jax.ShapeDtypeStruct((KB, 2 * HD), BF16),
        ),
        [pltpu.SemaphoreType.DMA((4,))],
        name="prep",
        vmem=None,
        in_specs=[pl.BlockSpec(memory_space=pltpu.HBM)] * 4,
    )(queries, out_grad, key_rows, value_rows)
    plane = lax.all_to_all(spread, "z", split_axis=0, concat_axis=0, tiled=True).reshape(PLANE, 2 * HD)
    pool_c = lax.ppermute(pool, "c", [(0, 1), (1, 0)])
    pool_y = lax.ppermute(jnp.concatenate([pool, pool_c], axis=0), "yl", [(0, 1), (1, 0)])
    ids = expert_ids.T
    chosen_rows = call(
        select_kernel,
        jax.ShapeDtypeStruct((8, 2, SLOTS, OWN * HD), BF16),
        [],
        flops=100 * 256 * ROWS * 2 * OWN * HD,
        name="select_rows",
    )(row_grad, ids)
    rows = lax.all_to_all(chosen_rows, ("yh", "yl"), split_axis=0, concat_axis=0, tiled=True)
    away = lax.dynamic_index_in_dim(rows, 1 - lax.axis_index("zh"), 1, keepdims=False)
    rows_other = lax.ppermute(away, "zh", [(0, 1), (1, 0)])

    lone = [((0 * Z + 5) * 2 + 1, (3 * Z + 0) * 2 + 1)]
    ahead2 = lax.ppermute(plane, "x", [(i, i + 2) for i in range(X - 2)])
    ahead1 = lax.ppermute(plane, "x", [(i, i + 1) for i in range(X - 1)])
    aheadx = lax.ppermute(own, ("x", "z", "c"), lone)

    doc = doc_ids.reshape(-1, ROWS)
    shared = (pool, pool_c, pool_y, aheadx, ahead2, ahead1, plane)
    pool_scratch = [
        pltpu.VMEM((HEADS, 2 * ROWS, HD), BF16),
        pltpu.VMEM((HEADS, 2 * ROWS, HD), BF16),
        pltpu.VMEM((PLACES, 2 * HD), BF16),
    ]
    pairs = SPAN * HEADS * 2 * ROWS
    stats = call(
        stats_kernel,
        jax.ShapeDtypeStruct((4, 32, ROWS), F32),
        pool_scratch,
        flops=30 * 2 * HD * pairs,
        name="softmax_stats",
    )(*shared, attn_out, doc)
    stats, _ = lax.optimization_barrier((stats, rows))
    stats = lax.all_to_all(stats, ("c", "yl"), split_axis=0, concat_axis=0, tiled=True)
    stats, _ = lax.optimization_barrier((stats, away))
    d2, d1, d0, dx, dq_keep, dq_send = call(
        grads_kernel,
        (
            jax.ShapeDtypeStruct((PLANE, 2 * HD), BF16),
            jax.ShapeDtypeStruct((PLANE, 2 * HD), BF16),
            jax.ShapeDtypeStruct((PLANE, 2 * HD), F32),
            jax.ShapeDtypeStruct((KB, 2 * HD), BF16),
            jax.ShapeDtypeStruct((2, OWN * HD, ROWS), F32),
            jax.ShapeDtypeStruct((2, OWN * HD, ROWS), BF16),
        ),
        pool_scratch + [pltpu.VMEM((PLACES, 2 * HD), F32)],
        flops=10 * HD * pairs,
        name="score_grads",
    )(*shared, doc, stats)
    back2 = lax.ppermute(d2, "x", [(i + 2, i) for i in range(X - 2)])
    back1 = lax.ppermute(d1, "x", [(i + 1, i) for i in range(X - 1)])
    backx = lax.ppermute(dx, ("x", "z", "c"), [(b, a) for a, b in lone])
    dq_mine, dq_other = call(
        pool_kernel,
        (jax.ShapeDtypeStruct((OWN * HD, ROWS), F32), jax.ShapeDtypeStruct((OWN * HD, ROWS), BF16)),
        [],
        name="query_pool",
        nbytes=1,
    )(dq_keep, lax.ppermute(dq_send, "c", [(0, 1), (1, 0)]))
    back1, dq_other = lax.optimization_barrier((back1, dq_other))
    dq_other = lax.ppermute(dq_other, "yl", [(0, 1), (1, 0)])
    gate_grad, expert_grad = call(
        combine_kernel,
        (
            jax.ShapeDtypeStruct((1, SLOTS), F32),
            jax.ShapeDtypeStruct((SLOTS, expert_out.shape[2]), BF16),
        ),
        [],
        name="combine_grads",
    )(rows, rows_other, ids, gate_weights.T, expert_out[0])
    back1, _ = lax.optimization_barrier((back1, expert_grad))
    plane_sums = call(plane_kernel, jax.ShapeDtypeStruct((2 * Z, KB, HD), BF16), [], name="plane_sum")(
        d0, back1, back2, backx
    )
    parts = lax.all_to_all(plane_sums, ("z", "yl"), split_axis=0, concat_axis=0, tiled=True)

    query_grad = call(query_kernel, jax.ShapeDtypeStruct((ROWS, OWN * HD), BF16), [], name="query_sum")(
        dq_mine, dq_other
    )
    parts, query_grad = lax.optimization_barrier((parts, query_grad))
    key_grad, value_grad = call(
        block_kernel,
        (jax.ShapeDtypeStruct((HD // 2, ROWS), BF16), jax.ShapeDtypeStruct((HD // 2, ROWS), BF16)),
        [],
        name="block_sum",
    )(parts)
    return (query_grad, key_grad.T, value_grad.T, gate_grad, expert_grad[None])


def solution(mesh):
    devices = mesh.devices.reshape(X, Z, 2, 2, 4, 2)
    split = Mesh(devices, ("x", "z", "c", "zh", "yh", "yl"))
    ctx, tp = ("x", "z", "c"), ("zh", "yh", "yl")
    in_specs = (
        P(ctx, tp),
        P(ctx, None),
        P(ctx, None),
        P(ctx, tp),
        P(ctx, tp),
        P(),
        P(ctx, tp),
        P(ctx, None),
        P(ctx, None),
        P(ctx, tp, None),
    )
    out_specs = (P(ctx, tp), P(ctx, tp), P(ctx, tp), P(ctx, tp), P(ctx, tp, None))
    return jax.shard_map(local, mesh=split, in_specs=in_specs, out_specs=out_specs, check_vma=False)
```

```python
import functools
import math

import jax
import jax.numpy as jnp
from jax import lax
from jax.experimental import pallas as pl
from jax.experimental.pallas import tpu as pltpu
from jax.sharding import Mesh
from jax.sharding import PartitionSpec as P

HD = 128
X, Z = 4, 6
ROWS = 128
KB = 64
PLANE = Z * KB
HEADS = 6
OWN = 3
WINDOW = 14
SPAN = WINDOW * KB
PLACES = KB + 3 * PLANE
SCALE = 1.0 / math.sqrt(HD)
LOG2E = 1.4426950408889634
NEG = -1e30
SLOTS = 32

F32 = jnp.float32
BF16 = jnp.bfloat16
VMEM_LIMIT = 48 * 1024 * 1024


def dot_nt(a, b):
    return lax.dot_general(a, b, (((1,), (1,)), ((), ())), preferred_element_type=F32)


def dot_nn(a, b):
    return lax.dot_general(a, b, (((1,), (0,)), ((), ())), preferred_element_type=F32)


def call(kernel, out_shape, scratch_shapes, flops=0, nbytes=1 << 20, name=None, vmem=VMEM_LIMIT, **specs):
    return pl.pallas_call(
        kernel,
        out_shape=out_shape,
        scratch_shapes=scratch_shapes,
        compiler_params=pltpu.CompilerParams(vmem_limit_bytes=vmem),
        cost_estimate=pl.CostEstimate(flops=flops, bytes_accessed=nbytes, transcendentals=0),
        name=name,
        **specs,
    )


def place(z, c, p, parts, q_s, do_s, kv_s):
    qd, qd_c, qd_y, kvx, kv2, kv1, kv0 = parts
    for owner, core, ref, base in (
        (p, c, qd, 0),
        (p, 1 - c, qd_c, 0),
        (1 - p, c, qd_y, 0),
        (1 - p, 1 - c, qd_y, ROWS),
    ):
        for h in range(OWN):
            q_s[owner * OWN + h, pl.ds(core * ROWS, ROWS), :] = ref[base : base + ROWS, h * HD : (h + 1) * HD]
            do_s[owner * OWN + h, pl.ds(core * ROWS, ROWS), :] = ref[
                base : base + ROWS, (OWN + h) * HD : (OWN + h + 1) * HD
            ]
    kv_s[0:KB, :] = kvx[...]
    kv_s[KB : KB + PLANE, :] = kv2[...]
    kv_s[KB + PLANE : KB + 2 * PLANE, :] = kv1[...]
    kv_s[KB + 2 * PLANE : KB + 3 * PLANE, :] = kv0[...]


def query_spans(doc, chip):
    docs = doc[...]
    mine = jnp.concatenate([doc[pl.ds(2 * chip, 1), :], doc[pl.ds(2 * chip + 1, 1), :]], axis=1)
    first = jnp.zeros((1, 2 * ROWS), jnp.int32)
    for d in range(1, 8):
        before = jnp.sum((docs < d).astype(F32)).astype(jnp.int32)
        first = jnp.where(mine == d, before, first)
    last = chip * 2 * ROWS + lax.broadcasted_iota(jnp.int32, (1, 2 * ROWS), 1)
    return first, last


def bias_of(chip, c, p, first, last):
    i = lax.broadcasted_iota(jnp.int32, (SPAN, 2 * ROWS), 0)
    base = (2 * (chip - (WINDOW - 1)) + c) * ROWS + p * KB
    pos = base + (i // KB) * (2 * ROWS) + i % KB
    return jnp.where((pos >= first) & (pos <= last), 0.0, NEG)


def prep_kernel(queries, out_grad, key_rows, value_rows, pool, spread, own, sems):
    group = lax.axis_index("zh") * 4 + lax.axis_index("yh")
    rows = pl.ds(pl.multiple_of(lax.axis_index("yl") * KB, KB), KB)
    cols = pl.ds(pl.multiple_of(group * HD, HD), HD)
    copies = [
        pltpu.make_async_copy(key_rows.at[rows, cols], spread.at[0, :, 0:HD], sems.at[0]),
        pltpu.make_async_copy(value_rows.at[rows, cols], spread.at[0, :, HD : 2 * HD], sems.at[1]),
        pltpu.make_async_copy(queries, pool.at[:, 0 : OWN * HD], sems.at[2]),
        pltpu.make_async_copy(out_grad, pool.at[:, OWN * HD : 2 * OWN * HD], sems.at[3]),
    ]
    for copy in copies:
        copy.start()
    copies[0].wait()
    copies[1].wait()
    for block in range(1, Z):
        spread[block] = spread[0]
    own[...] = spread[0]
    copies[2].wait()
    copies[3].wait()


def stats_kernel(qd, qd_c, qd_y, kvx, kv2, kv1, kv0, o_own, doc, stats, q_s, do_s, kv_s):
    x, z, c, p = (lax.axis_index(a) for a in ("x", "z", "c", "yl"))
    chip = x * Z + z
    place(z, c, p, (qd, qd_c, qd_y, kvx, kv2, kv1, kv0), q_s, do_s, kv_s)
    first, last = query_spans(doc, chip)
    keys = kv_s[pl.ds(pl.multiple_of(z * KB, KB), SPAN), 0:HD]
    bias = bias_of(chip, c, p, first, last)
    rows = []
    for h in range(HEADS):
        s = dot_nt(keys, q_s[h]) * (SCALE * LOG2E) + bias
        s = s.reshape(SPAN // 8, 8, 2 * ROWS)
        fold = jnp.max(s, axis=0)
        sums = jnp.sum(jnp.exp2(s - fold[None]), axis=0)
        top = jnp.max(fold, axis=0, keepdims=True)
        total = jnp.sum(sums * jnp.exp2(fold - top), axis=0, keepdims=True)
        for r in range(2):
            rows.append((2 * h + r, top[:, r * ROWS : (r + 1) * ROWS]))
            rows.append((12 + 2 * h + r, total[:, r * ROWS : (r + 1) * ROWS]))
    for h in range(OWN):
        prod = qd[:, (OWN + h) * HD : (OWN + h + 1) * HD].astype(F32) * o_own[:, h * HD : (h + 1) * HD].astype(F32)
        rows.append((24 + h, jnp.sum(prod.T, axis=0, keepdims=True)))
    for at, row in rows:
        stats[at : at + 1, :] = row
    stats[27:32, :] = jnp.zeros((5, ROWS), F32)


def merge_kernel(mine, arrived, out):
    c = lax.axis_index("c")
    top = jnp.maximum(mine[0:12, :], arrived[0:12, :])
    out[0:12, :] = top
    out[12:24, :] = mine[12:24, :] * jnp.exp2(mine[0:12, :] - top) + arrived[12:24, :] * jnp.exp2(
        arrived[0:12, :] - top
    )
    for h in range(OWN):
        a, b = mine[24 + h : 25 + h, :], arrived[24 + h : 25 + h, :]
        out[24 + h : 25 + h, :] = jnp.where(c == 0, a, b)
        out[27 + h : 28 + h, :] = jnp.where(c == 0, b, a)
    out[30:32, :] = jnp.zeros((2, ROWS), F32)


def grads_kernel(
    qd, qd_c, qd_y, kvx, kv2, kv1, kv0, doc, stats, stats_y, d2, d1, d0, dx, dq_keep, dq_send, q_s, do_s, kv_s, acc_s
):
    x, z, c, p = (lax.axis_index(a) for a in ("x", "z", "c", "yl"))
    chip = x * Z + z
    place(z, c, p, (qd, qd_c, qd_y, kvx, kv2, kv1, kv0), q_s, do_s, kv_s)
    first, last = query_spans(doc, chip)
    acc_s[...] = jnp.zeros(acc_s.shape, F32)
    top = jnp.maximum(stats[0:12, :], stats_y[0:12, :])
    total = stats[12:24, :] * jnp.exp2(stats[0:12, :] - top) + stats_y[12:24, :] * jnp.exp2(stats_y[0:12, :] - top)
    lse = top + jnp.log(total) * LOG2E

    at = pl.multiple_of(z * KB, KB)
    keys = kv_s[pl.ds(at, SPAN), 0:HD]
    values = kv_s[pl.ds(at, SPAN), HD : 2 * HD]
    keys_t = keys.astype(F32).T.astype(BF16)
    bias = bias_of(chip, c, p, first, last)
    dk = jnp.zeros((SPAN, HD), F32)
    dv = jnp.zeros((SPAN, HD), F32)
    for h in range(HEADS):
        owner, k = h // OWN, 24 + h % OWN
        row_lse = jnp.concatenate([lse[2 * h : 2 * h + 1, :], lse[2 * h + 1 : 2 * h + 2, :]], axis=1)
        deltas = [jnp.where(p == owner, stats[i : i + 1, :], stats_y[i : i + 1, :]) for i in (k, k + OWN)]
        delta = jnp.concatenate(deltas, axis=1)
        q, do = q_s[h], do_s[h]
        probs = jnp.exp2(dot_nt(keys, q) * (SCALE * LOG2E) + bias - row_lse)
        score = (probs * (dot_nt(values, do) - delta)).astype(BF16)
        dv = dv + dot_nn(probs.astype(BF16), do)
        dk = dk + dot_nn(score, q)
        part = dot_nn(keys_t, score) * SCALE
        lower, upper = part[:, 0:ROWS], part[:, ROWS : 2 * ROWS]
        rows = slice((h % OWN) * HD, (h % OWN + 1) * HD)
        dq_keep[owner, rows, :] = jnp.where(c == 0, lower, upper)
        dq_send[owner, rows, :] = jnp.where(c == 0, upper, lower).astype(BF16)
    acc_s[pl.ds(at, SPAN), 0:HD] = dk * SCALE
    acc_s[pl.ds(at, SPAN), HD : 2 * HD] = dv
    for ref, start, size in (
        (dx, 0, KB),
        (d2, KB, PLANE),
        (d1, KB + PLANE, PLANE),
        (d0, KB + 2 * PLANE, PLANE),
    ):
        dk, dv = acc_s[start : start + size, 0:HD], acc_s[start : start + size, HD : 2 * HD]
        low = lax.broadcasted_iota(jnp.int32, (size, HD), 1) < HD // 2
        ref[:, 0:HD] = jnp.where(low, dk, pltpu.roll(dv, HD // 2, 1)).astype(ref.dtype)
        ref[:, HD : 2 * HD] = jnp.where(low, pltpu.roll(dk, HD // 2, 1), dv).astype(ref.dtype)


def plane_kernel(d0, r1, r2, rx, out):
    for block in range(Z):
        rows = slice(block * KB, (block + 1) * KB)
        total = d0[rows, :] + r1[rows, :].astype(F32) + r2[rows, :].astype(F32)
        if block == Z - 1:
            total = total + rx[...].astype(F32)
        for half in range(2):
            out[2 * block + half] = total[:, half * HD : (half + 1) * HD].astype(BF16)


def block_kernel(parts, key_grad, value_grad):
    halves = []
    for half in range(2):
        total = parts[half].astype(F32)
        for block in range(1, Z):
            total = total + parts[2 * block + half].astype(F32)
        halves.append(total)
    total = jnp.concatenate(halves, axis=0).T
    key_grad[...] = total[0 : HD // 2, :].astype(BF16)
    value_grad[...] = total[HD // 2 :, :].astype(BF16)


def pool_kernel(keep, arrived, mine, other):
    p = lax.axis_index("yl")
    mine[...] = keep[p] + arrived[p].astype(F32)
    other[...] = (keep[1 - p] + arrived[1 - p].astype(F32)).astype(BF16)


def query_kernel(mine, arrived, query_grad):
    for h in range(OWN):
        rows = slice(h * HD, (h + 1) * HD)
        query_grad[:, rows] = (mine[rows, :] + arrived[rows, :].astype(F32)).T.astype(BF16)


def choice(ids, expert, second):
    first_hit, other_hit = ids[0:1, :] == expert, ids[1:2, :] == expert
    hit = jnp.where(first_hit | other_hit, 1.0, 0.0)
    earlier = lax.broadcasted_iota(jnp.int32, (ROWS, ROWS), 0) < lax.broadcasted_iota(jnp.int32, (ROWS, ROWS), 1)
    rank = dot_nn(
        jnp.broadcast_to(hit, (16, ROWS)).astype(BF16), jnp.where(earlier, 1.0, 0.0).astype(BF16)
    )[0:1, :].astype(jnp.int32)
    slot = second * SLOTS + lax.broadcasted_iota(jnp.int32, (SLOTS, ROWS), 0)
    return (slot == rank) & (hit > 0.0), first_hit, other_hit


def select_kernel(mine, ids, out):
    for high in range(2):
        for pair in range(4):
            for second in range(2):
                chosen, _, _ = choice(ids, high * 4 + pair, second)
                chosen = jnp.where(chosen, 1.0, 0.0).astype(BF16)
                out[2 * pair + second, high] = dot_nn(chosen, mine[...]).astype(BF16)


def combine_kernel(rows, rows_other, ids, gates, stored, gate_grad, expert_grad):
    here = lax.axis_index("zh")
    place_in_tp = here * 8 + lax.axis_index("yh") * 2 + lax.axis_index("yl")
    chosen, first_hit, other_hit = choice(ids, place_in_tp // 2, place_in_tp % 2)
    gate = jnp.where(first_hit, gates[0:1, :], 0.0) + jnp.where(other_hit, gates[1:2, :], 0.0)
    slot_gate = jnp.sum(jnp.where(chosen, gate, 0.0), axis=1, keepdims=True)
    total = jnp.zeros((SLOTS, OWN * HD), F32)
    for other in range(2):
        high = here if other == 0 else 1 - here
        for y in range(8):
            routed = (rows[y, here] if other == 0 else rows_other[y]).astype(F32)
            cols = pl.ds(pl.multiple_of((high * 8 + y) * OWN * HD, HD), OWN * HD)
            total = total + routed * stored[:, cols].astype(F32)
            expert_grad[:, cols] = (slot_gate * routed).astype(BF16)
    gate_grad[...] = jnp.sum(total.T, axis=0, keepdims=True)


def local(
    queries,
    key_rows,
    value_rows,
    out_grad,
    attn_out,
    doc_ids,
    row_grad,
    gate_weights,
    expert_ids,
    expert_out,
):
    pool, spread, own = call(
        prep_kernel,
        (
            jax.ShapeDtypeStruct((ROWS, 2 * OWN * HD), BF16),
            jax.ShapeDtypeStruct((Z, KB, 2 * HD), BF16),
            jax.ShapeDtypeStruct((KB, 2 * HD), BF16),
        ),
        [pltpu.SemaphoreType.DMA((4,))],
        name="prep",
        vmem=None,
        in_specs=[pl.BlockSpec(memory_space=pltpu.HBM)] * 4,
    )(queries, out_grad, key_rows, value_rows)
    plane = lax.all_to_all(spread, "z", split_axis=0, concat_axis=0, tiled=True).reshape(PLANE, 2 * HD)
    pool_c = lax.ppermute(pool, "c", [(0, 1), (1, 0)])
    pool_y = lax.ppermute(jnp.concatenate([pool, pool_c], axis=0), "yl", [(0, 1), (1, 0)])
    ids = expert_ids.T
    chosen_rows = call(
        select_kernel,
        jax.ShapeDtypeStruct((8, 2, SLOTS, OWN * HD), BF16),
        [],
        flops=100 * 256 * ROWS * 2 * OWN * HD,
        name="select_rows",
    )(row_grad, ids)
    rows = lax.all_to_all(chosen_rows, ("yh", "yl"), split_axis=0, concat_axis=0, tiled=True)
    away = lax.dynamic_index_in_dim(rows, 1 - lax.axis_index("zh"), 1, keepdims=False)
    rows_other = lax.ppermute(away, "zh", [(0, 1), (1, 0)])

    lone = [((0 * Z + 5) * 2 + 1, (3 * Z + 0) * 2 + 1)]
    ahead2 = lax.ppermute(plane, "x", [(i, i + 2) for i in range(X - 2)])
    ahead1 = lax.ppermute(plane, "x", [(i, i + 1) for i in range(X - 1)])
    aheadx = lax.ppermute(own, ("x", "z", "c"), lone)

    doc = doc_ids.reshape(-1, ROWS)
    shared = (pool, pool_c, pool_y, aheadx, ahead2, ahead1, plane)
    pool_scratch = [
        pltpu.VMEM((HEADS, 2 * ROWS, HD), BF16),
        pltpu.VMEM((HEADS, 2 * ROWS, HD), BF16),
        pltpu.VMEM((PLACES, 2 * HD), BF16),
    ]
    pairs = SPAN * HEADS * 2 * ROWS
    stats = call(
        stats_kernel,
        jax.ShapeDtypeStruct((32, ROWS), F32),
        pool_scratch,
        flops=30 * 2 * HD * pairs,
        name="softmax_stats",
    )(*shared, attn_out, doc)
    stats = call(merge_kernel, jax.ShapeDtypeStruct((32, ROWS), F32), [], nbytes=1 << 15, name="merge_stats")(
        stats, lax.ppermute(stats, "c", [(0, 1), (1, 0)])
    )
    stats_y = lax.ppermute(stats, "yl", [(0, 1), (1, 0)])
    d2, d1, d0, dx, dq_keep, dq_send = call(
        grads_kernel,
        (
            jax.ShapeDtypeStruct((PLANE, 2 * HD), BF16),
            jax.ShapeDtypeStruct((PLANE, 2 * HD), BF16),
            jax.ShapeDtypeStruct((PLANE, 2 * HD), F32),
            jax.ShapeDtypeStruct((KB, 2 * HD), BF16),
            jax.ShapeDtypeStruct((2, OWN * HD, ROWS), F32),
            jax.ShapeDtypeStruct((2, OWN * HD, ROWS), BF16),
        ),
        pool_scratch + [pltpu.VMEM((PLACES, 2 * HD), F32)],
        flops=10 * HD * pairs,
        name="score_grads",
    )(*shared, doc, stats, stats_y)
    back2 = lax.ppermute(d2, "x", [(i + 2, i) for i in range(X - 2)])
    back1 = lax.ppermute(d1, "x", [(i + 1, i) for i in range(X - 1)])
    backx = lax.ppermute(dx, ("x", "z", "c"), [(b, a) for a, b in lone])
    dq_mine, dq_other = call(
        pool_kernel,
        (jax.ShapeDtypeStruct((OWN * HD, ROWS), F32), jax.ShapeDtypeStruct((OWN * HD, ROWS), BF16)),
        [],
        name="query_pool",
        nbytes=1,
    )(dq_keep, lax.ppermute(dq_send, "c", [(0, 1), (1, 0)]))
    back1, dq_other = lax.optimization_barrier((back1, dq_other))
    dq_other = lax.ppermute(dq_other, "yl", [(0, 1), (1, 0)])
    gate_grad, expert_grad = call(
        combine_kernel,
        (
            jax.ShapeDtypeStruct((1, SLOTS), F32),
            jax.ShapeDtypeStruct((SLOTS, expert_out.shape[2]), BF16),
        ),
        [],
        name="combine_grads",
    )(rows, rows_other, ids, gate_weights.T, expert_out[0])
    back1, _ = lax.optimization_barrier((back1, expert_grad))
    plane_sums = call(plane_kernel, jax.ShapeDtypeStruct((2 * Z, KB, HD), BF16), [], name="plane_sum")(
        d0, back1, back2, backx
    )
    parts = lax.all_to_all(plane_sums, ("z", "yl"), split_axis=0, concat_axis=0, tiled=True)

    query_grad = call(query_kernel, jax.ShapeDtypeStruct((ROWS, OWN * HD), BF16), [], name="query_sum")(
        dq_mine, dq_other
    )
    parts, query_grad = lax.optimization_barrier((parts, query_grad))
    key_grad, value_grad = call(
        block_kernel,
        (jax.ShapeDtypeStruct((HD // 2, ROWS), BF16), jax.ShapeDtypeStruct((HD // 2, ROWS), BF16)),
        [],
        name="block_sum",
    )(parts)
    return (query_grad, key_grad.T, value_grad.T, gate_grad, expert_grad[None])


def solution(mesh):
    devices = mesh.devices.reshape(X, Z, 2, 2, 4, 2)
    split = Mesh(devices, ("x", "z", "c", "zh", "yh", "yl"))
    ctx, tp = ("x", "z", "c"), ("zh", "yh", "yl")
    in_specs = (
        P(ctx, tp),
        P(ctx, None),
        P(ctx, None),
        P(ctx, tp),
        P(ctx, tp),
        P(),
        P(ctx, tp),
        P(ctx, None),
        P(ctx, None),
        P(ctx, tp, None),
    )
    out_specs = (P(ctx, tp), P(ctx, tp), P(ctx, tp), P(ctx, tp), P(ctx, tp, None))
    return jax.shard_map(local, mesh=split, in_specs=in_specs, out_specs=out_specs, check_vma=False)
```

```python
import functools
import math

import jax
import jax.numpy as jnp
from jax import lax
from jax.experimental import pallas as pl
from jax.experimental.pallas import tpu as pltpu
from jax.sharding import Mesh
from jax.sharding import PartitionSpec as P

HD = 128
X, Z = 4, 6
ROWS = 128
KB = 64
PLANE = Z * KB
HEADS = 6
OWN = 3
WINDOW = 14
SPAN = WINDOW * KB
PLACES = KB + 3 * PLANE
SCALE = 1.0 / math.sqrt(HD)
LOG2E = 1.4426950408889634
NEG = -1e30
SLOTS = 32

F32 = jnp.float32
BF16 = jnp.bfloat16
VMEM_LIMIT = 48 * 1024 * 1024


def dot_nt(a, b):
    return lax.dot_general(a, b, (((1,), (1,)), ((), ())), preferred_element_type=F32)


def dot_nn(a, b):
    return lax.dot_general(a, b, (((1,), (0,)), ((), ())), preferred_element_type=F32)


def call(kernel, out_shape, scratch_shapes, flops=0, nbytes=1 << 20, name=None, vmem=VMEM_LIMIT, **specs):
    return pl.pallas_call(
        kernel,
        out_shape=out_shape,
        scratch_shapes=scratch_shapes,
        compiler_params=pltpu.CompilerParams(vmem_limit_bytes=vmem),
        cost_estimate=pl.CostEstimate(flops=flops, bytes_accessed=nbytes, transcendentals=0),
        name=name,
        **specs,
    )


def place(z, c, p, parts, q_s, do_s, kv_s):
    qd, qd_c, qd_y, kvx, kv2, kv1, kv0 = parts
    for owner, core, ref, base in (
        (p, c, qd, 0),
        (p, 1 - c, qd_c, 0),
        (1 - p, c, qd_y, 0),
        (1 - p, 1 - c, qd_y, ROWS),
    ):
        for h in range(OWN):
            q_s[owner * OWN + h, pl.ds(core * ROWS, ROWS), :] = ref[base : base + ROWS, h * HD : (h + 1) * HD]
            do_s[owner * OWN + h, pl.ds(core * ROWS, ROWS), :] = ref[
                base : base + ROWS, (OWN + h) * HD : (OWN + h + 1) * HD
            ]
    kv_s[0:KB, :] = kvx[...]
    kv_s[KB : KB + PLANE, :] = kv2[...]
    kv_s[KB + PLANE : KB + 2 * PLANE, :] = kv1[...]
    kv_s[KB + 2 * PLANE : KB + 3 * PLANE, :] = kv0[...]


def query_spans(doc, chip):
    docs = doc[...]
    mine = jnp.concatenate([doc[pl.ds(2 * chip, 1), :], doc[pl.ds(2 * chip + 1, 1), :]], axis=1)
    first = jnp.zeros((1, 2 * ROWS), jnp.int32)
    for d in range(1, 8):
        before = jnp.sum((docs < d).astype(F32)).astype(jnp.int32)
        first = jnp.where(mine == d, before, first)
    last = chip * 2 * ROWS + lax.broadcasted_iota(jnp.int32, (1, 2 * ROWS), 1)
    return first, last


def bias_of(chip, c, p, first, last):
    i = lax.broadcasted_iota(jnp.int32, (SPAN, 2 * ROWS), 0)
    base = (2 * (chip - (WINDOW - 1)) + c) * ROWS + p * KB
    pos = base + (i // KB) * (2 * ROWS) + i % KB
    return jnp.where((pos >= first) & (pos <= last), 0.0, NEG)


def prep_kernel(queries, out_grad, key_rows, value_rows, pool, spread, own, sems):
    group = lax.axis_index("zh") * 4 + lax.axis_index("yh")
    rows = pl.ds(pl.multiple_of(lax.axis_index("yl") * KB, KB), KB)
    cols = pl.ds(pl.multiple_of(group * HD, HD), HD)
    copies = [
        pltpu.make_async_copy(key_rows.at[rows, cols], spread.at[0, :, 0:HD], sems.at[0]),
        pltpu.make_async_copy(value_rows.at[rows, cols], spread.at[0, :, HD : 2 * HD], sems.at[1]),
        pltpu.make_async_copy(queries, pool.at[:, 0 : OWN * HD], sems.at[2]),
        pltpu.make_async_copy(out_grad, pool.at[:, OWN * HD : 2 * OWN * HD], sems.at[3]),
    ]
    for copy in copies:
        copy.start()
    copies[0].wait()
    copies[1].wait()
    for block in range(1, Z):
        spread[block] = spread[0]
    own[...] = spread[0]
    copies[2].wait()
    copies[3].wait()


def stats_kernel(qd, qd_c, qd_y, kvx, kv2, kv1, kv0, o_own, doc, stats, q_s, do_s, kv_s):
    x, z, c, p = (lax.axis_index(a) for a in ("x", "z", "c", "yl"))
    chip = x * Z + z
    place(z, c, p, (qd, qd_c, qd_y, kvx, kv2, kv1, kv0), q_s, do_s, kv_s)
    first, last = query_spans(doc, chip)
    keys = kv_s[pl.ds(pl.multiple_of(z * KB, KB), SPAN), 0:HD]
    bias = bias_of(chip, c, p, first, last)
    rows = []
    for h in range(HEADS):
        s = dot_nt(keys, q_s[h]) * (SCALE * LOG2E) + bias
        s = s.reshape(SPAN // 8, 8, 2 * ROWS)
        fold = jnp.max(s, axis=0)
        sums = jnp.sum(jnp.exp2(s - fold[None]), axis=0)
        top = jnp.max(fold, axis=0, keepdims=True)
        total = jnp.sum(sums * jnp.exp2(fold - top), axis=0, keepdims=True)
        for r in range(2):
            rows.append((2 * h + r, top[:, r * ROWS : (r + 1) * ROWS]))
            rows.append((12 + 2 * h + r, total[:, r * ROWS : (r + 1) * ROWS]))
    for h in range(OWN):
        prod = qd[:, (OWN + h) * HD : (OWN + h + 1) * HD].astype(F32) * o_own[:, h * HD : (h + 1) * HD].astype(F32)
        rows.append((24 + h, jnp.sum(prod.T, axis=0, keepdims=True)))
    for at, row in rows:
        stats[at : at + 1, :] = row
    stats[27:32, :] = jnp.zeros((5, ROWS), F32)


def merge_kernel(mine, arrived, out):
    c = lax.axis_index("c")
    top = jnp.maximum(mine[0:12, :], arrived[0:12, :])
    out[0:12, :] = top
    out[12:24, :] = mine[12:24, :] * jnp.exp2(mine[0:12, :] - top) + arrived[12:24, :] * jnp.exp2(
        arrived[0:12, :] - top
    )
    for h in range(OWN):
        a, b = mine[24 + h : 25 + h, :], arrived[24 + h : 25 + h, :]
        out[24 + h : 25 + h, :] = jnp.where(c == 0, a, b)
        out[27 + h : 28 + h, :] = jnp.where(c == 0, b, a)
    out[30:32, :] = jnp.zeros((2, ROWS), F32)


def grads_kernel(
    qd, qd_c, qd_y, kvx, kv2, kv1, kv0, doc, stats, stats_y, d2, d1, d0, dx, dq_keep, dq_send, q_s, do_s, kv_s, acc_s
):
    x, z, c, p = (lax.axis_index(a) for a in ("x", "z", "c", "yl"))
    chip = x * Z + z
    place(z, c, p, (qd, qd_c, qd_y, kvx, kv2, kv1, kv0), q_s, do_s, kv_s)
    first, last = query_spans(doc, chip)
    acc_s[...] = jnp.zeros(acc_s.shape, F32)
    top = jnp.maximum(stats[0:12, :], stats_y[0:12, :])
    total = stats[12:24, :] * jnp.exp2(stats[0:12, :] - top) + stats_y[12:24, :] * jnp.exp2(stats_y[0:12, :] - top)
    lse = top + jnp.log(total) * LOG2E

    at = pl.multiple_of(z * KB, KB)
    keys = kv_s[pl.ds(at, SPAN), 0:HD]
    values = kv_s[pl.ds(at, SPAN), HD : 2 * HD]
    keys_t = keys.astype(F32).T.astype(BF16)
    bias = bias_of(chip, c, p, first, last)
    dk = jnp.zeros((SPAN, HD), F32)
    dv = jnp.zeros((SPAN, HD), F32)
    for h in range(HEADS):
        owner, k = h // OWN, 24 + h % OWN
        row_lse = jnp.concatenate([lse[2 * h : 2 * h + 1, :], lse[2 * h + 1 : 2 * h + 2, :]], axis=1)
        deltas = [jnp.where(p == owner, stats[i : i + 1, :], stats_y[i : i + 1, :]) for i in (k, k + OWN)]
        delta = jnp.concatenate(deltas, axis=1)
        q, do = q_s[h], do_s[h]
        probs = jnp.exp2(dot_nt(keys, q) * (SCALE * LOG2E) + bias - row_lse)
        score = (probs * (dot_nt(values, do) - delta)).astype(BF16)
        dv = dv + dot_nn(probs.astype(BF16), do)
        dk = dk + dot_nn(score, q)
        part = dot_nn(keys_t, score) * SCALE
        lower, upper = part[:, 0:ROWS], part[:, ROWS : 2 * ROWS]
        rows = slice((h % OWN) * HD, (h % OWN + 1) * HD)
        dq_keep[owner, rows, :] = jnp.where(c == 0, lower, upper)
        dq_send[owner, rows, :] = jnp.where(c == 0, upper, lower).astype(BF16)
    acc_s[pl.ds(at, SPAN), 0:HD] = dk * SCALE
    acc_s[pl.ds(at, SPAN), HD : 2 * HD] = dv
    for ref, start, size in (
        (dx, 0, KB),
        (d2, KB, PLANE),
        (d1, KB + PLANE, PLANE),
        (d0, KB + 2 * PLANE, PLANE),
    ):
        dk, dv = acc_s[start : start + size, 0:HD], acc_s[start : start + size, HD : 2 * HD]
        low = lax.broadcasted_iota(jnp.int32, (size, HD), 1) < HD // 2
        ref[:, 0:HD] = jnp.where(low, dk, pltpu.roll(dv, HD // 2, 1)).astype(ref.dtype)
        ref[:, HD : 2 * HD] = jnp.where(low, pltpu.roll(dk, HD // 2, 1), dv).astype(ref.dtype)


def plane_kernel(d0, r1, r2, rx, out):
    for block in range(Z):
        rows = slice(block * KB, (block + 1) * KB)
        total = d0[rows, :] + r1[rows, :].astype(F32) + r2[rows, :].astype(F32)
        if block == Z - 1:
            total = total + rx[...].astype(F32)
        for half in range(2):
            out[2 * block + half] = total[:, half * HD : (half + 1) * HD].astype(BF16)


def pool_kernel(keep, arrived, mine, other):
    p = lax.axis_index("yl")
    mine[...] = keep[p] + arrived[p].astype(F32)
    other[...] = (keep[1 - p] + arrived[1 - p].astype(F32)).astype(BF16)


def final_kernel(parts, mine, arrived, query_grad, key_grad, value_grad):
    for h in range(OWN):
        rows = slice(h * HD, (h + 1) * HD)
        query_grad[:, rows] = (mine[rows, :] + arrived[rows, :].astype(F32)).T.astype(BF16)
    halves = []
    for half in range(2):
        total = parts[half].astype(F32)
        for block in range(1, Z):
            total = total + parts[2 * block + half].astype(F32)
        halves.append(total)
    total = jnp.concatenate(halves, axis=0).T
    key_grad[...] = total[0 : HD // 2, :].astype(BF16)
    value_grad[...] = total[HD // 2 :, :].astype(BF16)


def choice(ids, expert, second):
    first_hit, other_hit = ids[0:1, :] == expert, ids[1:2, :] == expert
    hit = jnp.where(first_hit | other_hit, 1.0, 0.0)
    earlier = lax.broadcasted_iota(jnp.int32, (ROWS, ROWS), 0) < lax.broadcasted_iota(jnp.int32, (ROWS, ROWS), 1)
    rank = dot_nn(
        jnp.broadcast_to(hit, (16, ROWS)).astype(BF16), jnp.where(earlier, 1.0, 0.0).astype(BF16)
    )[0:1, :].astype(jnp.int32)
    slot = second * SLOTS + lax.broadcasted_iota(jnp.int32, (SLOTS, ROWS), 0)
    return (slot == rank) & (hit > 0.0), first_hit, other_hit


def select_kernel(mine, ids, out):
    expert = lax.broadcasted_iota(jnp.int32, (16, ROWS), 0)
    hit = jnp.where((ids[0:1, :] == expert) | (ids[1:2, :] == expert), 1.0, 0.0)
    earlier = lax.broadcasted_iota(jnp.int32, (ROWS, ROWS), 0) < lax.broadcasted_iota(jnp.int32, (ROWS, ROWS), 1)
    rank = dot_nn(hit.astype(BF16), jnp.where(earlier, 1.0, 0.0).astype(BF16)).astype(jnp.int32)
    rank = jnp.where(hit > 0.0, rank, -1)
    slot = lax.broadcasted_iota(jnp.int32, (2 * SLOTS, ROWS), 0)
    chosen = [jnp.where(slot == rank[e : e + 1, :], 1.0, 0.0).astype(BF16) for e in range(8)]
    routed = dot_nn(jnp.concatenate(chosen, axis=0), mine[...]).astype(BF16)
    for high in range(2):
        for y in range(8):
            at = (high * 8 + y) * SLOTS
            out[y, high] = routed[at : at + SLOTS, :]


def combine_kernel(rows, rows_other, ids, gates, stored, gate_grad, expert_grad):
    here = lax.axis_index("zh")
    place_in_tp = here * 8 + lax.axis_index("yh") * 2 + lax.axis_index("yl")
    chosen, first_hit, other_hit = choice(ids, place_in_tp // 2, place_in_tp % 2)
    gate = jnp.where(first_hit, gates[0:1, :], 0.0) + jnp.where(other_hit, gates[1:2, :], 0.0)
    slot_gate = jnp.sum(jnp.where(chosen, gate, 0.0), axis=1, keepdims=True)
    total = jnp.zeros((SLOTS, OWN * HD), F32)
    for other in range(2):
        high = here if other == 0 else 1 - here
        for y in range(8):
            routed = (rows[y, here] if other == 0 else rows_other[y]).astype(F32)
            cols = pl.ds(pl.multiple_of((high * 8 + y) * OWN * HD, HD), OWN * HD)
            total = total + routed * stored[:, cols].astype(F32)
            expert_grad[:, cols] = (slot_gate * routed).astype(BF16)
    gate_grad[...] = jnp.sum(total.T, axis=0, keepdims=True)


def local(
    queries,
    key_rows,
    value_rows,
    out_grad,
    attn_out,
    doc_ids,
    row_grad,
    gate_weights,
    expert_ids,
    expert_out,
):
    pool, spread, own = call(
        prep_kernel,
        (
            jax.ShapeDtypeStruct((ROWS, 2 * OWN * HD), BF16),
            jax.ShapeDtypeStruct((Z, KB, 2 * HD), BF16),
            jax.ShapeDtypeStruct((KB, 2 * HD), BF16),
        ),
        [pltpu.SemaphoreType.DMA((4,))],
        name="prep",
        vmem=None,
        in_specs=[pl.BlockSpec(memory_space=pltpu.HBM)] * 4,
    )(queries, out_grad, key_rows, value_rows)
    plane = lax.all_to_all(spread, "z", split_axis=0, concat_axis=0, tiled=True).reshape(PLANE, 2 * HD)
    pool_c = lax.ppermute(pool, "c", [(0, 1), (1, 0)])
    pool_y = lax.ppermute(jnp.concatenate([pool, pool_c], axis=0), "yl", [(0, 1), (1, 0)])
    ids = expert_ids.T
    chosen_rows = call(
        select_kernel,
        jax.ShapeDtypeStruct((8, 2, SLOTS, OWN * HD), BF16),
        [],
        flops=100 * 256 * ROWS * 2 * OWN * HD,
        name="select_rows",
    )(row_grad, ids)
    rows = lax.all_to_all(chosen_rows, ("yh", "yl"), split_axis=0, concat_axis=0, tiled=True)
    away = lax.dynamic_index_in_dim(rows, 1 - lax.axis_index("zh"), 1, keepdims=False)
    rows_other = lax.ppermute(away, "zh", [(0, 1), (1, 0)])

    lone = [((0 * Z + 5) * 2 + 1, (3 * Z + 0) * 2 + 1)]
    ahead2 = lax.ppermute(plane, "x", [(i, i + 2) for i in range(X - 2)])
    ahead1 = lax.ppermute(plane, "x", [(i, i + 1) for i in range(X - 1)])
    aheadx = lax.ppermute(own, ("x", "z", "c"), lone)

    doc = doc_ids.reshape(-1, ROWS)
    shared = (pool, pool_c, pool_y, aheadx, ahead2, ahead1, plane)
    pool_scratch = [
        pltpu.VMEM((HEADS, 2 * ROWS, HD), BF16),
        pltpu.VMEM((HEADS, 2 * ROWS, HD), BF16),
        pltpu.VMEM((PLACES, 2 * HD), BF16),
    ]
    pairs = SPAN * HEADS * 2 * ROWS
    stats = call(
        stats_kernel,
        jax.ShapeDtypeStruct((32, ROWS), F32),
        pool_scratch,
        flops=30 * 2 * HD * pairs,
        name="softmax_stats",
    )(*shared, attn_out, doc)
    stats = call(merge_kernel, jax.ShapeDtypeStruct((32, ROWS), F32), [], nbytes=1 << 15, name="merge_stats")(
        stats, lax.ppermute(stats, "c", [(0, 1), (1, 0)])
    )
    stats_y = lax.ppermute(stats, "yl", [(0, 1), (1, 0)])
    d2, d1, d0, dx, dq_keep, dq_send = call(
        grads_kernel,
        (
            jax.ShapeDtypeStruct((PLANE, 2 * HD), BF16),
            jax.ShapeDtypeStruct((PLANE, 2 * HD), BF16),
            jax.ShapeDtypeStruct((PLANE, 2 * HD), F32),
            jax.ShapeDtypeStruct((KB, 2 * HD), BF16),
            jax.ShapeDtypeStruct((2, OWN * HD, ROWS), F32),
            jax.ShapeDtypeStruct((2, OWN * HD, ROWS), BF16),
        ),
        pool_scratch + [pltpu.VMEM((PLACES, 2 * HD), F32)],
        flops=10 * HD * pairs,
        name="score_grads",
    )(*shared, doc, stats, stats_y)
    back2 = lax.ppermute(d2, "x", [(i + 2, i) for i in range(X - 2)])
    back1 = lax.ppermute(d1, "x", [(i + 1, i) for i in range(X - 1)])
    backx = lax.ppermute(dx, ("x", "z", "c"), [(b, a) for a, b in lone])
    dq_arrived = lax.ppermute(dq_send, "c", [(0, 1), (1, 0)])
    back1, back2, dq_arrived = lax.optimization_barrier((back1, back2, dq_arrived))
    gate_grad, expert_grad = call(
        combine_kernel,
        (
            jax.ShapeDtypeStruct((1, SLOTS), F32),
            jax.ShapeDtypeStruct((SLOTS, expert_out.shape[2]), BF16),
        ),
        [],
        name="combine_grads",
    )(rows, rows_other, ids, gate_weights.T, expert_out[0])
    back1, _ = lax.optimization_barrier((back1, expert_grad))
    dq_mine, dq_other = call(
        pool_kernel,
        (jax.ShapeDtypeStruct((OWN * HD, ROWS), F32), jax.ShapeDtypeStruct((OWN * HD, ROWS), BF16)),
        [],
        name="query_pool",
    )(dq_keep, dq_arrived)
    dq_other = lax.ppermute(dq_other, "yl", [(0, 1), (1, 0)])
    plane_sums = call(plane_kernel, jax.ShapeDtypeStruct((2 * Z, KB, HD), BF16), [], name="plane_sum")(
        d0, back1, back2, backx
    )
    parts = lax.all_to_all(plane_sums, ("z", "yl"), split_axis=0, concat_axis=0, tiled=True)

    query_grad, key_grad, value_grad = call(
        final_kernel,
        (
            jax.ShapeDtypeStruct((ROWS, OWN * HD), BF16),
            jax.ShapeDtypeStruct((HD // 2, ROWS), BF16),
            jax.ShapeDtypeStruct((HD // 2, ROWS), BF16),
        ),
        [],
        name="final_sums",
    )(parts, dq_mine, dq_other)
    return (query_grad, key_grad.T, value_grad.T, gate_grad, expert_grad[None])


def solution(mesh):
    devices = mesh.devices.reshape(X, Z, 2, 2, 4, 2)
    split = Mesh(devices, ("x", "z", "c", "zh", "yh", "yl"))
    ctx, tp = ("x", "z", "c"), ("zh", "yh", "yl")
    in_specs = (
        P(ctx, tp),
        P(ctx, None),
        P(ctx, None),
        P(ctx, tp),
        P(ctx, tp),
        P(),
        P(ctx, tp),
        P(ctx, None),
        P(ctx, None),
        P(ctx, tp, None),
    )
    out_specs = (P(ctx, tp), P(ctx, tp), P(ctx, tp), P(ctx, tp), P(ctx, tp, None))
    return jax.shard_map(local, mesh=split, in_specs=in_specs, out_specs=out_specs, check_vma=False)
```

```python
import functools
import math

import jax
import jax.numpy as jnp
from jax import lax
from jax.experimental import pallas as pl
from jax.experimental.pallas import tpu as pltpu
from jax.sharding import Mesh
from jax.sharding import PartitionSpec as P

HD = 128
X, Z = 4, 6
ROWS = 128
KB = 64
PLANE = Z * KB
HEADS = 6
OWN = 3
WINDOW = 14
SPAN = WINDOW * KB
PLACES = KB + 3 * PLANE
SCALE = 1.0 / math.sqrt(HD)
LOG2E = 1.4426950408889634
NEG = -1e30
SLOTS = 32

F32 = jnp.float32
BF16 = jnp.bfloat16
VMEM_LIMIT = 48 * 1024 * 1024


def dot_nt(a, b):
    return lax.dot_general(a, b, (((1,), (1,)), ((), ())), preferred_element_type=F32)


def dot_nn(a, b):
    return lax.dot_general(a, b, (((1,), (0,)), ((), ())), preferred_element_type=F32)


def call(kernel, out_shape, scratch_shapes, flops=0, nbytes=1 << 20, name=None, vmem=VMEM_LIMIT, **specs):
    return pl.pallas_call(
        kernel,
        out_shape=out_shape,
        scratch_shapes=scratch_shapes,
        compiler_params=pltpu.CompilerParams(vmem_limit_bytes=vmem),
        cost_estimate=pl.CostEstimate(flops=flops, bytes_accessed=nbytes, transcendentals=0),
        name=name,
        **specs,
    )


def place(z, c, p, parts, q_s, do_s, kv_s):
    qd, qd_c, qd_y, kvx, kv2, kv1, kv0 = parts
    for owner, core, ref, base in (
        (p, c, qd, 0),
        (p, 1 - c, qd_c, 0),
        (1 - p, c, qd_y, 0),
        (1 - p, 1 - c, qd_y, ROWS),
    ):
        for h in range(OWN):
            q_s[owner * OWN + h, pl.ds(core * ROWS, ROWS), :] = ref[base : base + ROWS, h * HD : (h + 1) * HD]
            do_s[owner * OWN + h, pl.ds(core * ROWS, ROWS), :] = ref[
                base : base + ROWS, (OWN + h) * HD : (OWN + h + 1) * HD
            ]
    kv_s[0:KB, :] = kvx[...]
    kv_s[KB : KB + PLANE, :] = kv2[...]
    kv_s[KB + PLANE : KB + 2 * PLANE, :] = kv1[...]
    kv_s[KB + 2 * PLANE : KB + 3 * PLANE, :] = kv0[...]


def query_spans(doc, chip):
    docs = doc[...]
    mine = jnp.concatenate([doc[pl.ds(2 * chip, 1), :], doc[pl.ds(2 * chip + 1, 1), :]], axis=1)
    first = jnp.zeros((1, 2 * ROWS), jnp.int32)
    for d in range(1, 8):
        before = jnp.sum((docs < d).astype(F32)).astype(jnp.int32)
        first = jnp.where(mine == d, before, first)
    last = chip * 2 * ROWS + lax.broadcasted_iota(jnp.int32, (1, 2 * ROWS), 1)
    return first, last


def bias_of(chip, c, p, first, last):
    i = lax.broadcasted_iota(jnp.int32, (SPAN, 2 * ROWS), 0)
    base = (2 * (chip - (WINDOW - 1)) + c) * ROWS + p * KB
    pos = base + (i // KB) * (2 * ROWS) + i % KB
    return jnp.where((pos >= first) & (pos <= last), 0.0, NEG)


def prep_kernel(queries, out_grad, key_rows, value_rows, pool, spread, own, sems):
    group = lax.axis_index("zh") * 4 + lax.axis_index("yh")
    rows = pl.ds(pl.multiple_of(lax.axis_index("yl") * KB, KB), KB)
    cols = pl.ds(pl.multiple_of(group * HD, HD), HD)
    copies = [
        pltpu.make_async_copy(key_rows.at[rows, cols], spread.at[0, :, 0:HD], sems.at[0]),
        pltpu.make_async_copy(value_rows.at[rows, cols], spread.at[0, :, HD : 2 * HD], sems.at[1]),
        pltpu.make_async_copy(queries, pool.at[:, 0 : OWN * HD], sems.at[2]),
        pltpu.make_async_copy(out_grad, pool.at[:, OWN * HD : 2 * OWN * HD], sems.at[3]),
    ]
    for copy in copies:
        copy.start()
    copies[0].wait()
    copies[1].wait()
    for block in range(1, Z):
        spread[block] = spread[0]
    own[...] = spread[0]
    copies[2].wait()
    copies[3].wait()


def stats_kernel(qd, qd_c, qd_y, kvx, kv2, kv1, kv0, o_own, doc, stats, q_s, do_s, kv_s):
    x, z, c, p = (lax.axis_index(a) for a in ("x", "z", "c", "yl"))
    chip = x * Z + z
    place(z, c, p, (qd, qd_c, qd_y, kvx, kv2, kv1, kv0), q_s, do_s, kv_s)
    first, last = query_spans(doc, chip)
    keys = kv_s[pl.ds(pl.multiple_of(z * KB, KB), SPAN), 0:HD]
    bias = bias_of(chip, c, p, first, last)
    rows = []
    for h in range(HEADS):
        s = dot_nt(keys, q_s[h]) * (SCALE * LOG2E) + bias
        s = s.reshape(SPAN // 8, 8, 2 * ROWS)
        fold = jnp.max(s, axis=0)
        sums = jnp.sum(jnp.exp2(s - fold[None]), axis=0)
        top = jnp.max(fold, axis=0, keepdims=True)
        total = jnp.sum(sums * jnp.exp2(fold - top), axis=0, keepdims=True)
        for r in range(2):
            rows.append((2 * h + r, top[:, r * ROWS : (r + 1) * ROWS]))
            rows.append((12 + 2 * h + r, total[:, r * ROWS : (r + 1) * ROWS]))
    for h in range(OWN):
        prod = qd[:, (OWN + h) * HD : (OWN + h + 1) * HD].astype(F32) * o_own[:, h * HD : (h + 1) * HD].astype(F32)
        rows.append((24 + h, jnp.sum(prod.T, axis=0, keepdims=True)))
    for at, row in rows:
        stats[at : at + 1, :] = row
    stats[27:32, :] = jnp.zeros((5, ROWS), F32)


def merge_kernel(mine, arrived, out):
    c = lax.axis_index("c")
    top = jnp.maximum(mine[0:12, :], arrived[0:12, :])
    out[0:12, :] = top
    out[12:24, :] = mine[12:24, :] * jnp.exp2(mine[0:12, :] - top) + arrived[12:24, :] * jnp.exp2(
        arrived[0:12, :] - top
    )
    for h in range(OWN):
        a, b = mine[24 + h : 25 + h, :], arrived[24 + h : 25 + h, :]
        out[24 + h : 25 + h, :] = jnp.where(c == 0, a, b)
        out[27 + h : 28 + h, :] = jnp.where(c == 0, b, a)
    out[30:32, :] = jnp.zeros((2, ROWS), F32)


def grads_kernel(
    qd, qd_c, qd_y, kvx, kv2, kv1, kv0, doc, stats, stats_y, d2, d1, d0, dx, dq_keep, dq_send, q_s, do_s, kv_s, acc_s, dq_s
):
    x, z, c, p = (lax.axis_index(a) for a in ("x", "z", "c", "yl"))
    chip = x * Z + z
    place(z, c, p, (qd, qd_c, qd_y, kvx, kv2, kv1, kv0), q_s, do_s, kv_s)
    first, last = query_spans(doc, chip)
    acc_s[...] = jnp.zeros(acc_s.shape, F32)
    top = jnp.maximum(stats[0:12, :], stats_y[0:12, :])
    total = stats[12:24, :] * jnp.exp2(stats[0:12, :] - top) + stats_y[12:24, :] * jnp.exp2(stats_y[0:12, :] - top)
    lse = top + jnp.log(total) * LOG2E

    at = pl.multiple_of(z * KB, KB)
    keys = kv_s[pl.ds(at, SPAN), 0:HD]
    values = kv_s[pl.ds(at, SPAN), HD : 2 * HD]
    keys_t = keys.astype(F32).T.astype(BF16)
    bias = bias_of(chip, c, p, first, last)
    dk = jnp.zeros((SPAN, HD), F32)
    dv = jnp.zeros((SPAN, HD), F32)
    for h in range(HEADS):
        owner, k = h // OWN, 24 + h % OWN
        row_lse = jnp.concatenate([lse[2 * h : 2 * h + 1, :], lse[2 * h + 1 : 2 * h + 2, :]], axis=1)
        deltas = [jnp.where(p == owner, stats[i : i + 1, :], stats_y[i : i + 1, :]) for i in (k, k + OWN)]
        delta = jnp.concatenate(deltas, axis=1)
        q, do = q_s[h], do_s[h]
        probs = jnp.exp2(dot_nt(keys, q) * (SCALE * LOG2E) + bias - row_lse)
        score = (probs * (dot_nt(values, do) - delta)).astype(BF16)
        dv = dv + dot_nn(probs.astype(BF16), do)
        dk = dk + dot_nn(score, q)
        dq_s[h] = dot_nn(keys_t, score) * SCALE
    for h in range(OWN):
        rows = slice(h * HD, (h + 1) * HD)
        dq_keep[rows, :] = dq_s[p * OWN + h]
        dq_send[rows, :] = dq_s[(1 - p) * OWN + h].astype(BF16)
    acc_s[pl.ds(at, SPAN), 0:HD] = dk * SCALE
    acc_s[pl.ds(at, SPAN), HD : 2 * HD] = dv
    for ref, start, size in (
        (dx, 0, KB),
        (d2, KB, PLANE),
        (d1, KB + PLANE, PLANE),
        (d0, KB + 2 * PLANE, PLANE),
    ):
        dk, dv = acc_s[start : start + size, 0:HD], acc_s[start : start + size, HD : 2 * HD]
        low = lax.broadcasted_iota(jnp.int32, (size, HD), 1) < HD // 2
        ref[:, 0:HD] = jnp.where(low, dk, pltpu.roll(dv, HD // 2, 1)).astype(ref.dtype)
        ref[:, HD : 2 * HD] = jnp.where(low, pltpu.roll(dk, HD // 2, 1), dv).astype(ref.dtype)


def plane_kernel(d0, r1, r2, rx, out):
    for block in range(Z):
        rows = slice(block * KB, (block + 1) * KB)
        total = d0[rows, :] + r1[rows, :].astype(F32) + r2[rows, :].astype(F32)
        if block == Z - 1:
            total = total + rx[...].astype(F32)
        for half in range(2):
            out[2 * block + half] = total[:, half * HD : (half + 1) * HD].astype(BF16)


def pool_kernel(keep, arrived, mine, other):
    lower = lax.axis_index("c") == 0
    total = keep[...] + arrived[...].astype(F32)
    mine[...] = jnp.where(lower, total[:, 0:ROWS], total[:, ROWS : 2 * ROWS])
    other[...] = jnp.where(lower, total[:, ROWS : 2 * ROWS], total[:, 0:ROWS]).astype(BF16)


def final_kernel(parts, mine, arrived, query_grad, key_grad, value_grad):
    for h in range(OWN):
        rows = slice(h * HD, (h + 1) * HD)
        query_grad[:, rows] = (mine[rows, :] + arrived[rows, :].astype(F32)).T.astype(BF16)
    halves = []
    for half in range(2):
        total = parts[half].astype(F32)
        for block in range(1, Z):
            total = total + parts[2 * block + half].astype(F32)
        halves.append(total)
    total = jnp.concatenate(halves, axis=0).T
    key_grad[...] = total[0 : HD // 2, :].astype(BF16)
    value_grad[...] = total[HD // 2 :, :].astype(BF16)


def choice(ids, expert, second):
    first_hit, other_hit = ids[0:1, :] == expert, ids[1:2, :] == expert
    hit = jnp.where(first_hit | other_hit, 1.0, 0.0)
    earlier = lax.broadcasted_iota(jnp.int32, (ROWS, ROWS), 0) < lax.broadcasted_iota(jnp.int32, (ROWS, ROWS), 1)
    rank = dot_nn(
        jnp.broadcast_to(hit, (16, ROWS)).astype(BF16), jnp.where(earlier, 1.0, 0.0).astype(BF16)
    )[0:1, :].astype(jnp.int32)
    slot = second * SLOTS + lax.broadcasted_iota(jnp.int32, (SLOTS, ROWS), 0)
    return (slot == rank) & (hit > 0.0), first_hit, other_hit


def select_kernel(mine, ids, gates, out, ids_on, gates_on):
    ids_on[...] = ids[...]
    gates_on[...] = gates[...]
    expert = lax.broadcasted_iota(jnp.int32, (16, ROWS), 0)
    hit = jnp.where((ids[0:1, :] == expert) | (ids[1:2, :] == expert), 1.0, 0.0)
    earlier = lax.broadcasted_iota(jnp.int32, (ROWS, ROWS), 0) < lax.broadcasted_iota(jnp.int32, (ROWS, ROWS), 1)
    rank = dot_nn(hit.astype(BF16), jnp.where(earlier, 1.0, 0.0).astype(BF16)).astype(jnp.int32)
    rank = jnp.where(hit > 0.0, rank, -1)
    slot = lax.broadcasted_iota(jnp.int32, (2 * SLOTS, ROWS), 0)
    chosen = [jnp.where(slot == rank[e : e + 1, :], 1.0, 0.0).astype(BF16) for e in range(8)]
    routed = dot_nn(jnp.concatenate(chosen, axis=0), mine[...]).astype(BF16)
    for high in range(2):
        for y in range(8):
            at = (high * 8 + y) * SLOTS
            out[y, high] = routed[at : at + SLOTS, :]


def combine_kernel(rows, rows_other, ids, gates, stored, gate_grad, expert_grad):
    here = lax.axis_index("zh")
    place_in_tp = here * 8 + lax.axis_index("yh") * 2 + lax.axis_index("yl")
    chosen, first_hit, other_hit = choice(ids, place_in_tp // 2, place_in_tp % 2)
    gate = jnp.where(first_hit, gates[0:1, :], 0.0) + jnp.where(other_hit, gates[1:2, :], 0.0)
    slot_gate = jnp.sum(jnp.where(chosen, gate, 0.0), axis=1, keepdims=True)
    total = jnp.zeros((SLOTS, OWN * HD), F32)
    for other in range(2):
        high = here if other == 0 else 1 - here
        for y in range(8):
            routed = (rows[y, here] if other == 0 else rows_other[y]).astype(F32)
            cols = pl.ds(pl.multiple_of((high * 8 + y) * OWN * HD, HD), OWN * HD)
            total = total + routed * stored[:, cols].astype(F32)
            expert_grad[:, cols] = (slot_gate * routed).astype(BF16)
    gate_grad[...] = jnp.sum(total.T, axis=0, keepdims=True)


def local(
    queries,
    key_rows,
    value_rows,
    out_grad,
    attn_out,
    doc_ids,
    row_grad,
    gate_weights,
    expert_ids,
    expert_out,
):
    pool, spread, own = call(
        prep_kernel,
        (
            jax.ShapeDtypeStruct((ROWS, 2 * OWN * HD), BF16),
            jax.ShapeDtypeStruct((Z, KB, 2 * HD), BF16),
            jax.ShapeDtypeStruct((KB, 2 * HD), BF16),
        ),
        [pltpu.SemaphoreType.DMA((4,))],
        name="prep",
        vmem=None,
        in_specs=[pl.BlockSpec(memory_space=pltpu.HBM)] * 4,
    )(queries, out_grad, key_rows, value_rows)
    plane = lax.all_to_all(spread, "z", split_axis=0, concat_axis=0, tiled=True).reshape(PLANE, 2 * HD)
    pool_c = lax.ppermute(pool, "c", [(0, 1), (1, 0)])
    pool_y = lax.ppermute(jnp.concatenate([pool, pool_c], axis=0), "yl", [(0, 1), (1, 0)])
    ids = expert_ids.T
    chosen_rows, ids, gates = call(
        select_kernel,
        (
            jax.ShapeDtypeStruct((8, 2, SLOTS, OWN * HD), BF16),
            jax.ShapeDtypeStruct((2, ROWS), jnp.int32),
            jax.ShapeDtypeStruct((2, ROWS), F32),
        ),
        [],
        flops=100 * 256 * ROWS * 2 * OWN * HD,
        name="select_rows",
    )(row_grad, ids, gate_weights.T)
    rows = lax.all_to_all(chosen_rows, ("yh", "yl"), split_axis=0, concat_axis=0, tiled=True)
    away = lax.dynamic_index_in_dim(rows, 1 - lax.axis_index("zh"), 1, keepdims=False)
    rows_other = lax.ppermute(away, "zh", [(0, 1), (1, 0)])

    lone = [((0 * Z + 5) * 2 + 1, (3 * Z + 0) * 2 + 1)]
    ahead2 = lax.ppermute(plane, "x", [(i, i + 2) for i in range(X - 2)])
    ahead1 = lax.ppermute(plane, "x", [(i, i + 1) for i in range(X - 1)])
    aheadx = lax.ppermute(own, ("x", "z", "c"), lone)

    doc = doc_ids.reshape(-1, ROWS)
    shared = (pool, pool_c, pool_y, aheadx, ahead2, ahead1, plane)
    pool_scratch = [
        pltpu.VMEM((HEADS, 2 * ROWS, HD), BF16),
        pltpu.VMEM((HEADS, 2 * ROWS, HD), BF16),
        pltpu.VMEM((PLACES, 2 * HD), BF16),
    ]
    pairs = SPAN * HEADS * 2 * ROWS
    stats = call(
        stats_kernel,
        jax.ShapeDtypeStruct((32, ROWS), F32),
        pool_scratch,
        flops=30 * 2 * HD * pairs,
        name="softmax_stats",
    )(*shared, attn_out, doc)
    stats = call(merge_kernel, jax.ShapeDtypeStruct((32, ROWS), F32), [], nbytes=1 << 15, name="merge_stats")(
        stats, lax.ppermute(stats, "c", [(0, 1), (1, 0)])
    )
    stats_y = lax.ppermute(stats, "yl", [(0, 1), (1, 0)])
    d2, d1, d0, dx, dq_keep, dq_send = call(
        grads_kernel,
        (
            jax.ShapeDtypeStruct((PLANE, 2 * HD), BF16),
            jax.ShapeDtypeStruct((PLANE, 2 * HD), BF16),
            jax.ShapeDtypeStruct((PLANE, 2 * HD), F32),
            jax.ShapeDtypeStruct((KB, 2 * HD), BF16),
            jax.ShapeDtypeStruct((OWN * HD, 2 * ROWS), F32),
            jax.ShapeDtypeStruct((OWN * HD, 2 * ROWS), BF16),
        ),
        pool_scratch + [pltpu.VMEM((PLACES, 2 * HD), F32), pltpu.VMEM((HEADS, HD, 2 * ROWS), F32)],
        flops=10 * HD * pairs,
        name="score_grads",
    )(*shared, doc, stats, stats_y)
    back2 = lax.ppermute(d2, "x", [(i + 2, i) for i in range(X - 2)])
    back1 = lax.ppermute(d1, "x", [(i + 1, i) for i in range(X - 1)])
    backx = lax.ppermute(dx, ("x", "z", "c"), [(b, a) for a, b in lone])
    dq_arrived = lax.ppermute(dq_send, "yl", [(0, 1), (1, 0)])
    back1, back2, dq_arrived = lax.optimization_barrier((back1, back2, dq_arrived))
    gate_grad, expert_grad = call(
        combine_kernel,
        (
            jax.ShapeDtypeStruct((1, SLOTS), F32),
            jax.ShapeDtypeStruct((SLOTS, expert_out.shape[2]), BF16),
        ),
        [],
        name="combine_grads",
    )(rows, rows_other, ids, gates, expert_out[0])
    back1, _ = lax.optimization_barrier((back1, expert_grad))
    dq_mine, dq_other = call(
        pool_kernel,
        (jax.ShapeDtypeStruct((OWN * HD, ROWS), F32), jax.ShapeDtypeStruct((OWN * HD, ROWS), BF16)),
        [],
        name="query_pool",
    )(dq_keep, dq_arrived)
    dq_other = lax.ppermute(dq_other, "c", [(0, 1), (1, 0)])
    plane_sums = call(plane_kernel, jax.ShapeDtypeStruct((2 * Z, KB, HD), BF16), [], name="plane_sum")(
        d0, back1, back2, backx
    )
    parts = lax.all_to_all(plane_sums, ("z", "yl"), split_axis=0, concat_axis=0, tiled=True)

    query_grad, key_grad, value_grad = call(
        final_kernel,
        (
            jax.ShapeDtypeStruct((ROWS, OWN * HD), BF16),
            jax.ShapeDtypeStruct((HD // 2, ROWS), BF16),
            jax.ShapeDtypeStruct((HD // 2, ROWS), BF16),
        ),
        [],
        name="final_sums",
    )(parts, dq_mine, dq_other)
    return (query_grad, key_grad.T, value_grad.T, gate_grad, expert_grad[None])


def solution(mesh):
    devices = mesh.devices.reshape(X, Z, 2, 2, 4, 2)
    split = Mesh(devices, ("x", "z", "c", "zh", "yh", "yl"))
    ctx, tp = ("x", "z", "c"), ("zh", "yh", "yl")
    in_specs = (
        P(ctx, tp),
        P(ctx, None),
        P(ctx, None),
        P(ctx, tp),
        P(ctx, tp),
        P(),
        P(ctx, tp),
        P(ctx, None),
        P(ctx, None),
        P(ctx, tp, None),
    )
    out_specs = (P(ctx, tp), P(ctx, tp), P(ctx, tp), P(ctx, tp), P(ctx, tp, None))
    return jax.shard_map(local, mesh=split, in_specs=in_specs, out_specs=out_specs, check_vma=False)
```

```python
import functools
import math

import jax
import jax.numpy as jnp
from jax import lax
from jax.experimental import pallas as pl
from jax.experimental.pallas import tpu as pltpu
from jax.sharding import Mesh
from jax.sharding import PartitionSpec as P

HD = 128
X, Z = 4, 6
ROWS = 128
KB = 64
PLANE = Z * KB
HEADS = 6
OWN = 3
WINDOW = 14
SPAN = WINDOW * KB
PLACES = KB + 3 * PLANE
SCALE = 1.0 / math.sqrt(HD)
LOG2E = 1.4426950408889634
NEG = -1e30
SLOTS = 32

F32 = jnp.float32
BF16 = jnp.bfloat16
VMEM_LIMIT = 48 * 1024 * 1024


def dot_nt(a, b):
    return lax.dot_general(a, b, (((1,), (1,)), ((), ())), preferred_element_type=F32)


def dot_nn(a, b):
    return lax.dot_general(a, b, (((1,), (0,)), ((), ())), preferred_element_type=F32)


def call(kernel, out_shape, scratch_shapes, flops=0, nbytes=1 << 20, name=None, vmem=VMEM_LIMIT, **specs):
    return pl.pallas_call(
        kernel,
        out_shape=out_shape,
        scratch_shapes=scratch_shapes,
        compiler_params=pltpu.CompilerParams(vmem_limit_bytes=vmem),
        cost_estimate=pl.CostEstimate(flops=flops, bytes_accessed=nbytes, transcendentals=0),
        name=name,
        **specs,
    )


def place(z, c, p, parts, q_s, do_s, kv_s):
    qd, qd_c, qd_y, kvx, kv2, kv1, kv0 = parts
    for owner, core, ref, base in (
        (p, c, qd, 0),
        (p, 1 - c, qd_c, 0),
        (1 - p, c, qd_y, 0),
        (1 - p, 1 - c, qd_y, ROWS),
    ):
        for h in range(OWN):
            q_s[owner * OWN + h, pl.ds(core * ROWS, ROWS), :] = ref[base : base + ROWS, h * HD : (h + 1) * HD]
            do_s[owner * OWN + h, pl.ds(core * ROWS, ROWS), :] = ref[
                base : base + ROWS, (OWN + h) * HD : (OWN + h + 1) * HD
            ]
    kv_s[0:KB, :] = kvx[...]
    kv_s[KB : KB + PLANE, :] = kv2[...]
    kv_s[KB + PLANE : KB + 2 * PLANE, :] = kv1[...]
    kv_s[KB + 2 * PLANE : KB + 3 * PLANE, :] = kv0[...]


def query_spans(doc, chip):
    docs = doc[...]
    mine = jnp.concatenate([doc[pl.ds(2 * chip, 1), :], doc[pl.ds(2 * chip + 1, 1), :]], axis=1)
    first = jnp.zeros((1, 2 * ROWS), jnp.int32)
    for d in range(1, 8):
        before = jnp.sum((docs < d).astype(F32)).astype(jnp.int32)
        first = jnp.where(mine == d, before, first)
    last = chip * 2 * ROWS + lax.broadcasted_iota(jnp.int32, (1, 2 * ROWS), 1)
    return first, last


def bias_of(chip, c, p, first, last):
    i = lax.broadcasted_iota(jnp.int32, (SPAN, 2 * ROWS), 0)
    base = (2 * (chip - (WINDOW - 1)) + c) * ROWS + p * KB
    pos = base + (i // KB) * (2 * ROWS) + i % KB
    return jnp.where((pos >= first) & (pos <= last), 0.0, NEG)


def prep_kernel(queries, out_grad, key_rows, value_rows, pool, spread, own, sems):
    group = lax.axis_index("zh") * 4 + lax.axis_index("yh")
    rows = pl.ds(pl.multiple_of(lax.axis_index("yl") * KB, KB), KB)
    cols = pl.ds(pl.multiple_of(group * HD, HD), HD)
    copies = [
        pltpu.make_async_copy(key_rows.at[rows, cols], spread.at[0, :, 0:HD], sems.at[0]),
        pltpu.make_async_copy(value_rows.at[rows, cols], spread.at[0, :, HD : 2 * HD], sems.at[1]),
        pltpu.make_async_copy(queries, pool.at[:, 0 : OWN * HD], sems.at[2]),
        pltpu.make_async_copy(out_grad, pool.at[:, OWN * HD : 2 * OWN * HD], sems.at[3]),
    ]
    for copy in copies:
        copy.start()
    copies[0].wait()
    copies[1].wait()
    for block in range(1, Z):
        spread[block] = spread[0]
    own[...] = spread[0]
    copies[2].wait()
    copies[3].wait()


def stats_kernel(qd, qd_c, qd_y, kvx, kv2, kv1, kv0, o_own, doc, stats, q_s, do_s, kv_s):
    x, z, c, p = (lax.axis_index(a) for a in ("x", "z", "c", "yl"))
    chip = x * Z + z
    place(z, c, p, (qd, qd_c, qd_y, kvx, kv2, kv1, kv0), q_s, do_s, kv_s)
    first, last = query_spans(doc, chip)
    keys = kv_s[pl.ds(pl.multiple_of(z * KB, KB), SPAN), 0:HD]
    bias = bias_of(chip, c, p, first, last)
    rows = []
    for h in range(HEADS):
        s = dot_nt(keys, q_s[h]) * (SCALE * LOG2E) + bias
        s = s.reshape(SPAN // 8, 8, 2 * ROWS)
        fold = jnp.max(s, axis=0)
        sums = jnp.sum(jnp.exp2(s - fold[None]), axis=0)
        top = jnp.max(fold, axis=0, keepdims=True)
        total = jnp.sum(sums * jnp.exp2(fold - top), axis=0, keepdims=True)
        for r in range(2):
            rows.append((2 * h + r, top[:, r * ROWS : (r + 1) * ROWS]))
            rows.append((12 + 2 * h + r, total[:, r * ROWS : (r + 1) * ROWS]))
    for h in range(OWN):
        prod = qd[:, (OWN + h) * HD : (OWN + h + 1) * HD].astype(F32) * o_own[:, h * HD : (h + 1) * HD].astype(F32)
        rows.append((24 + h, jnp.sum(prod.T, axis=0, keepdims=True)))
    for at, row in rows:
        stats[at : at + 1, :] = row
    stats[27:32, :] = jnp.zeros((5, ROWS), F32)


def merge_kernel(mine, arrived, out):
    c = lax.axis_index("c")
    top = jnp.maximum(mine[0:12, :], arrived[0:12, :])
    out[0:12, :] = top
    out[12:24, :] = mine[12:24, :] * jnp.exp2(mine[0:12, :] - top) + arrived[12:24, :] * jnp.exp2(
        arrived[0:12, :] - top
    )
    for h in range(OWN):
        a, b = mine[24 + h : 25 + h, :], arrived[24 + h : 25 + h, :]
        out[24 + h : 25 + h, :] = jnp.where(c == 0, a, b)
        out[27 + h : 28 + h, :] = jnp.where(c == 0, b, a)
    out[30:32, :] = jnp.zeros((2, ROWS), F32)


def grads_kernel(
    qd, qd_c, qd_y, kvx, kv2, kv1, kv0, doc, stats, stats_y, d2, d1, d0, dx, dq_keep, dq_send, q_s, do_s, kv_s, acc_s, dq_s
):
    x, z, c, p = (lax.axis_index(a) for a in ("x", "z", "c", "yl"))
    chip = x * Z + z
    place(z, c, p, (qd, qd_c, qd_y, kvx, kv2, kv1, kv0), q_s, do_s, kv_s)
    first, last = query_spans(doc, chip)
    acc_s[...] = jnp.zeros(acc_s.shape, F32)
    top = jnp.maximum(stats[0:12, :], stats_y[0:12, :])
    total = stats[12:24, :] * jnp.exp2(stats[0:12, :] - top) + stats_y[12:24, :] * jnp.exp2(stats_y[0:12, :] - top)
    lse = top + jnp.log(total) * LOG2E

    at = pl.multiple_of(z * KB, KB)
    keys = kv_s[pl.ds(at, SPAN), 0:HD]
    values = kv_s[pl.ds(at, SPAN), HD : 2 * HD]
    keys_t = keys.astype(F32).T.astype(BF16)
    bias = bias_of(chip, c, p, first, last)
    dk = jnp.zeros((SPAN, HD), F32)
    dv = jnp.zeros((SPAN, HD), F32)
    for h in range(HEADS):
        owner, k = h // OWN, 24 + h % OWN
        row_lse = jnp.concatenate([lse[2 * h : 2 * h + 1, :], lse[2 * h + 1 : 2 * h + 2, :]], axis=1)
        deltas = [jnp.where(p == owner, stats[i : i + 1, :], stats_y[i : i + 1, :]) for i in (k, k + OWN)]
        delta = jnp.concatenate(deltas, axis=1)
        q, do = q_s[h], do_s[h]
        probs = jnp.exp2(dot_nt(keys, q) * (SCALE * LOG2E) + bias - row_lse)
        score = (probs * (dot_nt(values, do) - delta)).astype(BF16)
        dv = dv + dot_nn(probs.astype(BF16), do)
        dk = dk + dot_nn(score, q)
        dq_s[h] = dot_nn(keys_t, score) * SCALE
    for h in range(OWN):
        rows = slice(h * HD, (h + 1) * HD)
        dq_keep[rows, :] = dq_s[p * OWN + h]
        dq_send[rows, :] = dq_s[(1 - p) * OWN + h].astype(BF16)
    acc_s[pl.ds(at, SPAN), 0:HD] = dk * SCALE
    acc_s[pl.ds(at, SPAN), HD : 2 * HD] = dv
    for ref, start, size in (
        (dx, 0, KB),
        (d2, KB, PLANE),
        (d1, KB + PLANE, PLANE),
        (d0, KB + 2 * PLANE, PLANE),
    ):
        dk, dv = acc_s[start : start + size, 0:HD], acc_s[start : start + size, HD : 2 * HD]
        low = lax.broadcasted_iota(jnp.int32, (size, HD), 1) < HD // 2
        ref[:, 0:HD] = jnp.where(low, dk, pltpu.roll(dv, HD // 2, 1)).astype(ref.dtype)
        ref[:, HD : 2 * HD] = jnp.where(low, pltpu.roll(dk, HD // 2, 1), dv).astype(ref.dtype)


def plane_kernel(d0, r2, r1, rx, out):
    for block in range(Z):
        rows = slice(block * KB, (block + 1) * KB)
        total = d0[rows, :] + r1[rows, :].astype(F32) + r2[rows, :].astype(F32)
        if block == Z - 1:
            total = total + rx[...].astype(F32)
        for half in range(2):
            out[2 * block + half] = total[:, half * HD : (half + 1) * HD].astype(BF16)


def pool_kernel(keep, arrived, mine, other):
    lower = lax.axis_index("c") == 0
    total = keep[...] + arrived[...].astype(F32)
    mine[...] = jnp.where(lower, total[:, 0:ROWS], total[:, ROWS : 2 * ROWS])
    other[...] = jnp.where(lower, total[:, ROWS : 2 * ROWS], total[:, 0:ROWS]).astype(BF16)


def final_kernel(parts, mine, arrived, query_grad, key_grad, value_grad):
    for h in range(OWN):
        rows = slice(h * HD, (h + 1) * HD)
        query_grad[:, rows] = (mine[rows, :] + arrived[rows, :].astype(F32)).T.astype(BF16)
    halves = []
    for half in range(2):
        total = parts[half].astype(F32)
        for block in range(1, Z):
            total = total + parts[2 * block + half].astype(F32)
        halves.append(total)
    total = jnp.concatenate(halves, axis=0).T
    key_grad[...] = total[0 : HD // 2, :].astype(BF16)
    value_grad[...] = total[HD // 2 :, :].astype(BF16)


def choice(ids, expert, second):
    first_hit, other_hit = ids[0:1, :] == expert, ids[1:2, :] == expert
    hit = jnp.where(first_hit | other_hit, 1.0, 0.0)
    earlier = lax.broadcasted_iota(jnp.int32, (ROWS, ROWS), 0) < lax.broadcasted_iota(jnp.int32, (ROWS, ROWS), 1)
    rank = dot_nn(
        jnp.broadcast_to(hit, (16, ROWS)).astype(BF16), jnp.where(earlier, 1.0, 0.0).astype(BF16)
    )[0:1, :].astype(jnp.int32)
    slot = second * SLOTS + lax.broadcasted_iota(jnp.int32, (SLOTS, ROWS), 0)
    return (slot == rank) & (hit > 0.0), first_hit, other_hit


def select_kernel(mine, ids, gates, out, ids_on, gates_on):
    ids_on[...] = ids[...]
    gates_on[...] = gates[...]
    expert = lax.broadcasted_iota(jnp.int32, (16, ROWS), 0)
    hit = jnp.where((ids[0:1, :] == expert) | (ids[1:2, :] == expert), 1.0, 0.0)
    earlier = lax.broadcasted_iota(jnp.int32, (ROWS, ROWS), 0) < lax.broadcasted_iota(jnp.int32, (ROWS, ROWS), 1)
    rank = dot_nn(hit.astype(BF16), jnp.where(earlier, 1.0, 0.0).astype(BF16)).astype(jnp.int32)
    rank = jnp.where(hit > 0.0, rank, -1)
    slot = lax.broadcasted_iota(jnp.int32, (2 * SLOTS, ROWS), 0)
    chosen = [jnp.where(slot == rank[e : e + 1, :], 1.0, 0.0).astype(BF16) for e in range(8)]
    routed = dot_nn(jnp.concatenate(chosen, axis=0), mine[...]).astype(BF16)
    for high in range(2):
        for y in range(8):
            at = (high * 8 + y) * SLOTS
            out[y, high] = routed[at : at + SLOTS, :]


def combine_kernel(rows, rows_other, ids, gates, stored, gate_grad, expert_grad):
    here = lax.axis_index("zh")
    place_in_tp = here * 8 + lax.axis_index("yh") * 2 + lax.axis_index("yl")
    chosen, first_hit, other_hit = choice(ids, place_in_tp // 2, place_in_tp % 2)
    gate = jnp.where(first_hit, gates[0:1, :], 0.0) + jnp.where(other_hit, gates[1:2, :], 0.0)
    slot_gate = jnp.sum(jnp.where(chosen, gate, 0.0), axis=1, keepdims=True)
    total = jnp.zeros((SLOTS, OWN * HD), F32)
    for other in range(2):
        high = here if other == 0 else 1 - here
        for y in range(8):
            routed = (rows[y, here] if other == 0 else rows_other[y]).astype(F32)
            cols = pl.ds(pl.multiple_of((high * 8 + y) * OWN * HD, HD), OWN * HD)
            total = total + routed * stored[:, cols].astype(F32)
            expert_grad[:, cols] = (slot_gate * routed).astype(BF16)
    gate_grad[...] = jnp.sum(total.T, axis=0, keepdims=True)


def local(
    queries,
    key_rows,
    value_rows,
    out_grad,
    attn_out,
    doc_ids,
    row_grad,
    gate_weights,
    expert_ids,
    expert_out,
):
    pool, spread, own = call(
        prep_kernel,
        (
            jax.ShapeDtypeStruct((ROWS, 2 * OWN * HD), BF16),
            jax.ShapeDtypeStruct((Z, KB, 2 * HD), BF16),
            jax.ShapeDtypeStruct((KB, 2 * HD), BF16),
        ),
        [pltpu.SemaphoreType.DMA((4,))],
        name="prep",
        vmem=None,
        in_specs=[pl.BlockSpec(memory_space=pltpu.HBM)] * 4,
    )(queries, out_grad, key_rows, value_rows)
    plane = lax.all_to_all(spread, "z", split_axis=0, concat_axis=0, tiled=True).reshape(PLANE, 2 * HD)
    pool_c = lax.ppermute(pool, "c", [(0, 1), (1, 0)])
    pool_y = lax.ppermute(jnp.concatenate([pool, pool_c], axis=0), "yl", [(0, 1), (1, 0)])
    ids = expert_ids.T
    chosen_rows, ids, gates = call(
        select_kernel,
        (
            jax.ShapeDtypeStruct((8, 2, SLOTS, OWN * HD), BF16),
            jax.ShapeDtypeStruct((2, ROWS), jnp.int32),
            jax.ShapeDtypeStruct((2, ROWS), F32),
        ),
        [],
        flops=100 * 256 * ROWS * 2 * OWN * HD,
        name="select_rows",
    )(row_grad, ids, gate_weights.T)
    rows = lax.all_to_all(chosen_rows, ("yh", "yl"), split_axis=0, concat_axis=0, tiled=True)
    away = lax.dynamic_index_in_dim(rows, 1 - lax.axis_index("zh"), 1, keepdims=False)
    rows_other = lax.ppermute(away, "zh", [(0, 1), (1, 0)])

    lone = [((0 * Z + 5) * 2 + 1, (3 * Z + 0) * 2 + 1)]
    ahead2 = lax.ppermute(plane, "x", [(i, i + 2) for i in range(X - 2)])
    ahead1 = lax.ppermute(plane, "x", [(i, i + 1) for i in range(X - 1)])
    aheadx = lax.ppermute(own, ("x", "z", "c"), lone)

    doc = doc_ids.reshape(-1, ROWS)
    shared = (pool, pool_c, pool_y, aheadx, ahead2, ahead1, plane)
    pool_scratch = [
        pltpu.VMEM((HEADS, 2 * ROWS, HD), BF16),
        pltpu.VMEM((HEADS, 2 * ROWS, HD), BF16),
        pltpu.VMEM((PLACES, 2 * HD), BF16),
    ]
    pairs = SPAN * HEADS * 2 * ROWS
    stats = call(
        stats_kernel,
        jax.ShapeDtypeStruct((32, ROWS), F32),
        pool_scratch,
        flops=30 * 2 * HD * pairs,
        name="softmax_stats",
    )(*shared, attn_out, doc)
    stats = call(merge_kernel, jax.ShapeDtypeStruct((32, ROWS), F32), [], nbytes=1 << 15, name="merge_stats")(
        stats, lax.ppermute(stats, "c", [(0, 1), (1, 0)])
    )
    stats_y = lax.ppermute(stats, "yl", [(0, 1), (1, 0)])
    d2, d1, d0, dx, dq_keep, dq_send = call(
        grads_kernel,
        (
            jax.ShapeDtypeStruct((PLANE, 2 * HD), BF16),
            jax.ShapeDtypeStruct((PLANE, 2 * HD), BF16),
            jax.ShapeDtypeStruct((PLANE, 2 * HD), F32),
            jax.ShapeDtypeStruct((KB, 2 * HD), BF16),
            jax.ShapeDtypeStruct((OWN * HD, 2 * ROWS), F32),
            jax.ShapeDtypeStruct((OWN * HD, 2 * ROWS), BF16),
        ),
        pool_scratch + [pltpu.VMEM((PLACES, 2 * HD), F32), pltpu.VMEM((HEADS, HD, 2 * ROWS), F32)],
        flops=10 * HD * pairs,
        name="score_grads",
    )(*shared, doc, stats, stats_y)
    back1 = lax.ppermute(d1, "x", [(i + 1, i) for i in range(X - 1)])
    back2 = lax.ppermute(d2, "x", [(i + 2, i) for i in range(X - 2)])
    backx = lax.ppermute(dx, ("x", "z", "c"), [(b, a) for a, b in lone])
    dq_arrived = lax.ppermute(dq_send, "yl", [(0, 1), (1, 0)])
    back2, back1, dq_arrived = lax.optimization_barrier((back2, back1, dq_arrived))
    gate_grad, expert_grad = call(
        combine_kernel,
        (
            jax.ShapeDtypeStruct((1, SLOTS), F32),
            jax.ShapeDtypeStruct((SLOTS, expert_out.shape[2]), BF16),
        ),
        [],
        name="combine_grads",
    )(rows, rows_other, ids, gates, expert_out[0])
    back2, _ = lax.optimization_barrier((back2, expert_grad))
    dq_mine, dq_other = call(
        pool_kernel,
        (jax.ShapeDtypeStruct((OWN * HD, ROWS), F32), jax.ShapeDtypeStruct((OWN * HD, ROWS), BF16)),
        [],
        name="query_pool",
    )(dq_keep, dq_arrived)
    dq_other = lax.ppermute(dq_other, "c", [(0, 1), (1, 0)])
    plane_sums = call(plane_kernel, jax.ShapeDtypeStruct((2 * Z, KB, HD), BF16), [], name="plane_sum")(
        d0, back2, back1, backx
    )
    parts = lax.all_to_all(plane_sums, ("z", "yl"), split_axis=0, concat_axis=0, tiled=True)

    query_grad, key_grad, value_grad = call(
        final_kernel,
        (
            jax.ShapeDtypeStruct((ROWS, OWN * HD), BF16),
            jax.ShapeDtypeStruct((HD // 2, ROWS), BF16),
            jax.ShapeDtypeStruct((HD // 2, ROWS), BF16),
        ),
        [],
        name="final_sums",
    )(parts, dq_mine, dq_other)
    return (query_grad, key_grad.T, value_grad.T, gate_grad, expert_grad[None])


def solution(mesh):
    devices = mesh.devices.reshape(X, Z, 2, 2, 4, 2)
    split = Mesh(devices, ("x", "z", "c", "zh", "yh", "yl"))
    ctx, tp = ("x", "z", "c"), ("zh", "yh", "yl")
    in_specs = (
        P(ctx, tp),
        P(ctx, None),
        P(ctx, None),
        P(ctx, tp),
        P(ctx, tp),
        P(),
        P(ctx, tp),
        P(ctx, None),
        P(ctx, None),
        P(ctx, tp, None),
    )
    out_specs = (P(ctx, tp), P(ctx, tp), P(ctx, tp), P(ctx, tp), P(ctx, tp, None))
    return jax.shard_map(local, mesh=split, in_specs=in_specs, out_specs=out_specs, check_vma=False)
```
